256 devices in a mesh: sec: 2 (over y_hi), row: 64 (over z, x, y_lo), col: 2 (over core).
Axes of the slice: x: 4, y: 4 (y_hi: 2, y_lo: 2; y = y_hi * 2 + y_lo), z: 8, core: 2. Of those that a mesh axis runs over, the one named last changes fastest.
Arguments:
- basis_matrix: bfloat16 [81920, 4096], P('row', 'col'), may hold values from -6 to 6
- operator_blocks: bfloat16 [640, 7, 128, 128], P('row', None, 'sec'), may hold values from -0.1875 to 0.1875
- neighbours: int32 [640, 7], P('row'), may hold values from 0 to 639, as said below
- neighbour_mask: int32 [640, 7], P('row'), may hold values from 0 to 1, as said below
Outputs:
- reduced: float32 [4096, 4096], P(('sec', 'row'), 'col')
The draws below stay inside these ranges and needn't reach their ends.
Inputs may be any that keep to these rules, and one draw needn't show every extreme that they name: `neighbours`: slot 0 of row block b is b; slots 1 to 4 are b - 1, b + 1, b - 2, b + 2; slots 5 and 6 lie within 2 blocks of b; a slot whose mask is 0 holds b. `neighbour_mask`: 0 exactly where slots 1 to 4 fall outside the slab, and at random in slots 5 and 6 (also where they fall outside); slot 0 is always 1.
All inputs are finite; a program needn't handle non-finite values.
Results may differ from the reference program's by a relative error of at most 0.0029.
Values may be sent and summed in bfloat16 or wider, within the bound.
A program may use at most 192 MiB of HBM per device.

```python
import jax
import jax.numpy as jnp

K = 4096
BLOCK = 128
NEIGH = 7
REACH = 2
NB = 640
NODES = 81920


def neighbour_table(key):
    local_key = jax.random.fold_in(key, 7)
    first_key, second_key = jax.random.split(local_key)
    own_block = jnp.arange(NB, dtype=jnp.int32)[:, None]
    stencil = jnp.array([0, -1, 1, -REACH, REACH], dtype=jnp.int32)
    stencil_offsets = jnp.broadcast_to(stencil[None, :], (NB, 5))
    random_offsets = jax.random.randint(first_key, (NB, NEIGH - 5), -REACH, REACH + 1, dtype=jnp.int32)
    offsets = jnp.concatenate([stencil_offsets, random_offsets], axis=1)
    destination_rows = own_block + offsets
    inside = (destination_rows >= 0) & (destination_rows < NB)
    random_keep = jax.random.randint(second_key, (NB, NEIGH), 0, 4, dtype=jnp.int32) > 0
    kept_slot = jnp.where(jnp.arange(NEIGH)[None, :] < 5, True, random_keep)
    live_slot = inside & kept_slot
    return (jnp.where(live_slot, destination_rows, own_block).astype(jnp.int32), live_slot.astype(jnp.int32))


def draw_neighbours(key, part):
    return neighbour_table(key)[0]


def draw_neighbour_mask(key, part):
    return neighbour_table(key)[1]


def levels(rng, shape, cuts, low, high):
    factor_of, own = 1.0, jax.random.fold_in(rng, 6)
    for position, parts in cuts:
        draws = jnp.exp(jax.random.uniform(jax.random.fold_in(own, position), (parts,), jnp.float32, low / len(cuts), high / len(cuts)))
        factor_of = factor_of * jnp.repeat(draws, shape[position] // parts).reshape([-1 if axis == position else 1 for axis in range(len(shape))])
    return factor_of


def centred(key, extent, scale, most, cuts=(), held_as=jnp.bfloat16):
    gain = levels(key, extent, cuts, -0.22, 0.18) if cuts else 1.0
    values = jax.random.normal(key, extent, jnp.float32) * scale * gain
    return jnp.minimum(jnp.maximum(values, -most), most).astype(held_as)


def setup_inputs(seed: int = 0) -> dict:
    splits = jax.random.split(jax.random.key(seed), 5)
    return {
        "basis_matrix": centred(splits[0], (NODES, K), 1.0, 6.0, ((0, 64), (1, 2))),
        "operator_blocks": centred(splits[1], (NB, NEIGH, BLOCK, BLOCK), (NEIGH * BLOCK) ** -0.5, 0.1875, ((0, 64), (2, 2))),
        "neighbours": draw_neighbours(jax.random.fold_in(splits[4], 71), 0),
        "neighbour_mask": draw_neighbour_mask(jax.random.fold_in(splits[4], 71), 0),
    }


def reference(basis_matrix, operator_blocks, neighbours, neighbour_mask):
    block_count = operator_blocks.shape[0]
    reduced_basis_tiles = basis_matrix.reshape(block_count, BLOCK, K)
    applied_total_sum = jnp.zeros((block_count, BLOCK, K), jnp.float32)
    for neighbour in range(NEIGH):
        selected_entries = jnp.take(reduced_basis_tiles, neighbours[:, neighbour].astype(jnp.int32), axis=0).astype(jnp.float32)
        sparse_block_list = operator_blocks[:, neighbour].astype(jnp.float32)
        coupling_weight = neighbour_mask[:, neighbour].astype(jnp.float32)
        applied_total_sum = applied_total_sum + coupling_weight[:, None, None] * jnp.einsum('hol,hla->hoa', sparse_block_list, selected_entries)
    applied = applied_total_sum.astype(jnp.bfloat16).reshape(block_count * BLOCK, K)
    total = jnp.dot(basis_matrix.T, applied, preferred_element_type=jnp.float32)
    return total / jnp.sqrt(jnp.float32(NODES))
```

```python
import math

import jax
import jax.numpy as jnp
import numpy as np
from jax import lax
from jax.sharding import Mesh
from jax.sharding import PartitionSpec as P

REACH = 2
ROW_PARTS = (("z", 8), ("x", 4), ("y", 2))
ROW = tuple(name for name, _ in ROW_PARTS)
STATIC_OFFSETS = (0, -1, 1, -2, 2)


def halo(shard, width):
    count = 1
    for _, size in ROW_PARTS:
        count *= size
    length = shard.shape[0]
    up = [(i, i + 1) for i in range(count - 1)]
    down = [(j, i) for i, j in up]
    before = lax.ppermute(shard[length - width :], ROW, up)
    after = lax.ppermute(shard[:width], ROW, down)
    return jnp.concatenate([before, shard, after], axis=0)


def take_chunk(x, index, dim):
    return lax.dynamic_index_in_dim(x, index, axis=dim, keepdims=False)


def ring_sum(x, dim, axis, n):
    p = lax.axis_index(axis)
    if n == 2:
        partner = [(0, 1), (1, 0)]
        got = lax.ppermute(take_chunk(x, 1 - p, dim), axis, partner)
        return got + take_chunk(x, p, dim)
    half = x.shape[-1] // 2
    forward, backward = x[..., :half], x[..., half:]
    right = [(i, (i + 1) % n) for i in range(n)]
    left = [(i, (i - 1) % n) for i in range(n)]
    acc_f = take_chunk(forward, (p - 1) % n, dim)
    acc_b = take_chunk(backward, (p + 1) % n, dim)
    for step in range(1, n):
        got_f = lax.ppermute(acc_f, axis, right)
        got_b = lax.ppermute(acc_b, axis, left)
        acc_f = got_f + take_chunk(forward, (p - step - 1) % n, dim)
        acc_b = got_b + take_chunk(backward, (p + step + 1) % n, dim)
    return jnp.concatenate([acc_f, acc_b], axis=-1)


def per_device(basis_matrix, operator_blocks, neighbours, neighbour_mask):
    local_rows, column_count = basis_matrix.shape
    block_count, slot_count, half_rows, block_rows = operator_blocks.shape
    sec = lax.axis_index("sec")
    col = lax.axis_index("col")
    row = 0
    for name, size in ROW_PARTS:
        row = row * size + lax.axis_index(name)

    other_half = lax.ppermute(operator_blocks, "sec", [(0, 1), (1, 0)])
    first = jnp.where(sec == 0, operator_blocks, other_half)
    second = jnp.where(sec == 0, other_half, operator_blocks)
    full_ops = jnp.concatenate([first, second], axis=2)

    other_basis = lax.ppermute(basis_matrix, "col", [(0, 1), (1, 0)])
    left_projector = jnp.where(sec == col, basis_matrix, other_basis)

    weights = neighbour_mask.astype(jnp.float32)
    extended = halo(basis_matrix, REACH * block_rows)
    tiles = extended.reshape(block_count + 2 * REACH, block_rows, column_count)
    applied = jnp.zeros((block_count, block_rows, column_count), jnp.float32)
    for slot in range(slot_count):
        if slot < len(STATIC_OFFSETS):
            start = REACH + STATIC_OFFSETS[slot]
            selected = tiles[start : start + block_count]
        else:
            offset_index = neighbours[:, slot] - row * block_count + REACH
            selected = jnp.take(tiles, offset_index, axis=0)
        product = jnp.einsum(
            "hol,hla->hoa", full_ops[:, slot], selected, preferred_element_type=jnp.float32
        )
        applied = applied + weights[:, slot][:, None, None] * product
    applied = applied.astype(jnp.bfloat16).reshape(local_rows, column_count)

    row_count = 1
    for _, size in ROW_PARTS:
        row_count *= size
    scaling = 1.0 / math.sqrt(local_rows * row_count)
    partial_tile = scaling * lax.dot_general(
        left_projector, applied, (((0,), (0,)), ((), ())), preferred_element_type=jnp.float32
    )
    chunk_rows = partial_tile.shape[0] // row_count
    shape = tuple(size for _, size in ROW_PARTS) + (chunk_rows, column_count)
    partial = partial_tile.reshape(shape)
    for name, size in ROW_PARTS:
        partial = ring_sum(partial, 0, name, size)
    return partial


def solution(mesh):
    sizes = [mesh.shape["sec"]] + [size for _, size in ROW_PARTS] + [mesh.shape["col"]]
    fine = Mesh(np.asarray(mesh.devices).reshape(sizes), ("sec",) + ROW + ("col",))
    return jax.shard_map(
        per_device,
        mesh=fine,
        in_specs=(P(ROW, "col"), P(ROW, None, "sec", None), P(ROW, None), P(ROW, None)),
        out_specs=P(("sec",) + ROW, "col"),
        check_vma=False,
    )
```

```python
import math

import jax
import jax.numpy as jnp
import numpy as np
from jax import lax
from jax.experimental import pallas as pl
from jax.experimental.pallas import tpu as pltpu
from jax.sharding import Mesh
from jax.sharding import PartitionSpec as P

REACH = 2
ROW_PARTS = (("z", 8), ("x", 4), ("y", 2))
ROW = tuple(name for name, _ in ROW_PARTS)
UNIT = 256
ORDERS = ((("z", "x", "y"), 2), (("x", "z", "y"), 3), (("y", "z", "x"), 2), (("y", "x", "z"), 1))
TILE_COLUMNS = 512


def halo(shard, width):
    count = 1
    for _, size in ROW_PARTS:
        count *= size
    length = shard.shape[0]
    up = [(i, i + 1) for i in range(count - 1)]
    down = [(j, i) for i, j in up]
    before = lax.ppermute(shard[length - width :], ROW, up)
    after = lax.ppermute(shard[:width], ROW, down)
    return jnp.concatenate([before, shard, after], axis=0)


def take_chunk(x, index, dim):
    return lax.dynamic_index_in_dim(x, index, axis=dim, keepdims=False)


def ring_sum(x, dim, axis, n):
    p = lax.axis_index(axis)
    if n == 2:
        partner = [(0, 1), (1, 0)]
        got = lax.ppermute(take_chunk(x, 1 - p, dim), axis, partner)
        return got + take_chunk(x, p, dim)
    half = x.shape[-1] // 2
    forward, backward = x[..., :half], x[..., half:]
    right = [(i, (i + 1) % n) for i in range(n)]
    left = [(i, (i - 1) % n) for i in range(n)]
    acc_f = take_chunk(forward, (p - 1) % n, dim)
    acc_b = take_chunk(backward, (p + 1) % n, dim)
    for step in range(1, n):
        got_f = lax.ppermute(acc_f, axis, right)
        got_b = lax.ppermute(acc_b, axis, left)
        acc_f = got_f + take_chunk(forward, (p - step - 1) % n, dim)
        acc_b = got_b + take_chunk(backward, (p + step + 1) % n, dim)
    return jnp.concatenate([acc_f, acc_b], axis=-1)


def applied_kernel(offsets_ref, mask_ref, ops_ref, ext_ref, out_ref):
    block = pl.program_id(1)
    slot_count, block_rows = ops_ref.shape[1], ops_ref.shape[2]
    acc = jnp.zeros(out_ref.shape, jnp.float32)
    for slot in range(slot_count):
        tile_index = offsets_ref[block * slot_count + slot]
        start = pl.multiple_of(tile_index * block_rows, block_rows)
        tile = ext_ref[pl.ds(start, block_rows), :]
        product = jnp.dot(ops_ref[0, slot], tile, preferred_element_type=jnp.float32)
        live = mask_ref[block * slot_count + slot] != 0
        acc = acc + jnp.where(live, product, 0.0)
    out_ref[...] = acc.astype(out_ref.dtype)


def apply_operator(offsets, mask, full_ops, extended):
    block_count, slot_count, block_rows, _ = full_ops.shape
    ext_rows, column_count = extended.shape
    tile = min(TILE_COLUMNS, column_count)
    grid_spec = pltpu.PrefetchScalarGridSpec(
        num_scalar_prefetch=2,
        grid=(column_count // tile, block_count),
        in_specs=[
            pl.BlockSpec((1, slot_count, block_rows, block_rows), lambda j, b, *_: (b, 0, 0, 0)),
            pl.BlockSpec((ext_rows, tile), lambda j, b, *_: (0, j)),
        ],
        out_specs=pl.BlockSpec((block_rows, tile), lambda j, b, *_: (b, j)),
    )
    flops = 2 * block_count * slot_count * block_rows * block_rows * column_count
    return pl.pallas_call(
        applied_kernel,
        grid_spec=grid_spec,
        out_shape=jax.ShapeDtypeStruct((block_count * block_rows, column_count), jnp.bfloat16),
        compiler_params=pltpu.CompilerParams(dimension_semantics=("arbitrary", "arbitrary")),
        cost_estimate=pl.CostEstimate(
            flops=flops, bytes_accessed=3 * ext_rows * column_count * 2, transcendentals=0
        ),
    )(offsets, mask, full_ops, extended)


def per_device(basis_matrix, operator_blocks, neighbours, neighbour_mask):
    local_rows, column_count = basis_matrix.shape
    block_count, slot_count, half_rows, block_rows = operator_blocks.shape
    sec = lax.axis_index("sec")
    col = lax.axis_index("col")
    row = 0
    for name, size in ROW_PARTS:
        row = row * size + lax.axis_index(name)

    other_half = lax.ppermute(operator_blocks, "sec", [(0, 1), (1, 0)])
    first = jnp.where(sec == 0, operator_blocks, other_half)
    second = jnp.where(sec == 0, other_half, operator_blocks)
    full_ops = jnp.concatenate([first, second], axis=2)

    other_basis = lax.ppermute(basis_matrix, "col", [(0, 1), (1, 0)])
    left_projector = jnp.where(sec == col, basis_matrix, other_basis)

    extended = halo(basis_matrix, REACH * block_rows)
    offsets = jnp.clip(neighbours - row * block_count + REACH, 0, block_count + 2 * REACH - 1)
    applied = apply_operator(
        offsets.reshape(-1), neighbour_mask.reshape(-1), full_ops, extended
    )

    row_count = 1
    for _, size in ROW_PARTS:
        row_count *= size
    scaling = 1.0 / math.sqrt(local_rows * row_count)
    partial_tile = scaling * lax.dot_general(
        left_projector, applied, (((0,), (0,)), ((), ())), preferred_element_type=jnp.float32
    )
    chunk_rows = partial_tile.shape[0] // row_count
    sizes = dict(ROW_PARTS)
    pieces, start = [], 0
    for order, units in ORDERS:
        width = units * UNIT
        part = partial_tile[:, start : start + width]
        start += width
        part = part.reshape(tuple(size for _, size in ROW_PARTS) + (chunk_rows, width))
        names = list(ROW)
        for name in order:
            part = ring_sum(part, names.index(name), name, sizes[name])
            names.remove(name)
        pieces.append(part)
    return jnp.concatenate(pieces, axis=-1)


def solution(mesh):
    sizes = [mesh.shape["sec"]] + [size for _, size in ROW_PARTS] + [mesh.shape["col"]]
    fine = Mesh(np.asarray(mesh.devices).reshape(sizes), ("sec",) + ROW + ("col",))
    return jax.shard_map(
        per_device,
        mesh=fine,
        in_specs=(P(ROW, "col"), P(ROW, None, "sec", None), P(ROW, None), P(ROW, None)),
        out_specs=P(("sec",) + ROW, "col"),
        check_vma=False,
    )
```

```python
import math

import jax
import jax.numpy as jnp
import numpy as np
from jax import lax
from jax.experimental import pallas as pl
from jax.experimental.pallas import tpu as pltpu
from jax.sharding import Mesh
from jax.sharding import PartitionSpec as P

REACH = 2
ROW_PARTS = (("z", 8), ("x", 4), ("y", 2))
ROW = tuple(name for name, _ in ROW_PARTS)
UNIT = 256
ORDERS = ((("z", "x", "y"), 5), (("x", "z", "y"), 3))
TILE_COLUMNS = 512


def halo(shard, width):
    count = 1
    for _, size in ROW_PARTS:
        count *= size
    length = shard.shape[0]
    up = [(i, i + 1) for i in range(count - 1)]
    down = [(j, i) for i, j in up]
    before = lax.ppermute(shard[length - width :], ROW, up)
    after = lax.ppermute(shard[:width], ROW, down)
    return jnp.concatenate([before, shard, after], axis=0)


def take_chunk(x, index, dim):
    return lax.dynamic_index_in_dim(x, index, axis=dim, keepdims=False)


def ring_sum(x, dim, axis, n):
    p = lax.axis_index(axis)
    if n == 2:
        partner = [(0, 1), (1, 0)]
        got = lax.ppermute(take_chunk(x, 1 - p, dim), axis, partner)
        return got + take_chunk(x, p, dim)
    half = x.shape[-1] // 2
    forward, backward = x[..., :half], x[..., half:]
    right = [(i, (i + 1) % n) for i in range(n)]
    left = [(i, (i - 1) % n) for i in range(n)]
    acc_f = take_chunk(forward, (p - 1) % n, dim)
    acc_b = take_chunk(backward, (p + 1) % n, dim)
    for step in range(1, n):
        got_f = lax.ppermute(acc_f, axis, right)
        got_b = lax.ppermute(acc_b, axis, left)
        acc_f = got_f + take_chunk(forward, (p - step - 1) % n, dim)
        acc_b = got_b + take_chunk(backward, (p + step + 1) % n, dim)
    return jnp.concatenate([acc_f, acc_b], axis=-1)


def applied_kernel(offsets_ref, mask_ref, ops_ref, ext_ref, out_ref):
    block = pl.program_id(1)
    slot_count, block_rows = ops_ref.shape[1], ops_ref.shape[2]
    acc = jnp.zeros(out_ref.shape, jnp.float32)
    for slot in range(slot_count):
        tile_index = offsets_ref[block * slot_count + slot]
        start = pl.multiple_of(tile_index * block_rows, block_rows)
        tile = ext_ref[pl.ds(start, block_rows), :]
        product = jnp.dot(ops_ref[0, slot], tile, preferred_element_type=jnp.float32)
        live = mask_ref[block * slot_count + slot] != 0
        acc = acc + jnp.where(live, product, 0.0)
    out_ref[...] = acc.astype(out_ref.dtype)


def apply_operator(offsets, mask, full_ops, extended):
    block_count, slot_count, block_rows, _ = full_ops.shape
    ext_rows, column_count = extended.shape
    tile = min(TILE_COLUMNS, column_count)
    grid_spec = pltpu.PrefetchScalarGridSpec(
        num_scalar_prefetch=2,
        grid=(column_count // tile, block_count),
        in_specs=[
            pl.BlockSpec((1, slot_count, block_rows, block_rows), lambda j, b, *_: (b, 0, 0, 0)),
            pl.BlockSpec((ext_rows, tile), lambda j, b, *_: (0, j)),
        ],
        out_specs=pl.BlockSpec((block_rows, tile), lambda j, b, *_: (b, j)),
    )
    flops = 2 * block_count * slot_count * block_rows * block_rows * column_count
    return pl.pallas_call(
        applied_kernel,
        grid_spec=grid_spec,
        out_shape=jax.ShapeDtypeStruct((block_count * block_rows, column_count), jnp.bfloat16),
        compiler_params=pltpu.CompilerParams(dimension_semantics=("arbitrary", "arbitrary")),
        cost_estimate=pl.CostEstimate(
            flops=flops, bytes_accessed=3 * ext_rows * column_count * 2, transcendentals=0
        ),
    )(offsets, mask, full_ops, extended)


def per_device(basis_matrix, operator_blocks, neighbours, neighbour_mask):
    local_rows, column_count = basis_matrix.shape
    block_count, slot_count, half_rows, block_rows = operator_blocks.shape
    sec = lax.axis_index("sec")
    col = lax.axis_index("col")
    row = 0
    for name, size in ROW_PARTS:
        row = row * size + lax.axis_index(name)

    other_half = lax.ppermute(operator_blocks, "sec", [(0, 1), (1, 0)])
    first = jnp.where(sec == 0, operator_blocks, other_half)
    second = jnp.where(sec == 0, other_half, operator_blocks)
    full_ops = jnp.concatenate([first, second], axis=2)

    other_basis = lax.ppermute(basis_matrix, "col", [(0, 1), (1, 0)])
    left_projector = jnp.where(sec == col, basis_matrix, other_basis)

    extended = halo(basis_matrix, REACH * block_rows)
    offsets = jnp.clip(neighbours - row * block_count + REACH, 0, block_count + 2 * REACH - 1)
    applied = apply_operator(
        offsets.reshape(-1), neighbour_mask.reshape(-1), full_ops, extended
    )

    row_count = 1
    for _, size in ROW_PARTS:
        row_count *= size
    scaling = 1.0 / math.sqrt(local_rows * row_count)
    partial_tile = scaling * lax.dot_general(
        left_projector, applied, (((0,), (0,)), ((), ())), preferred_element_type=jnp.float32
    )
    chunk_rows = partial_tile.shape[0] // row_count
    sizes = dict(ROW_PARTS)
    pieces, start = [], 0
    for order, units in ORDERS:
        width = units * UNIT
        part = partial_tile[:, start : start + width]
        start += width
        part = part.reshape(tuple(size for _, size in ROW_PARTS) + (chunk_rows, width))
        names = list(ROW)
        for name in order:
            part = ring_sum(part, names.index(name), name, sizes[name])
            names.remove(name)
        pieces.append(part)
    return jnp.concatenate(pieces, axis=-1)


def solution(mesh):
    sizes = [mesh.shape["sec"]] + [size for _, size in ROW_PARTS] + [mesh.shape["col"]]
    fine = Mesh(np.asarray(mesh.devices).reshape(sizes), ("sec",) + ROW + ("col",))
    return jax.shard_map(
        per_device,
        mesh=fine,
        in_specs=(P(ROW, "col"), P(ROW, None, "sec", None), P(ROW, None), P(ROW, None)),
        out_specs=P(("sec",) + ROW, "col"),
        check_vma=False,
    )
```

```python
import math

import jax
import jax.numpy as jnp
import numpy as np
from jax import lax
from jax.experimental import pallas as pl
from jax.experimental.pallas import tpu as pltpu
from jax.sharding import Mesh
from jax.sharding import PartitionSpec as P

REACH = 2
ROW_PARTS = (("z", 8), ("x", 4), ("y", 2))
ROW = tuple(name for name, _ in ROW_PARTS)
UNIT = 256
ORDERS = ((("z", "x", "y"), 4), (("x", "z", "y"), 4))
TILE_COLUMNS = 512


def halo(shard, width):
    count = 1
    for _, size in ROW_PARTS:
        count *= size
    length = shard.shape[0]
    up = [(i, i + 1) for i in range(count - 1)]
    down = [(j, i) for i, j in up]
    before = lax.ppermute(shard[length - width :], ROW, up)
    after = lax.ppermute(shard[:width], ROW, down)
    return jnp.concatenate([before, shard, after], axis=0)


def take_chunk(x, index, dim):
    return lax.dynamic_index_in_dim(x, index, axis=dim, keepdims=False)


def ring_sum(x, dim, axis, n):
    p = lax.axis_index(axis)
    if n == 2:
        partner = [(0, 1), (1, 0)]
        got = lax.ppermute(take_chunk(x, 1 - p, dim), axis, partner)
        return got + take_chunk(x, p, dim)
    half = x.shape[-1] // 2
    forward, backward = x[..., :half], x[..., half:]
    right = [(i, (i + 1) % n) for i in range(n)]
    left = [(i, (i - 1) % n) for i in range(n)]
    acc_f = take_chunk(forward, (p - 1) % n, dim)
    acc_b = take_chunk(backward, (p + 1) % n, dim)
    for step in range(1, n):
        got_f = lax.ppermute(acc_f, axis, right)
        got_b = lax.ppermute(acc_b, axis, left)
        acc_f = got_f + take_chunk(forward, (p - step - 1) % n, dim)
        acc_b = got_b + take_chunk(backward, (p + step + 1) % n, dim)
    return jnp.concatenate([acc_f, acc_b], axis=-1)


def applied_kernel(offsets_ref, mask_ref, ops_ref, ext_ref, out_ref):
    block = pl.program_id(1)
    slot_count, block_rows = ops_ref.shape[1], ops_ref.shape[2]
    acc = jnp.zeros(out_ref.shape, jnp.float32)
    for slot in range(slot_count):
        tile_index = offsets_ref[block * slot_count + slot]
        start = pl.multiple_of(tile_index * block_rows, block_rows)
        tile = ext_ref[pl.ds(start, block_rows), :]
        product = jnp.dot(ops_ref[0, slot], tile, preferred_element_type=jnp.float32)
        live = mask_ref[block * slot_count + slot] != 0
        acc = acc + jnp.where(live, product, 0.0)
    out_ref[...] = acc.astype(out_ref.dtype)


def apply_operator(offsets, mask, full_ops, extended):
    block_count, slot_count, block_rows, _ = full_ops.shape
    ext_rows, column_count = extended.shape
    tile = min(TILE_COLUMNS, column_count)
    grid_spec = pltpu.PrefetchScalarGridSpec(
        num_scalar_prefetch=2,
        grid=(column_count // tile, block_count),
        in_specs=[
            pl.BlockSpec((1, slot_count, block_rows, block_rows), lambda j, b, *_: (b, 0, 0, 0)),
            pl.BlockSpec((ext_rows, tile), lambda j, b, *_: (0, j)),
        ],
        out_specs=pl.BlockSpec((block_rows, tile), lambda j, b, *_: (b, j)),
    )
    flops = 2 * block_count * slot_count * block_rows * block_rows * column_count
    return pl.pallas_call(
        applied_kernel,
        grid_spec=grid_spec,
        out_shape=jax.ShapeDtypeStruct((block_count * block_rows, column_count), jnp.bfloat16),
        compiler_params=pltpu.CompilerParams(dimension_semantics=("arbitrary", "arbitrary")),
        cost_estimate=pl.CostEstimate(
            flops=flops, bytes_accessed=3 * ext_rows * column_count * 2, transcendentals=0
        ),
    )(offsets, mask, full_ops, extended)


def per_device(basis_matrix, operator_blocks, neighbours, neighbour_mask):
    local_rows, column_count = basis_matrix.shape
    block_count, slot_count, half_rows, block_rows = operator_blocks.shape
    sec = lax.axis_index("sec")
    col = lax.axis_index("col")
    row = 0
    for name, size in ROW_PARTS:
        row = row * size + lax.axis_index(name)

    other_half = lax.ppermute(operator_blocks, "sec", [(0, 1), (1, 0)])
    first = jnp.where(sec == 0, operator_blocks, other_half)
    second = jnp.where(sec == 0, other_half, operator_blocks)
    full_ops = jnp.concatenate([first, second], axis=2)

    other_basis = lax.ppermute(basis_matrix, "col", [(0, 1), (1, 0)])
    left_projector = jnp.where(sec == col, basis_matrix, other_basis)

    extended = halo(basis_matrix, REACH * block_rows)
    offsets = jnp.clip(neighbours - row * block_count + REACH, 0, block_count + 2 * REACH - 1)
    applied = apply_operator(
        offsets.reshape(-1), neighbour_mask.reshape(-1), full_ops, extended
    )

    row_count = 1
    for _, size in ROW_PARTS:
        row_count *= size
    scaling = 1.0 / math.sqrt(local_rows * row_count)
    partial_tile = scaling * lax.dot_general(
        left_projector, applied, (((0,), (0,)), ((), ())), preferred_element_type=jnp.float32
    )
    chunk_rows = partial_tile.shape[0] // row_count
    sizes = dict(ROW_PARTS)
    pieces, start = [], 0
    for order, units in ORDERS:
        width = units * UNIT
        part = partial_tile[:, start : start + width]
        start += width
        part = part.reshape(tuple(size for _, size in ROW_PARTS) + (chunk_rows, width))
        names = list(ROW)
        for name in order:
            part = ring_sum(part, names.index(name), name, sizes[name])
            names.remove(name)
        pieces.append(part)
    return jnp.concatenate(pieces, axis=-1)


def solution(mesh):
    sizes = [mesh.shape["sec"]] + [size for _, size in ROW_PARTS] + [mesh.shape["col"]]
    fine = Mesh(np.asarray(mesh.devices).reshape(sizes), ("sec",) + ROW + ("col",))
    return jax.shard_map(
        per_device,
        mesh=fine,
        in_specs=(P(ROW, "col"), P(ROW, None, "sec", None), P(ROW, None), P(ROW, None)),
        out_specs=P(("sec",) + ROW, "col"),
        check_vma=False,
    )
```

```python
import math

import jax
import jax.numpy as jnp
import numpy as np
from jax import lax
from jax.experimental import pallas as pl
from jax.experimental.pallas import tpu as pltpu
from jax.sharding import Mesh
from jax.sharding import PartitionSpec as P

REACH = 2
ROW_PARTS = (("z", 8), ("x", 4), ("y", 2))
ROW = tuple(name for name, _ in ROW_PARTS)
UNIT = 256
ORDERS = ((("z", "x", "y"), 4), (("x", "z", "y"), 4))
TILE_COLUMNS = 1024
STATIC_OFFSETS = (0, -1, 1, -2, 2)
WINDOW_SLOTS = tuple(range(len(STATIC_OFFSETS)))


def halo(shard, width):
    count = 1
    for _, size in ROW_PARTS:
        count *= size
    length = shard.shape[0]
    up = [(i, i + 1) for i in range(count - 1)]
    down = [(j, i) for i, j in up]
    before = lax.ppermute(shard[length - width :], ROW, up)
    after = lax.ppermute(shard[:width], ROW, down)
    return jnp.concatenate([before, shard, after], axis=0)


def take_chunk(x, index, dim):
    return lax.dynamic_index_in_dim(x, index, axis=dim, keepdims=False)


def ring_sum(x, dim, axis, n):
    p = lax.axis_index(axis)
    if n == 2:
        partner = [(0, 1), (1, 0)]
        got = lax.ppermute(take_chunk(x, 1 - p, dim), axis, partner)
        return got + take_chunk(x, p, dim)
    half = x.shape[-1] // 2
    forward, backward = x[..., :half], x[..., half:]
    right = [(i, (i + 1) % n) for i in range(n)]
    left = [(i, (i - 1) % n) for i in range(n)]
    acc_f = take_chunk(forward, (p - 1) % n, dim)
    acc_b = take_chunk(backward, (p + 1) % n, dim)
    for step in range(1, n):
        got_f = lax.ppermute(acc_f, axis, right)
        got_b = lax.ppermute(acc_b, axis, left)
        acc_f = got_f + take_chunk(forward, (p - step - 1) % n, dim)
        acc_b = got_b + take_chunk(backward, (p + step + 1) % n, dim)
    return jnp.concatenate([acc_f, acc_b], axis=-1)


def applied_kernel(offsets_ref, mask_ref, window_ops_ref, extra_ops_ref, ext_ref, out_ref):
    block = pl.program_id(1)
    block_rows, window = window_ops_ref.shape[1], window_ops_ref.shape[2]
    extra_count = extra_ops_ref.shape[1]
    slot_count = len(WINDOW_SLOTS) + extra_count
    first = pl.multiple_of(block * block_rows, block_rows)
    acc = jnp.dot(
        window_ops_ref[0], ext_ref[pl.ds(first, window), :], preferred_element_type=jnp.float32
    )
    for extra in range(extra_count):
        slot = len(WINDOW_SLOTS) + extra
        tile_index = offsets_ref[block * slot_count + slot]
        start = pl.multiple_of(tile_index * block_rows, block_rows)
        tile = ext_ref[pl.ds(start, block_rows), :]
        product = jnp.dot(extra_ops_ref[0, extra], tile, preferred_element_type=jnp.float32)
        live = mask_ref[block * slot_count + slot] != 0
        acc = acc + jnp.where(live, product, 0.0)
    out_ref[...] = acc.astype(out_ref.dtype)


def apply_operator(offsets, mask, full_ops, extended):
    block_count, slot_count, block_rows, _ = full_ops.shape
    ext_rows, column_count = extended.shape
    tile = min(TILE_COLUMNS, column_count)
    order = [slot for _, slot in sorted(zip(STATIC_OFFSETS, WINDOW_SLOTS))]
    weights = mask.reshape(block_count, slot_count)[:, order].astype(full_ops.dtype)
    window_ops = full_ops[:, order] * weights[:, :, None, None]
    window = len(order) * block_rows
    window_ops = window_ops.transpose(0, 2, 1, 3).reshape(block_count, block_rows, window)
    extra_ops = full_ops[:, len(WINDOW_SLOTS) :]
    extra_count = extra_ops.shape[1]
    grid_spec = pltpu.PrefetchScalarGridSpec(
        num_scalar_prefetch=2,
        grid=(column_count // tile, block_count),
        in_specs=[
            pl.BlockSpec((1, block_rows, window), lambda j, b, *_: (b, 0, 0)),
            pl.BlockSpec((1, extra_count, block_rows, block_rows), lambda j, b, *_: (b, 0, 0, 0)),
            pl.BlockSpec((ext_rows, tile), lambda j, b, *_: (0, j)),
        ],
        out_specs=pl.BlockSpec((block_rows, tile), lambda j, b, *_: (b, j)),
    )
    flops = 2 * block_count * slot_count * block_rows * block_rows * column_count
    return pl.pallas_call(
        applied_kernel,
        grid_spec=grid_spec,
        out_shape=jax.ShapeDtypeStruct((block_count * block_rows, column_count), jnp.bfloat16),
        compiler_params=pltpu.CompilerParams(dimension_semantics=("arbitrary", "arbitrary")),
        cost_estimate=pl.CostEstimate(
            flops=flops, bytes_accessed=3 * ext_rows * column_count * 2, transcendentals=0
        ),
    )(offsets, mask, window_ops, extra_ops, extended)


def per_device(basis_matrix, operator_blocks, neighbours, neighbour_mask):
    local_rows, column_count = basis_matrix.shape
    block_count, slot_count, half_rows, block_rows = operator_blocks.shape
    sec = lax.axis_index("sec")
    col = lax.axis_index("col")
    row = 0
    for name, size in ROW_PARTS:
        row = row * size + lax.axis_index(name)

    other_half = lax.ppermute(operator_blocks, "sec", [(0, 1), (1, 0)])
    first = jnp.where(sec == 0, operator_blocks, other_half)
    second = jnp.where(sec == 0, other_half, operator_blocks)
    full_ops = jnp.concatenate([first, second], axis=2)

    other_basis = lax.ppermute(basis_matrix, "col", [(0, 1), (1, 0)])
    left_projector = jnp.where(sec == col, basis_matrix, other_basis)

    extended = halo(basis_matrix, REACH * block_rows)
    offsets = jnp.clip(neighbours - row * block_count + REACH, 0, block_count + 2 * REACH - 1)
    applied = apply_operator(
        offsets.reshape(-1), neighbour_mask.reshape(-1), full_ops, extended
    )

    row_count = 1
    for _, size in ROW_PARTS:
        row_count *= size
    scaling = 1.0 / math.sqrt(local_rows * row_count)
    partial_tile = scaling * lax.dot_general(
        left_projector, applied, (((0,), (0,)), ((), ())), preferred_element_type=jnp.float32
    )
    chunk_rows = partial_tile.shape[0] // row_count
    sizes = dict(ROW_PARTS)
    pieces, start = [], 0
    for order, units in ORDERS:
        width = units * UNIT
        part = partial_tile[:, start : start + width]
        start += width
        part = part.reshape(tuple(size for _, size in ROW_PARTS) + (chunk_rows, width))
        names = list(ROW)
        for name in order:
            part = ring_sum(part, names.index(name), name, sizes[name])
            names.remove(name)
        pieces.append(part)
    return jnp.concatenate(pieces, axis=-1)


def solution(mesh):
    sizes = [mesh.shape["sec"]] + [size for _, size in ROW_PARTS] + [mesh.shape["col"]]
    fine = Mesh(np.asarray(mesh.devices).reshape(sizes), ("sec",) + ROW + ("col",))
    return jax.shard_map(
        per_device,
        mesh=fine,
        in_specs=(P(ROW, "col"), P(ROW, None, "sec", None), P(ROW, None), P(ROW, None)),
        out_specs=P(("sec",) + ROW, "col"),
        check_vma=False,
    )
```

```python
import math

import jax
import jax.numpy as jnp
import numpy as np
from jax import lax
from jax.experimental import pallas as pl
from jax.experimental.pallas import tpu as pltpu
from jax.sharding import Mesh
from jax.sharding import PartitionSpec as P

REACH = 2
ROW_PARTS = (("z", 8), ("x", 4), ("y", 2))
ROW = tuple(name for name, _ in ROW_PARTS)
UNIT = 256
ORDERS = ((("z", "x", "y"), 4), (("x", "z", "y"), 4))
TILE_COLUMNS = 1024
STATIC_OFFSETS = (0, -1, 1, -2, 2)
WINDOW_SLOTS = tuple(range(len(STATIC_OFFSETS)))


def halo(shard, width):
    count = 1
    for _, size in ROW_PARTS:
        count *= size
    length = shard.shape[0]
    axes = ("sec",) + ROW

    def index(sec, row):
        return sec * count + row

    after_pairs, before_pairs = [], []
    for sec in range(2):
        for row in range(count):
            other = sec if row % 2 == 0 else 1 - sec
            if row + 1 < count:
                after_pairs.append((index(other, row + 1), index(sec, row)))
            other = 1 - sec if row % 2 == 0 else sec
            if row >= 1:
                before_pairs.append((index(other, row - 1), index(sec, row)))
    before = lax.ppermute(shard[length - width :], axes, before_pairs)
    after = lax.ppermute(shard[:width], axes, after_pairs)
    return jnp.concatenate([before, shard, after], axis=0)


def take_chunk(x, index, dim):
    return lax.dynamic_index_in_dim(x, index, axis=dim, keepdims=False)


def ring_sum(x, dim, axis, n):
    p = lax.axis_index(axis)
    if n == 2:
        partner = [(0, 1), (1, 0)]
        got = lax.ppermute(take_chunk(x, 1 - p, dim), axis, partner)
        return got + take_chunk(x, p, dim)
    half = x.shape[-1] // 2
    forward, backward = x[..., :half], x[..., half:]
    right = [(i, (i + 1) % n) for i in range(n)]
    left = [(i, (i - 1) % n) for i in range(n)]
    acc_f = take_chunk(forward, (p - 1) % n, dim)
    acc_b = take_chunk(backward, (p + 1) % n, dim)
    for step in range(1, n):
        got_f = lax.ppermute(acc_f, axis, right)
        got_b = lax.ppermute(acc_b, axis, left)
        acc_f = got_f + take_chunk(forward, (p - step - 1) % n, dim)
        acc_b = got_b + take_chunk(backward, (p + step + 1) % n, dim)
    return jnp.concatenate([acc_f, acc_b], axis=-1)


def applied_kernel(offsets_ref, mask_ref, ops_ref, ext_ref, out_ref):
    block = pl.program_id(1)
    slot_count, block_rows = ops_ref.shape[1], ops_ref.shape[2]
    order = [slot for _, slot in sorted(zip(STATIC_OFFSETS, WINDOW_SLOTS))]
    lhs = jnp.concatenate(
        [
            jnp.where(mask_ref[block * slot_count + slot] != 0, ops_ref[0, slot], 0)
            for slot in order
        ],
        axis=1,
    )
    first = pl.multiple_of(block * block_rows, block_rows)
    acc = jnp.dot(
        lhs, ext_ref[pl.ds(first, len(order) * block_rows), :], preferred_element_type=jnp.float32
    )
    for slot in range(len(WINDOW_SLOTS), slot_count):
        tile_index = offsets_ref[block * slot_count + slot]
        start = pl.multiple_of(tile_index * block_rows, block_rows)
        tile = ext_ref[pl.ds(start, block_rows), :]
        product = jnp.dot(ops_ref[0, slot], tile, preferred_element_type=jnp.float32)
        live = mask_ref[block * slot_count + slot] != 0
        acc = acc + jnp.where(live, product, 0.0)
    out_ref[...] = acc.astype(out_ref.dtype)


def apply_operator(offsets, mask, full_ops, extended):
    block_count, slot_count, block_rows, _ = full_ops.shape
    ext_rows, column_count = extended.shape
    tile = min(TILE_COLUMNS, column_count)
    grid_spec = pltpu.PrefetchScalarGridSpec(
        num_scalar_prefetch=2,
        grid=(column_count // tile, block_count),
        in_specs=[
            pl.BlockSpec((1, slot_count, block_rows, block_rows), lambda j, b, *_: (b, 0, 0, 0)),
            pl.BlockSpec((ext_rows, tile), lambda j, b, *_: (0, j)),
        ],
        out_specs=pl.BlockSpec((block_rows, tile), lambda j, b, *_: (b, j)),
    )
    flops = 2 * block_count * slot_count * block_rows * block_rows * column_count
    return pl.pallas_call(
        applied_kernel,
        grid_spec=grid_spec,
        out_shape=jax.ShapeDtypeStruct((block_count * block_rows, column_count), jnp.bfloat16),
        compiler_params=pltpu.CompilerParams(dimension_semantics=("arbitrary", "arbitrary")),
        cost_estimate=pl.CostEstimate(
            flops=flops, bytes_accessed=3 * ext_rows * column_count * 2, transcendentals=0
        ),
    )(offsets, mask, full_ops, extended)


def per_device(basis_matrix, operator_blocks, neighbours, neighbour_mask):
    local_rows, column_count = basis_matrix.shape
    block_count, slot_count, half_rows, block_rows = operator_blocks.shape
    sec = lax.axis_index("sec")
    col = lax.axis_index("col")
    row = 0
    for name, size in ROW_PARTS:
        row = row * size + lax.axis_index(name)

    share = block_count // 2
    mine = lax.dynamic_slice_in_dim(operator_blocks, col * share, share, 0)
    from_sec = lax.ppermute(mine, "sec", [(0, 1), (1, 0)])
    from_col = lax.ppermute(from_sec, "col", [(0, 1), (1, 0)])
    other_half = jnp.where(
        col == 0,
        jnp.concatenate([from_sec, from_col], axis=0),
        jnp.concatenate([from_col, from_sec], axis=0),
    )
    first = jnp.where(sec == 0, operator_blocks, other_half)
    second = jnp.where(sec == 0, other_half, operator_blocks)
    full_ops = jnp.concatenate([first, second], axis=2)

    other_basis = lax.ppermute(basis_matrix, "col", [(0, 1), (1, 0)])
    left_projector = jnp.where(sec == col, basis_matrix, other_basis)

    extended = halo(basis_matrix, REACH * block_rows)
    offsets = jnp.clip(neighbours - row * block_count + REACH, 0, block_count + 2 * REACH - 1)
    applied = apply_operator(
        offsets.reshape(-1), neighbour_mask.reshape(-1), full_ops, extended
    )

    row_count = 1
    for _, size in ROW_PARTS:
        row_count *= size
    scaling = 1.0 / math.sqrt(local_rows * row_count)
    partial_tile = scaling * lax.dot_general(
        left_projector, applied, (((0,), (0,)), ((), ())), preferred_element_type=jnp.float32
    )
    chunk_rows = partial_tile.shape[0] // row_count
    sizes = dict(ROW_PARTS)
    pieces, start = [], 0
    for order, units in ORDERS:
        width = units * UNIT
        part = partial_tile[:, start : start + width]
        start += width
        part = part.reshape(tuple(size for _, size in ROW_PARTS) + (chunk_rows, width))
        names = list(ROW)
        for name in order:
            part = ring_sum(part, names.index(name), name, sizes[name])
            names.remove(name)
        pieces.append(part)
    return jnp.concatenate(pieces, axis=-1)


def solution(mesh):
    sizes = [mesh.shape["sec"]] + [size for _, size in ROW_PARTS] + [mesh.shape["col"]]
    fine = Mesh(np.asarray(mesh.devices).reshape(sizes), ("sec",) + ROW + ("col",))
    return jax.shard_map(
        per_device,
        mesh=fine,
        in_specs=(P(ROW, "col"), P(ROW, None, "sec", None), P(ROW, None), P(ROW, None)),
        out_specs=P(("sec",) + ROW, "col"),
        check_vma=False,
    )
```

```python
import math

import jax
import jax.numpy as jnp
import numpy as np
from jax import lax
from jax.experimental import pallas as pl
from jax.experimental.pallas import tpu as pltpu
from jax.sharding import Mesh
from jax.sharding import PartitionSpec as P

REACH = 2
ROW_PARTS = (("z", 8), ("x", 4), ("y", 2))
ROW = tuple(name for name, _ in ROW_PARTS)
UNIT = 256
ORDERS = ((("z", "x", "y"), 4), (("x", "z", "y"), 4))
TILE_COLUMNS = 1024
STATIC_OFFSETS = (0, -1, 1, -2, 2)
WINDOW_SLOTS = tuple(range(len(STATIC_OFFSETS)))


def halo(shard, width):
    count = 1
    for _, size in ROW_PARTS:
        count *= size
    length = shard.shape[0]
    axes = ("sec",) + ROW

    def index(sec, row):
        return sec * count + row

    after_pairs, before_pairs = [], []
    for sec in range(2):
        for row in range(count):
            other = sec if row % 2 == 0 else 1 - sec
            if row + 1 < count:
                after_pairs.append((index(other, row + 1), index(sec, row)))
            other = 1 - sec if row % 2 == 0 else sec
            if row >= 1:
                before_pairs.append((index(other, row - 1), index(sec, row)))
    before = lax.ppermute(shard[length - width :], axes, before_pairs)
    after = lax.ppermute(shard[:width], axes, after_pairs)
    return jnp.concatenate([before, shard, after], axis=0)


def take_chunk(x, index, dim):
    return lax.dynamic_index_in_dim(x, index, axis=dim, keepdims=False)


def ring_sum(x, dim, axis, n):
    p = lax.axis_index(axis)
    if n == 2:
        partner = [(0, 1), (1, 0)]
        got = lax.ppermute(take_chunk(x, 1 - p, dim), axis, partner)
        return got + take_chunk(x, p, dim)
    half = x.shape[-1] // 2
    forward, backward = x[..., :half], x[..., half:]
    right = [(i, (i + 1) % n) for i in range(n)]
    left = [(i, (i - 1) % n) for i in range(n)]
    acc_f = take_chunk(forward, (p - 1) % n, dim)
    acc_b = take_chunk(backward, (p + 1) % n, dim)
    for step in range(1, n):
        got_f = lax.ppermute(acc_f, axis, right)
        got_b = lax.ppermute(acc_b, axis, left)
        acc_f = got_f + take_chunk(forward, (p - step - 1) % n, dim)
        acc_b = got_b + take_chunk(backward, (p + step + 1) % n, dim)
    return jnp.concatenate([acc_f, acc_b], axis=-1)


def applied_kernel(offsets_ref, mask_ref, ops_ref, ext_ref, out_ref):
    block = pl.program_id(1)
    slot_count, block_rows = ops_ref.shape[1], ops_ref.shape[2]
    order = [slot for _, slot in sorted(zip(STATIC_OFFSETS, WINDOW_SLOTS))]
    lhs = jnp.concatenate(
        [
            jnp.where(mask_ref[block * slot_count + slot] != 0, ops_ref[0, slot], 0)
            for slot in order
        ],
        axis=1,
    )
    first = pl.multiple_of(block * block_rows, block_rows)
    acc = jnp.dot(
        lhs, ext_ref[pl.ds(first, len(order) * block_rows), :], preferred_element_type=jnp.float32
    )
    for slot in range(len(WINDOW_SLOTS), slot_count):
        tile_index = offsets_ref[block * slot_count + slot]
        start = pl.multiple_of(tile_index * block_rows, block_rows)
        tile = ext_ref[pl.ds(start, block_rows), :]
        product = jnp.dot(ops_ref[0, slot], tile, preferred_element_type=jnp.float32)
        live = mask_ref[block * slot_count + slot] != 0
        acc = acc + jnp.where(live, product, 0.0)
    out_ref[...] = acc.astype(out_ref.dtype)


def apply_operator(offsets, mask, full_ops, extended, column_start, column_count):
    block_count, slot_count, block_rows, _ = full_ops.shape
    ext_rows = extended.shape[0]
    tile = min(TILE_COLUMNS, column_count)
    skip = column_start // tile
    grid_spec = pltpu.PrefetchScalarGridSpec(
        num_scalar_prefetch=2,
        grid=(column_count // tile, block_count),
        in_specs=[
            pl.BlockSpec((1, slot_count, block_rows, block_rows), lambda j, b, *_: (b, 0, 0, 0)),
            pl.BlockSpec((ext_rows, tile), lambda j, b, *_: (0, j + skip)),
        ],
        out_specs=pl.BlockSpec((block_rows, tile), lambda j, b, *_: (b, j)),
    )
    flops = 2 * block_count * slot_count * block_rows * block_rows * column_count
    return pl.pallas_call(
        applied_kernel,
        grid_spec=grid_spec,
        out_shape=jax.ShapeDtypeStruct((block_count * block_rows, column_count), jnp.bfloat16),
        compiler_params=pltpu.CompilerParams(dimension_semantics=("arbitrary", "arbitrary")),
        cost_estimate=pl.CostEstimate(
            flops=flops, bytes_accessed=3 * ext_rows * column_count * 2, transcendentals=0
        ),
    )(offsets, mask, full_ops, extended)


def per_device(basis_matrix, operator_blocks, neighbours, neighbour_mask):
    local_rows, column_count = basis_matrix.shape
    block_count, slot_count, half_rows, block_rows = operator_blocks.shape
    sec = lax.axis_index("sec")
    col = lax.axis_index("col")
    row = 0
    for name, size in ROW_PARTS:
        row = row * size + lax.axis_index(name)

    share = block_count // 2
    mine = lax.dynamic_slice_in_dim(operator_blocks, col * share, share, 0)
    from_sec = lax.ppermute(mine, "sec", [(0, 1), (1, 0)])
    from_col = lax.ppermute(from_sec, "col", [(0, 1), (1, 0)])
    other_half = jnp.where(
        col == 0,
        jnp.concatenate([from_sec, from_col], axis=0),
        jnp.concatenate([from_col, from_sec], axis=0),
    )
    first = jnp.where(sec == 0, operator_blocks, other_half)
    second = jnp.where(sec == 0, other_half, operator_blocks)
    full_ops = jnp.concatenate([first, second], axis=2)

    other_basis = lax.ppermute(basis_matrix, "col", [(0, 1), (1, 0)])
    left_projector = jnp.where(sec == col, basis_matrix, other_basis)

    extended = halo(basis_matrix, REACH * block_rows)
    offsets = jnp.clip(neighbours - row * block_count + REACH, 0, block_count + 2 * REACH - 1)
    row_count = 1
    for _, size in ROW_PARTS:
        row_count *= size
    scaling = 1.0 / math.sqrt(local_rows * row_count)
    chunk_rows = left_projector.shape[1] // row_count
    sizes = dict(ROW_PARTS)
    pieces, start = [], 0
    for order, units in ORDERS:
        width = units * UNIT
        applied = apply_operator(
            offsets.reshape(-1), neighbour_mask.reshape(-1), full_ops, extended, start, width
        )
        start += width
        part = scaling * lax.dot_general(
            left_projector, applied, (((0,), (0,)), ((), ())), preferred_element_type=jnp.float32
        )
        part = part.reshape(tuple(size for _, size in ROW_PARTS) + (chunk_rows, width))
        names = list(ROW)
        for name in order:
            part = ring_sum(part, names.index(name), name, sizes[name])
            names.remove(name)
        pieces.append(part)
    return jnp.concatenate(pieces, axis=-1)


def solution(mesh):
    sizes = [mesh.shape["sec"]] + [size for _, size in ROW_PARTS] + [mesh.shape["col"]]
    fine = Mesh(np.asarray(mesh.devices).reshape(sizes), ("sec",) + ROW + ("col",))
    return jax.shard_map(
        per_device,
        mesh=fine,
        in_specs=(P(ROW, "col"), P(ROW, None, "sec", None), P(ROW, None), P(ROW, None)),
        out_specs=P(("sec",) + ROW, "col"),
        check_vma=False,
    )
```

```python
import functools
import itertools
import math

import jax
import jax.numpy as jnp
import numpy as np
from jax import lax
from jax.experimental import pallas as pl
from jax.experimental.pallas import tpu as pltpu
from jax.sharding import Mesh
from jax.sharding import PartitionSpec as P

REACH = 2
ROW_PARTS = (("z", 8), ("x", 4), ("y", 2))
ROW = tuple(name for name, _ in ROW_PARTS)
UNIT = 256
ORDERS = ((("z", "x", "y"), 4), (("x", "z", "y"), 4))
TILE_COLUMNS = 1024
STATIC_OFFSETS = (0, -1, 1, -2, 2)
WINDOW_SLOTS = tuple(range(len(STATIC_OFFSETS)))


def halo(shard, width):
    count = 1
    for _, size in ROW_PARTS:
        count *= size
    length = shard.shape[0]
    axes = ("sec",) + ROW

    def index(sec, row):
        return sec * count + row

    after_pairs, before_pairs = [], []
    for sec in range(2):
        for row in range(count):
            other = sec if row % 2 == 0 else 1 - sec
            if row + 1 < count:
                after_pairs.append((index(other, row + 1), index(sec, row)))
            other = 1 - sec if row % 2 == 0 else sec
            if row >= 1:
                before_pairs.append((index(other, row - 1), index(sec, row)))
    before = lax.ppermute(shard[length - width :], axes, before_pairs)
    after = lax.ppermute(shard[:width], axes, after_pairs)
    return jnp.concatenate([before, shard, after], axis=0)


def take_chunk(x, index, dim):
    return lax.dynamic_index_in_dim(x, index, axis=dim, keepdims=False)


def ring_kernel(n, axis, x_ref, o_ref, out_f, in_f, out_b, in_b, send_sem, recv_sem, credit_sem):
    p = lax.axis_index(axis)
    right = lax.rem(p + 1, n)
    left = lax.rem(p + n - 1, n)
    half = x_ref.shape[-1] // 2
    mesh = pl.DeviceIdType.MESH

    barrier = pltpu.get_barrier_semaphore()
    for neighbour in (left, right):
        pl.semaphore_signal(barrier, 1, device_id={axis: neighbour}, device_id_type=mesh)
    pl.semaphore_wait(barrier, 2)

    for step in range(n - 1):
        slot = step % 2
        chunk_f = lax.rem(p - step - 1 + 2 * n, n)
        chunk_b = lax.rem(p + step + 1, n)
        if step == 0:
            out_f[slot] = x_ref[chunk_f, :, :half]
            out_b[slot] = x_ref[chunk_b, :, half:]
        else:
            out_f[slot] = in_f[1 - slot] + x_ref[chunk_f, :, :half]
            out_b[slot] = in_b[1 - slot] + x_ref[chunk_b, :, half:]
            if step <= n - 3:
                pl.semaphore_signal(credit_sem.at[0], 1, device_id={axis: left}, device_id_type=mesh)
                pl.semaphore_signal(credit_sem.at[1], 1, device_id={axis: right}, device_id_type=mesh)
        if step >= 2:
            pl.semaphore_wait(credit_sem.at[0], 1)
            pl.semaphore_wait(credit_sem.at[1], 1)
        copy_f = pltpu.make_async_remote_copy(
            src_ref=out_f.at[slot], dst_ref=in_f.at[slot],
            send_sem=send_sem.at[0, slot], recv_sem=recv_sem.at[0, slot],
            device_id={axis: right}, device_id_type=mesh,
        )
        copy_b = pltpu.make_async_remote_copy(
            src_ref=out_b.at[slot], dst_ref=in_b.at[slot],
            send_sem=send_sem.at[1, slot], recv_sem=recv_sem.at[1, slot],
            device_id={axis: left}, device_id_type=mesh,
        )
        copy_f.start()
        copy_b.start()
        copy_f.wait()
        copy_b.wait()
    last = (n - 2) % 2
    o_ref[:, :half] = in_f[last] + x_ref[p, :, :half]
    o_ref[:, half:] = in_b[last] + x_ref[p, :, half:]


def ring_reduce(x, axis, n, collective_id):
    _, rows, width = x.shape
    half = width // 2
    vmem = pltpu.VMEM
    return pl.pallas_call(
        functools.partial(ring_kernel, n, axis),
        out_shape=jax.ShapeDtypeStruct((rows, width), x.dtype),
        in_specs=[pl.BlockSpec(memory_space=vmem)],
        out_specs=pl.BlockSpec(memory_space=vmem),
        scratch_shapes=[
            vmem((2, rows, half), x.dtype),
            vmem((2, rows, half), x.dtype),
            vmem((2, rows, half), x.dtype),
            vmem((2, rows, half), x.dtype),
            pltpu.SemaphoreType.DMA((2, 2)),
            pltpu.SemaphoreType.DMA((2, 2)),
            pltpu.SemaphoreType.REGULAR((2,)),
        ],
        compiler_params=pltpu.CompilerParams(
            collective_id=collective_id, has_side_effects=True, vmem_limit_bytes=60 * 1024 * 1024
        ),
    )(x)


def ring_sum(x, dim, axis, n, collective_id):
    p = lax.axis_index(axis)
    if n == 2:
        partner = [(0, 1), (1, 0)]
        got = lax.ppermute(take_chunk(x, 1 - p, dim), axis, partner)
        return got + take_chunk(x, p, dim)
    rest = x.shape[:dim] + x.shape[dim + 1 :]
    chunks = jnp.moveaxis(x, dim, 0).reshape(n, -1, x.shape[-1])
    return ring_reduce(chunks, axis, n, collective_id).reshape(rest)


def applied_kernel(offsets_ref, mask_ref, ops_ref, ext_ref, out_ref):
    block = pl.program_id(1)
    slot_count, block_rows = ops_ref.shape[1], ops_ref.shape[2]
    order = [slot for _, slot in sorted(zip(STATIC_OFFSETS, WINDOW_SLOTS))]
    lhs = jnp.concatenate(
        [
            jnp.where(mask_ref[block * slot_count + slot] != 0, ops_ref[0, slot], 0)
            for slot in order
        ],
        axis=1,
    )
    first = pl.multiple_of(block * block_rows, block_rows)
    acc = jnp.dot(
        lhs, ext_ref[pl.ds(first, len(order) * block_rows), :], preferred_element_type=jnp.float32
    )
    for slot in range(len(WINDOW_SLOTS), slot_count):
        tile_index = offsets_ref[block * slot_count + slot]
        start = pl.multiple_of(tile_index * block_rows, block_rows)
        tile = ext_ref[pl.ds(start, block_rows), :]
        product = jnp.dot(ops_ref[0, slot], tile, preferred_element_type=jnp.float32)
        live = mask_ref[block * slot_count + slot] != 0
        acc = acc + jnp.where(live, product, 0.0)
    out_ref[...] = acc.astype(out_ref.dtype)


def apply_operator(offsets, mask, full_ops, extended, column_start, column_count):
    block_count, slot_count, block_rows, _ = full_ops.shape
    ext_rows = extended.shape[0]
    tile = min(TILE_COLUMNS, column_count)
    skip = column_start // tile
    grid_spec = pltpu.PrefetchScalarGridSpec(
        num_scalar_prefetch=2,
        grid=(column_count // tile, block_count),
        in_specs=[
            pl.BlockSpec((1, slot_count, block_rows, block_rows), lambda j, b, *_: (b, 0, 0, 0)),
            pl.BlockSpec((ext_rows, tile), lambda j, b, *_: (0, j + skip)),
        ],
        out_specs=pl.BlockSpec((block_rows, tile), lambda j, b, *_: (b, j)),
    )
    flops = 2 * block_count * slot_count * block_rows * block_rows * column_count
    return pl.pallas_call(
        applied_kernel,
        grid_spec=grid_spec,
        out_shape=jax.ShapeDtypeStruct((block_count * block_rows, column_count), jnp.bfloat16),
        compiler_params=pltpu.CompilerParams(dimension_semantics=("arbitrary", "arbitrary")),
        cost_estimate=pl.CostEstimate(
            flops=flops, bytes_accessed=3 * ext_rows * column_count * 2, transcendentals=0
        ),
    )(offsets, mask, full_ops, extended)


def per_device(basis_matrix, operator_blocks, neighbours, neighbour_mask):
    local_rows, column_count = basis_matrix.shape
    block_count, slot_count, half_rows, block_rows = operator_blocks.shape
    sec = lax.axis_index("sec")
    col = lax.axis_index("col")
    row = 0
    for name, size in ROW_PARTS:
        row = row * size + lax.axis_index(name)

    share = block_count // 2
    mine = lax.dynamic_slice_in_dim(operator_blocks, col * share, share, 0)
    from_sec = lax.ppermute(mine, "sec", [(0, 1), (1, 0)])
    from_col = lax.ppermute(from_sec, "col", [(0, 1), (1, 0)])
    other_half = jnp.where(
        col == 0,
        jnp.concatenate([from_sec, from_col], axis=0),
        jnp.concatenate([from_col, from_sec], axis=0),
    )
    first = jnp.where(sec == 0, operator_blocks, other_half)
    second = jnp.where(sec == 0, other_half, operator_blocks)
    full_ops = jnp.concatenate([first, second], axis=2)

    other_basis = lax.ppermute(basis_matrix, "col", [(0, 1), (1, 0)])
    left_projector = jnp.where(sec == col, basis_matrix, other_basis)

    extended = halo(basis_matrix, REACH * block_rows)
    offsets = jnp.clip(neighbours - row * block_count + REACH, 0, block_count + 2 * REACH - 1)
    row_count = 1
    for _, size in ROW_PARTS:
        row_count *= size
    scaling = 1.0 / math.sqrt(local_rows * row_count)
    chunk_rows = left_projector.shape[1] // row_count
    sizes = dict(ROW_PARTS)
    pieces, start = [], 0
    kernel_ids = itertools.count()
    for order, units in ORDERS:
        width = units * UNIT
        applied = apply_operator(
            offsets.reshape(-1), neighbour_mask.reshape(-1), full_ops, extended, start, width
        )
        start += width
        part = scaling * lax.dot_general(
            left_projector, applied, (((0,), (0,)), ((), ())), preferred_element_type=jnp.float32
        )
        part = part.reshape(tuple(size for _, size in ROW_PARTS) + (chunk_rows, width))
        names = list(ROW)
        for name in order:
            part = ring_sum(part, names.index(name), name, sizes[name], next(kernel_ids))
            names.remove(name)
        pieces.append(part)
    return jnp.concatenate(pieces, axis=-1)


def solution(mesh):
    sizes = [mesh.shape["sec"]] + [size for _, size in ROW_PARTS] + [mesh.shape["col"]]
    fine = Mesh(np.asarray(mesh.devices).reshape(sizes), ("sec",) + ROW + ("col",))
    return jax.shard_map(
        per_device,
        mesh=fine,
        in_specs=(P(ROW, "col"), P(ROW, None, "sec", None), P(ROW, None), P(ROW, None)),
        out_specs=P(("sec",) + ROW, "col"),
        check_vma=False,
    )
```

```python
import functools
import math

import jax
import jax.numpy as jnp
import numpy as np
from jax import lax
from jax.experimental import pallas as pl
from jax.experimental.pallas import tpu as pltpu
from jax.sharding import Mesh
from jax.sharding import PartitionSpec as P

REACH = 2
ROW_PARTS = (("z", 8), ("x", 4), ("y", 2))
ROW = tuple(name for name, _ in ROW_PARTS)
UNIT = 256
ORDERS = ((("z", "x", "y"), 4), (("x", "z", "y"), 4))
TILE_COLUMNS = 1024
STATIC_OFFSETS = (0, -1, 1, -2, 2)
WINDOW_SLOTS = tuple(range(len(STATIC_OFFSETS)))


def halo(shard, width):
    count = 1
    for _, size in ROW_PARTS:
        count *= size
    length = shard.shape[0]
    axes = ("sec",) + ROW

    def index(sec, row):
        return sec * count + row

    after_pairs, before_pairs = [], []
    for sec in range(2):
        for row in range(count):
            other = sec if row % 2 == 0 else 1 - sec
            if row + 1 < count:
                after_pairs.append((index(other, row + 1), index(sec, row)))
            other = 1 - sec if row % 2 == 0 else sec
            if row >= 1:
                before_pairs.append((index(other, row - 1), index(sec, row)))
    before = lax.ppermute(shard[length - width :], axes, before_pairs)
    after = lax.ppermute(shard[:width], axes, after_pairs)
    return jnp.concatenate([before, shard, after], axis=0)


def take_chunk(x, index, dim):
    return lax.dynamic_index_in_dim(x, index, axis=dim, keepdims=False)


def multi_ring_kernel(plan, *refs):
    count = len(plan)
    x_refs, o_refs = refs[:count], refs[count : 2 * count]
    scratch = refs[2 * count :]
    mesh = pl.DeviceIdType.MESH
    rings = []
    for index, (axis, n) in enumerate(plan):
        out_f, in_f, out_b, in_b, send_sem, recv_sem, credit_sem = scratch[7 * index : 7 * index + 7]
        p = lax.axis_index(axis)
        rings.append(
            dict(
                axis=axis, n=n, p=p, x=x_refs[index], o=o_refs[index],
                right=lax.rem(p + 1, n), left=lax.rem(p + n - 1, n),
                out_f=out_f, in_f=in_f, out_b=out_b, in_b=in_b,
                send=send_sem, recv=recv_sem, credit=credit_sem, copies=None,
            )
        )

    barrier = pltpu.get_barrier_semaphore()
    for ring in rings:
        for neighbour in (ring["left"], ring["right"]):
            pl.semaphore_signal(barrier, 1, device_id={ring["axis"]: neighbour}, device_id_type=mesh)
    pl.semaphore_wait(barrier, 2 * count)

    ticks = max(n - 1 for _, n in plan)
    for tick in range(ticks):
        for ring in rings:
            n = ring["n"]
            due = [step for step in range(n - 1) if (step * ticks) // (n - 1) == tick]
            for step in due:
                if ring["copies"] is not None:
                    for copy in ring["copies"]:
                        copy.wait()
                    ring["copies"] = None
                slot = step % 2
                p, x, half = ring["p"], ring["x"], ring["x"].shape[-1] // 2
                chunk_f = lax.rem(p - step - 1 + 2 * n, n)
                chunk_b = lax.rem(p + step + 1, n)
                if step == 0:
                    ring["out_f"][slot] = x[chunk_f, :, :half]
                    ring["out_b"][slot] = x[chunk_b, :, half:]
                else:
                    ring["out_f"][slot] = ring["in_f"][1 - slot] + x[chunk_f, :, :half]
                    ring["out_b"][slot] = ring["in_b"][1 - slot] + x[chunk_b, :, half:]
                    if step <= n - 3:
                        pl.semaphore_signal(
                            ring["credit"].at[0], 1, device_id={ring["axis"]: ring["left"]}, device_id_type=mesh
                        )
                        pl.semaphore_signal(
                            ring["credit"].at[1], 1, device_id={ring["axis"]: ring["right"]}, device_id_type=mesh
                        )
                if step >= 2:
                    pl.semaphore_wait(ring["credit"].at[0], 1)
                    pl.semaphore_wait(ring["credit"].at[1], 1)
                copy_f = pltpu.make_async_remote_copy(
                    src_ref=ring["out_f"].at[slot], dst_ref=ring["in_f"].at[slot],
                    send_sem=ring["send"].at[0, slot], recv_sem=ring["recv"].at[0, slot],
                    device_id={ring["axis"]: ring["right"]}, device_id_type=mesh,
                )
                copy_b = pltpu.make_async_remote_copy(
                    src_ref=ring["out_b"].at[slot], dst_ref=ring["in_b"].at[slot],
                    send_sem=ring["send"].at[1, slot], recv_sem=ring["recv"].at[1, slot],
                    device_id={ring["axis"]: ring["left"]}, device_id_type=mesh,
                )
                copy_f.start()
                copy_b.start()
                ring["copies"] = (copy_f, copy_b)
    for ring in rings:
        for copy in ring["copies"]:
            copy.wait()
        n, p, x = ring["n"], ring["p"], ring["x"]
        half = x.shape[-1] // 2
        last = (n - 2) % 2
        ring["o"][:, :half] = ring["in_f"][last] + x[p, :, :half]
        ring["o"][:, half:] = ring["in_b"][last] + x[p, :, half:]


def multi_ring_reduce(inputs, plan, collective_id):
    vmem = pltpu.VMEM
    scratch = []
    for x in inputs:
        _, rows, width = x.shape
        half = width // 2
        scratch += [vmem((2, rows, half), x.dtype) for _ in range(4)]
        scratch += [
            pltpu.SemaphoreType.DMA((2, 2)),
            pltpu.SemaphoreType.DMA((2, 2)),
            pltpu.SemaphoreType.REGULAR((2,)),
        ]
    return pl.pallas_call(
        functools.partial(multi_ring_kernel, tuple(plan)),
        out_shape=[jax.ShapeDtypeStruct(x.shape[1:], x.dtype) for x in inputs],
        in_specs=[pl.BlockSpec(memory_space=vmem) for _ in inputs],
        out_specs=[pl.BlockSpec(memory_space=vmem) for _ in inputs],
        scratch_shapes=scratch,
        compiler_params=pltpu.CompilerParams(
            collective_id=collective_id, has_side_effects=True, vmem_limit_bytes=60 * 1024 * 1024
        ),
    )(*inputs)


def ring_sum(x, dim, axis, n):
    p = lax.axis_index(axis)
    partner = [(0, 1), (1, 0)]
    got = lax.ppermute(take_chunk(x, 1 - p, dim), axis, partner)
    return got + take_chunk(x, p, dim)


def applied_kernel(offsets_ref, mask_ref, ops_ref, ext_ref, out_ref):
    block = pl.program_id(1)
    slot_count, block_rows = ops_ref.shape[1], ops_ref.shape[2]
    order = [slot for _, slot in sorted(zip(STATIC_OFFSETS, WINDOW_SLOTS))]
    lhs = jnp.concatenate(
        [
            jnp.where(mask_ref[block * slot_count + slot] != 0, ops_ref[0, slot], 0)
            for slot in order
        ],
        axis=1,
    )
    first = pl.multiple_of(block * block_rows, block_rows)
    acc = jnp.dot(
        lhs, ext_ref[pl.ds(first, len(order) * block_rows), :], preferred_element_type=jnp.float32
    )
    for slot in range(len(WINDOW_SLOTS), slot_count):
        tile_index = offsets_ref[block * slot_count + slot]
        start = pl.multiple_of(tile_index * block_rows, block_rows)
        tile = ext_ref[pl.ds(start, block_rows), :]
        product = jnp.dot(ops_ref[0, slot], tile, preferred_element_type=jnp.float32)
        live = mask_ref[block * slot_count + slot] != 0
        acc = acc + jnp.where(live, product, 0.0)
    out_ref[...] = acc.astype(out_ref.dtype)


def apply_operator(offsets, mask, full_ops, extended, column_start, column_count):
    block_count, slot_count, block_rows, _ = full_ops.shape
    ext_rows = extended.shape[0]
    tile = min(TILE_COLUMNS, column_count)
    skip = column_start // tile
    grid_spec = pltpu.PrefetchScalarGridSpec(
        num_scalar_prefetch=2,
        grid=(column_count // tile, block_count),
        in_specs=[
            pl.BlockSpec((1, slot_count, block_rows, block_rows), lambda j, b, *_: (b, 0, 0, 0)),
            pl.BlockSpec((ext_rows, tile), lambda j, b, *_: (0, j + skip)),
        ],
        out_specs=pl.BlockSpec((block_rows, tile), lambda j, b, *_: (b, j)),
    )
    flops = 2 * block_count * slot_count * block_rows * block_rows * column_count
    return pl.pallas_call(
        applied_kernel,
        grid_spec=grid_spec,
        out_shape=jax.ShapeDtypeStruct((block_count * block_rows, column_count), jnp.bfloat16),
        compiler_params=pltpu.CompilerParams(dimension_semantics=("arbitrary", "arbitrary")),
        cost_estimate=pl.CostEstimate(
            flops=flops, bytes_accessed=3 * ext_rows * column_count * 2, transcendentals=0
        ),
    )(offsets, mask, full_ops, extended)


def per_device(basis_matrix, operator_blocks, neighbours, neighbour_mask):
    local_rows, column_count = basis_matrix.shape
    block_count, slot_count, half_rows, block_rows = operator_blocks.shape
    sec = lax.axis_index("sec")
    col = lax.axis_index("col")
    row = 0
    for name, size in ROW_PARTS:
        row = row * size + lax.axis_index(name)

    share = block_count // 2
    mine = lax.dynamic_slice_in_dim(operator_blocks, col * share, share, 0)
    from_sec = lax.ppermute(mine, "sec", [(0, 1), (1, 0)])
    from_col = lax.ppermute(from_sec, "col", [(0, 1), (1, 0)])
    other_half = jnp.where(
        col == 0,
        jnp.concatenate([from_sec, from_col], axis=0),
        jnp.concatenate([from_col, from_sec], axis=0),
    )
    first = jnp.where(sec == 0, operator_blocks, other_half)
    second = jnp.where(sec == 0, other_half, operator_blocks)
    full_ops = jnp.concatenate([first, second], axis=2)

    other_basis = lax.ppermute(basis_matrix, "col", [(0, 1), (1, 0)])
    left_projector = jnp.where(sec == col, basis_matrix, other_basis)

    extended = halo(basis_matrix, REACH * block_rows)
    offsets = jnp.clip(neighbours - row * block_count + REACH, 0, block_count + 2 * REACH - 1)
    row_count = 1
    for _, size in ROW_PARTS:
        row_count *= size
    scaling = 1.0 / math.sqrt(local_rows * row_count)
    chunk_rows = left_projector.shape[1] // row_count
    sizes = dict(ROW_PARTS)
    parts, names, start = [], [], 0
    for order, units in ORDERS:
        width = units * UNIT
        applied = apply_operator(
            offsets.reshape(-1), neighbour_mask.reshape(-1), full_ops, extended, start, width
        )
        start += width
        part = scaling * lax.dot_general(
            left_projector, applied, (((0,), (0,)), ((), ())), preferred_element_type=jnp.float32
        )
        parts.append(part.reshape(tuple(size for _, size in ROW_PARTS) + (chunk_rows, width)))
        names.append(list(ROW))
    for stage in range(len(ROW_PARTS)):
        axes = [order[stage] for order, _ in ORDERS]
        if sizes[axes[0]] == 2:
            for index, axis in enumerate(axes):
                dim = names[index].index(axis)
                parts[index] = ring_sum(parts[index], dim, axis, 2)
                names[index].remove(axis)
            continue
        inputs, shapes = [], []
        for index, axis in enumerate(axes):
            dim = names[index].index(axis)
            x = parts[index]
            shapes.append(x.shape[:dim] + x.shape[dim + 1 :])
            inputs.append(jnp.moveaxis(x, dim, 0).reshape(sizes[axis], -1, x.shape[-1]))
            names[index].remove(axis)
        outs = multi_ring_reduce(inputs, [(axis, sizes[axis]) for axis in axes], stage)
        parts = [out.reshape(shape) for out, shape in zip(outs, shapes)]
    pieces = parts
    return jnp.concatenate(pieces, axis=-1)


def solution(mesh):
    sizes = [mesh.shape["sec"]] + [size for _, size in ROW_PARTS] + [mesh.shape["col"]]
    fine = Mesh(np.asarray(mesh.devices).reshape(sizes), ("sec",) + ROW + ("col",))
    return jax.shard_map(
        per_device,
        mesh=fine,
        in_specs=(P(ROW, "col"), P(ROW, None, "sec", None), P(ROW, None), P(ROW, None)),
        out_specs=P(("sec",) + ROW, "col"),
        check_vma=False,
    )
```

```python
import functools
import math

import jax
import jax.numpy as jnp
import numpy as np
from jax import lax
from jax.experimental import pallas as pl
from jax.experimental.pallas import tpu as pltpu
from jax.sharding import Mesh
from jax.sharding import PartitionSpec as P

REACH = 2
ROW_PARTS = (("z", 8), ("x", 4), ("y", 2))
ROW = tuple(name for name, _ in ROW_PARTS)
UNIT = 256
ORDERS = ((("x", "z", "y"), 5), (("z", "x", "y"), 3))
TILE_COLUMNS = 1024
STATIC_OFFSETS = (0, -1, 1, -2, 2)
WINDOW_SLOTS = tuple(range(len(STATIC_OFFSETS)))


def halo(shard, width):
    count = 1
    for _, size in ROW_PARTS:
        count *= size
    length = shard.shape[0]
    axes = ("sec",) + ROW

    def index(sec, row):
        return sec * count + row

    after_pairs, before_pairs = [], []
    for sec in range(2):
        for row in range(count):
            other = sec if row % 2 == 0 else 1 - sec
            if row + 1 < count:
                after_pairs.append((index(other, row + 1), index(sec, row)))
            other = 1 - sec if row % 2 == 0 else sec
            if row >= 1:
                before_pairs.append((index(other, row - 1), index(sec, row)))
    before = lax.ppermute(shard[length - width :], axes, before_pairs)
    after = lax.ppermute(shard[:width], axes, after_pairs)
    return jnp.concatenate([before, shard, after], axis=0)


def take_chunk(x, index, dim):
    return lax.dynamic_index_in_dim(x, index, axis=dim, keepdims=False)


def multi_ring_kernel(plan, *refs):
    count = len(plan)
    x_refs, o_refs = refs[:count], refs[count : 2 * count]
    scratch = refs[2 * count :]
    mesh = pl.DeviceIdType.MESH
    rings = []
    for index, (axis, n) in enumerate(plan):
        out_f, in_f, out_b, in_b, send_sem, recv_sem, credit_sem = scratch[7 * index : 7 * index + 7]
        p = lax.axis_index(axis)
        rings.append(
            dict(
                axis=axis, n=n, p=p, x=x_refs[index], o=o_refs[index],
                right=lax.rem(p + 1, n), left=lax.rem(p + n - 1, n),
                out_f=out_f, in_f=in_f, out_b=out_b, in_b=in_b,
                send=send_sem, recv=recv_sem, credit=credit_sem, copies=None,
            )
        )

    barrier = pltpu.get_barrier_semaphore()
    for ring in rings:
        for neighbour in (ring["left"], ring["right"]):
            pl.semaphore_signal(barrier, 1, device_id={ring["axis"]: neighbour}, device_id_type=mesh)
    pl.semaphore_wait(barrier, 2 * count)

    ticks = max(n - 1 for _, n in plan)
    for tick in range(ticks):
        for ring in rings:
            n = ring["n"]
            due = [step for step in range(n - 1) if (step * ticks) // (n - 1) == tick]
            for step in due:
                if ring["copies"] is not None:
                    for copy in ring["copies"]:
                        copy.wait()
                    ring["copies"] = None
                slot = step % 2
                p, x, half = ring["p"], ring["x"], ring["x"].shape[-1] // 2
                chunk_f = lax.rem(p - step - 1 + 2 * n, n)
                chunk_b = lax.rem(p + step + 1, n)
                if step == 0:
                    ring["out_f"][slot] = x[chunk_f, :, :half]
                    ring["out_b"][slot] = x[chunk_b, :, half:]
                else:
                    ring["out_f"][slot] = ring["in_f"][1 - slot] + x[chunk_f, :, :half]
                    ring["out_b"][slot] = ring["in_b"][1 - slot] + x[chunk_b, :, half:]
                    if step <= n - 3:
                        pl.semaphore_signal(
                            ring["credit"].at[0], 1, device_id={ring["axis"]: ring["left"]}, device_id_type=mesh
                        )
                        pl.semaphore_signal(
                            ring["credit"].at[1], 1, device_id={ring["axis"]: ring["right"]}, device_id_type=mesh
                        )
                if step >= 2:
                    pl.semaphore_wait(ring["credit"].at[0], 1)
                    pl.semaphore_wait(ring["credit"].at[1], 1)
                copy_f = pltpu.make_async_remote_copy(
                    src_ref=ring["out_f"].at[slot], dst_ref=ring["in_f"].at[slot],
                    send_sem=ring["send"].at[0, slot], recv_sem=ring["recv"].at[0, slot],
                    device_id={ring["axis"]: ring["right"]}, device_id_type=mesh,
                )
                copy_b = pltpu.make_async_remote_copy(
                    src_ref=ring["out_b"].at[slot], dst_ref=ring["in_b"].at[slot],
                    send_sem=ring["send"].at[1, slot], recv_sem=ring["recv"].at[1, slot],
                    device_id={ring["axis"]: ring["left"]}, device_id_type=mesh,
                )
                copy_f.start()
                copy_b.start()
                ring["copies"] = (copy_f, copy_b)
    for ring in rings:
        for copy in ring["copies"]:
            copy.wait()
        n, p, x = ring["n"], ring["p"], ring["x"]
        half = x.shape[-1] // 2
        last = (n - 2) % 2
        ring["o"][:, :half] = ring["in_f"][last] + x[p, :, :half]
        ring["o"][:, half:] = ring["in_b"][last] + x[p, :, half:]


def multi_ring_reduce(inputs, plan, collective_id):
    vmem = pltpu.VMEM
    scratch = []
    for x in inputs:
        _, rows, width = x.shape
        half = width // 2
        scratch += [vmem((2, rows, half), x.dtype) for _ in range(4)]
        scratch += [
            pltpu.SemaphoreType.DMA((2, 2)),
            pltpu.SemaphoreType.DMA((2, 2)),
            pltpu.SemaphoreType.REGULAR((2,)),
        ]
    return pl.pallas_call(
        functools.partial(multi_ring_kernel, tuple(plan)),
        out_shape=[jax.ShapeDtypeStruct(x.shape[1:], x.dtype) for x in inputs],
        in_specs=[pl.BlockSpec(memory_space=vmem) for _ in inputs],
        out_specs=[pl.BlockSpec(memory_space=vmem) for _ in inputs],
        scratch_shapes=scratch,
        compiler_params=pltpu.CompilerParams(
            collective_id=collective_id, has_side_effects=True, vmem_limit_bytes=60 * 1024 * 1024
        ),
    )(*inputs)


def ring_sum(x, dim, axis, n):
    p = lax.axis_index(axis)
    partner = [(0, 1), (1, 0)]
    got = lax.ppermute(take_chunk(x, 1 - p, dim), axis, partner)
    return got + take_chunk(x, p, dim)


def applied_kernel(offsets_ref, mask_ref, ops_ref, ext_ref, out_ref):
    block = pl.program_id(1)
    slot_count, block_rows = ops_ref.shape[1], ops_ref.shape[2]
    order = [slot for _, slot in sorted(zip(STATIC_OFFSETS, WINDOW_SLOTS))]
    lhs = jnp.concatenate(
        [
            jnp.where(mask_ref[block * slot_count + slot] != 0, ops_ref[0, slot], 0)
            for slot in order
        ],
        axis=1,
    )
    first = pl.multiple_of(block * block_rows, block_rows)
    acc = jnp.dot(
        lhs, ext_ref[pl.ds(first, len(order) * block_rows), :], preferred_element_type=jnp.float32
    )
    for slot in range(len(WINDOW_SLOTS), slot_count):
        tile_index = offsets_ref[block * slot_count + slot]
        start = pl.multiple_of(tile_index * block_rows, block_rows)
        tile = ext_ref[pl.ds(start, block_rows), :]
        product = jnp.dot(ops_ref[0, slot], tile, preferred_element_type=jnp.float32)
        live = mask_ref[block * slot_count + slot] != 0
        acc = acc + jnp.where(live, product, 0.0)
    out_ref[...] = acc.astype(out_ref.dtype)


def apply_operator(offsets, mask, full_ops, extended, column_start, column_count):
    block_count, slot_count, block_rows, _ = full_ops.shape
    ext_rows = extended.shape[0]
    tile = max(
        size
        for size in range(128, TILE_COLUMNS + 1, 128)
        if column_count % size == 0 and column_start % size == 0
    )
    skip = column_start // tile
    grid_spec = pltpu.PrefetchScalarGridSpec(
        num_scalar_prefetch=2,
        grid=(column_count // tile, block_count),
        in_specs=[
            pl.BlockSpec((1, slot_count, block_rows, block_rows), lambda j, b, *_: (b, 0, 0, 0)),
            pl.BlockSpec((ext_rows, tile), lambda j, b, *_: (0, j + skip)),
        ],
        out_specs=pl.BlockSpec((block_rows, tile), lambda j, b, *_: (b, j)),
    )
    flops = 2 * block_count * slot_count * block_rows * block_rows * column_count
    return pl.pallas_call(
        applied_kernel,
        grid_spec=grid_spec,
        out_shape=jax.ShapeDtypeStruct((block_count * block_rows, column_count), jnp.bfloat16),
        compiler_params=pltpu.CompilerParams(dimension_semantics=("arbitrary", "arbitrary")),
        cost_estimate=pl.CostEstimate(
            flops=flops, bytes_accessed=3 * ext_rows * column_count * 2, transcendentals=0
        ),
    )(offsets, mask, full_ops, extended)


def per_device(basis_matrix, operator_blocks, neighbours, neighbour_mask):
    local_rows, column_count = basis_matrix.shape
    block_count, slot_count, half_rows, block_rows = operator_blocks.shape
    sec = lax.axis_index("sec")
    col = lax.axis_index("col")
    row = 0
    for name, size in ROW_PARTS:
        row = row * size + lax.axis_index(name)

    share = block_count // 2
    mine = lax.dynamic_slice_in_dim(operator_blocks, col * share, share, 0)
    from_sec = lax.ppermute(mine, "sec", [(0, 1), (1, 0)])
    from_col = lax.ppermute(from_sec, "col", [(0, 1), (1, 0)])
    other_half = jnp.where(
        col == 0,
        jnp.concatenate([from_sec, from_col], axis=0),
        jnp.concatenate([from_col, from_sec], axis=0),
    )
    first = jnp.where(sec == 0, operator_blocks, other_half)
    second = jnp.where(sec == 0, other_half, operator_blocks)
    full_ops = jnp.concatenate([first, second], axis=2)

    other_basis = lax.ppermute(basis_matrix, "col", [(0, 1), (1, 0)])
    left_projector = jnp.where(sec == col, basis_matrix, other_basis)

    extended = halo(basis_matrix, REACH * block_rows)
    offsets = jnp.clip(neighbours - row * block_count + REACH, 0, block_count + 2 * REACH - 1)
    row_count = 1
    for _, size in ROW_PARTS:
        row_count *= size
    scaling = 1.0 / math.sqrt(local_rows * row_count)
    chunk_rows = left_projector.shape[1] // row_count
    sizes = dict(ROW_PARTS)
    parts, names, start = [], [], 0
    for order, units in ORDERS:
        width = units * UNIT
        applied = apply_operator(
            offsets.reshape(-1), neighbour_mask.reshape(-1), full_ops, extended, start, width
        )
        start += width
        part = scaling * lax.dot_general(
            left_projector, applied, (((0,), (0,)), ((), ())), preferred_element_type=jnp.float32
        )
        parts.append(part.reshape(tuple(size for _, size in ROW_PARTS) + (chunk_rows, width)))
        names.append(list(ROW))
    for stage in range(len(ROW_PARTS)):
        axes = [order[stage] for order, _ in ORDERS]
        if sizes[axes[0]] == 2:
            for index, axis in enumerate(axes):
                dim = names[index].index(axis)
                parts[index] = ring_sum(parts[index], dim, axis, 2)
                names[index].remove(axis)
            continue
        inputs, shapes = [], []
        for index, axis in enumerate(axes):
            dim = names[index].index(axis)
            x = parts[index]
            shapes.append(x.shape[:dim] + x.shape[dim + 1 :])
            inputs.append(jnp.moveaxis(x, dim, 0).reshape(sizes[axis], -1, x.shape[-1]))
            names[index].remove(axis)
        outs = multi_ring_reduce(inputs, [(axis, sizes[axis]) for axis in axes], stage)
        parts = [out.reshape(shape) for out, shape in zip(outs, shapes)]
    pieces = parts
    return jnp.concatenate(pieces, axis=-1)


def solution(mesh):
    sizes = [mesh.shape["sec"]] + [size for _, size in ROW_PARTS] + [mesh.shape["col"]]
    fine = Mesh(np.asarray(mesh.devices).reshape(sizes), ("sec",) + ROW + ("col",))
    return jax.shard_map(
        per_device,
        mesh=fine,
        in_specs=(P(ROW, "col"), P(ROW, None, "sec", None), P(ROW, None), P(ROW, None)),
        out_specs=P(("sec",) + ROW, "col"),
        check_vma=False,
    )
```

```python
import functools
import math

import jax
import jax.numpy as jnp
import numpy as np
from jax import lax
from jax.experimental import pallas as pl
from jax.experimental.pallas import tpu as pltpu
from jax.sharding import Mesh
from jax.sharding import PartitionSpec as P

REACH = 2
ROW_PARTS = (("z", 8), ("x", 4), ("y", 2))
ROW = tuple(name for name, _ in ROW_PARTS)
UNIT = 256
ORDERS = ((("z", "x", "y"), 4), (("x", "z", "y"), 4))
TILE_COLUMNS = 1024
STATIC_OFFSETS = (0, -1, 1, -2, 2)
WINDOW_SLOTS = tuple(range(len(STATIC_OFFSETS)))


def halo(shard, width):
    count = 1
    for _, size in ROW_PARTS:
        count *= size
    length = shard.shape[0]
    axes = ("sec",) + ROW

    def index(sec, row):
        return sec * count + row

    after_pairs, before_pairs = [], []
    for sec in range(2):
        for row in range(count):
            other = sec if row % 2 == 0 else 1 - sec
            if row + 1 < count:
                after_pairs.append((index(other, row + 1), index(sec, row)))
            other = 1 - sec if row % 2 == 0 else sec
            if row >= 1:
                before_pairs.append((index(other, row - 1), index(sec, row)))
    before = lax.ppermute(shard[length - width :], axes, before_pairs)
    after = lax.ppermute(shard[:width], axes, after_pairs)
    return jnp.concatenate([before, shard, after], axis=0)


def take_chunk(x, index, dim):
    return lax.dynamic_index_in_dim(x, index, axis=dim, keepdims=False)


def multi_ring_kernel(plan, pair_axis, *refs):
    count = len(plan)
    x_refs, o_refs = refs[:count], refs[count : 2 * count]
    scratch = refs[2 * count : 2 * count + 7 * count]
    pair_scratch = refs[2 * count + 7 * count :]
    mesh = pl.DeviceIdType.MESH
    rings = []
    for index, (axis, n) in enumerate(plan):
        out_f, in_f, out_b, in_b, send_sem, recv_sem, credit_sem = scratch[7 * index : 7 * index + 7]
        p = lax.axis_index(axis)
        rings.append(
            dict(
                axis=axis, n=n, p=p, x=x_refs[index], o=o_refs[index],
                right=lax.rem(p + 1, n), left=lax.rem(p + n - 1, n),
                out_f=out_f, in_f=in_f, out_b=out_b, in_b=in_b,
                send=send_sem, recv=recv_sem, credit=credit_sem, copies=None,
            )
        )

    barrier = pltpu.get_barrier_semaphore()
    for ring in rings:
        for neighbour in (ring["left"], ring["right"]):
            pl.semaphore_signal(barrier, 1, device_id={ring["axis"]: neighbour}, device_id_type=mesh)
    signals = 2 * count
    if pair_axis is not None:
        partner = 1 - lax.axis_index(pair_axis)
        pl.semaphore_signal(barrier, 1, device_id={pair_axis: partner}, device_id_type=mesh)
        signals += 1
    pl.semaphore_wait(barrier, signals)

    ticks = max(n - 1 for _, n in plan)
    for tick in range(ticks):
        for ring in rings:
            n = ring["n"]
            due = [step for step in range(n - 1) if (step * ticks) // (n - 1) == tick]
            for step in due:
                if ring["copies"] is not None:
                    for copy in ring["copies"]:
                        copy.wait()
                    ring["copies"] = None
                slot = step % 2
                p, x, half = ring["p"], ring["x"], ring["x"].shape[-1] // 2
                chunk_f = lax.rem(p - step - 1 + 2 * n, n)
                chunk_b = lax.rem(p + step + 1, n)
                if step == 0:
                    ring["out_f"][slot] = x[chunk_f, :, :half]
                    ring["out_b"][slot] = x[chunk_b, :, half:]
                else:
                    ring["out_f"][slot] = ring["in_f"][1 - slot] + x[chunk_f, :, :half]
                    ring["out_b"][slot] = ring["in_b"][1 - slot] + x[chunk_b, :, half:]
                    if step <= n - 3:
                        pl.semaphore_signal(
                            ring["credit"].at[0], 1, device_id={ring["axis"]: ring["left"]}, device_id_type=mesh
                        )
                        pl.semaphore_signal(
                            ring["credit"].at[1], 1, device_id={ring["axis"]: ring["right"]}, device_id_type=mesh
                        )
                if step >= 2:
                    pl.semaphore_wait(ring["credit"].at[0], 1)
                    pl.semaphore_wait(ring["credit"].at[1], 1)
                copy_f = pltpu.make_async_remote_copy(
                    src_ref=ring["out_f"].at[slot], dst_ref=ring["in_f"].at[slot],
                    send_sem=ring["send"].at[0, slot], recv_sem=ring["recv"].at[0, slot],
                    device_id={ring["axis"]: ring["right"]}, device_id_type=mesh,
                )
                copy_b = pltpu.make_async_remote_copy(
                    src_ref=ring["out_b"].at[slot], dst_ref=ring["in_b"].at[slot],
                    send_sem=ring["send"].at[1, slot], recv_sem=ring["recv"].at[1, slot],
                    device_id={ring["axis"]: ring["left"]}, device_id_type=mesh,
                )
                copy_f.start()
                copy_b.start()
                ring["copies"] = (copy_f, copy_b)
    for index, ring in enumerate(rings):
        for copy in ring["copies"]:
            copy.wait()
        n, p, x = ring["n"], ring["p"], ring["x"]
        half = x.shape[-1] // 2
        last = (n - 2) % 2
        total = ring["o"] if pair_axis is None else pair_scratch[4 * index]
        total[:, :half] = ring["in_f"][last] + x[p, :, :half]
        total[:, half:] = ring["in_b"][last] + x[p, :, half:]
    if pair_axis is None:
        return
    mine = lax.axis_index(pair_axis)
    copies = []
    for index, ring in enumerate(rings):
        total, got, send_sem, recv_sem = pair_scratch[4 * index : 4 * index + 4]
        rows = got.shape[0]
        theirs = pl.multiple_of((1 - mine) * rows, rows)
        copy = pltpu.make_async_remote_copy(
            src_ref=total.at[pl.ds(theirs, rows)], dst_ref=got,
            send_sem=send_sem, recv_sem=recv_sem,
            device_id={pair_axis: 1 - mine}, device_id_type=mesh,
        )
        copy.start()
        copies.append(copy)
    for index, ring in enumerate(rings):
        total, got = pair_scratch[4 * index : 4 * index + 2]
        rows = got.shape[0]
        copies[index].wait()
        own = pl.multiple_of(mine * rows, rows)
        ring["o"][...] = got[...] + total[pl.ds(own, rows), :]


def multi_ring_reduce(inputs, plan, collective_id, pair_axis=None):
    vmem = pltpu.VMEM
    scratch = []
    for x in inputs:
        _, rows, width = x.shape
        half = width // 2
        scratch += [vmem((2, rows, half), x.dtype) for _ in range(4)]
        scratch += [
            pltpu.SemaphoreType.DMA((2, 2)),
            pltpu.SemaphoreType.DMA((2, 2)),
            pltpu.SemaphoreType.REGULAR((2,)),
        ]
    out_shapes = [x.shape[1:] for x in inputs]
    if pair_axis is not None:
        for x in inputs:
            _, rows, width = x.shape
            scratch += [
                vmem((rows, width), x.dtype),
                vmem((rows // 2, width), x.dtype),
                pltpu.SemaphoreType.DMA(()),
                pltpu.SemaphoreType.DMA(()),
            ]
        out_shapes = [(x.shape[1] // 2, x.shape[2]) for x in inputs]
    return pl.pallas_call(
        functools.partial(multi_ring_kernel, tuple(plan), pair_axis),
        out_shape=[jax.ShapeDtypeStruct(shape, x.dtype) for shape, x in zip(out_shapes, inputs)],
        in_specs=[pl.BlockSpec(memory_space=vmem) for _ in inputs],
        out_specs=[pl.BlockSpec(memory_space=vmem) for _ in inputs],
        scratch_shapes=scratch,
        compiler_params=pltpu.CompilerParams(
            collective_id=collective_id, has_side_effects=True, vmem_limit_bytes=60 * 1024 * 1024
        ),
    )(*inputs)


def ring_sum(x, dim, axis, n):
    p = lax.axis_index(axis)
    partner = [(0, 1), (1, 0)]
    got = lax.ppermute(take_chunk(x, 1 - p, dim), axis, partner)
    return got + take_chunk(x, p, dim)


def applied_kernel(offsets_ref, mask_ref, ops_ref, ext_ref, out_ref):
    block = pl.program_id(1)
    slot_count, block_rows = ops_ref.shape[1], ops_ref.shape[2]
    order = [slot for _, slot in sorted(zip(STATIC_OFFSETS, WINDOW_SLOTS))]
    lhs = jnp.concatenate(
        [
            jnp.where(mask_ref[block * slot_count + slot] != 0, ops_ref[0, slot], 0)
            for slot in order
        ],
        axis=1,
    )
    first = pl.multiple_of(block * block_rows, block_rows)
    acc = jnp.dot(
        lhs, ext_ref[pl.ds(first, len(order) * block_rows), :], preferred_element_type=jnp.float32
    )
    for slot in range(len(WINDOW_SLOTS), slot_count):
        tile_index = offsets_ref[block * slot_count + slot]
        start = pl.multiple_of(tile_index * block_rows, block_rows)
        tile = ext_ref[pl.ds(start, block_rows), :]
        product = jnp.dot(ops_ref[0, slot], tile, preferred_element_type=jnp.float32)
        live = mask_ref[block * slot_count + slot] != 0
        acc = acc + jnp.where(live, product, 0.0)
    out_ref[...] = acc.astype(out_ref.dtype)


def apply_operator(offsets, mask, full_ops, extended, column_start, column_count):
    block_count, slot_count, block_rows, _ = full_ops.shape
    ext_rows = extended.shape[0]
    tile = min(TILE_COLUMNS, column_count)
    skip = column_start // tile
    grid_spec = pltpu.PrefetchScalarGridSpec(
        num_scalar_prefetch=2,
        grid=(column_count // tile, block_count),
        in_specs=[
            pl.BlockSpec((1, slot_count, block_rows, block_rows), lambda j, b, *_: (b, 0, 0, 0)),
            pl.BlockSpec((ext_rows, tile), lambda j, b, *_: (0, j + skip)),
        ],
        out_specs=pl.BlockSpec((block_rows, tile), lambda j, b, *_: (b, j)),
    )
    flops = 2 * block_count * slot_count * block_rows * block_rows * column_count
    return pl.pallas_call(
        applied_kernel,
        grid_spec=grid_spec,
        out_shape=jax.ShapeDtypeStruct((block_count * block_rows, column_count), jnp.bfloat16),
        compiler_params=pltpu.CompilerParams(dimension_semantics=("arbitrary", "arbitrary")),
        cost_estimate=pl.CostEstimate(
            flops=flops, bytes_accessed=3 * ext_rows * column_count * 2, transcendentals=0
        ),
    )(offsets, mask, full_ops, extended)


def per_device(basis_matrix, operator_blocks, neighbours, neighbour_mask):
    local_rows, column_count = basis_matrix.shape
    block_count, slot_count, half_rows, block_rows = operator_blocks.shape
    sec = lax.axis_index("sec")
    col = lax.axis_index("col")
    row = 0
    for name, size in ROW_PARTS:
        row = row * size + lax.axis_index(name)

    share = block_count // 2
    mine = lax.dynamic_slice_in_dim(operator_blocks, col * share, share, 0)
    from_sec = lax.ppermute(mine, "sec", [(0, 1), (1, 0)])
    from_col = lax.ppermute(from_sec, "col", [(0, 1), (1, 0)])
    other_half = jnp.where(
        col == 0,
        jnp.concatenate([from_sec, from_col], axis=0),
        jnp.concatenate([from_col, from_sec], axis=0),
    )
    first = jnp.where(sec == 0, operator_blocks, other_half)
    second = jnp.where(sec == 0, other_half, operator_blocks)
    full_ops = jnp.concatenate([first, second], axis=2)

    other_basis = lax.ppermute(basis_matrix, "col", [(0, 1), (1, 0)])
    left_projector = jnp.where(sec == col, basis_matrix, other_basis)

    extended = halo(basis_matrix, REACH * block_rows)
    offsets = jnp.clip(neighbours - row * block_count + REACH, 0, block_count + 2 * REACH - 1)
    row_count = 1
    for _, size in ROW_PARTS:
        row_count *= size
    scaling = 1.0 / math.sqrt(local_rows * row_count)
    chunk_rows = left_projector.shape[1] // row_count
    sizes = dict(ROW_PARTS)
    parts, names, start = [], [], 0
    for order, units in ORDERS:
        width = units * UNIT
        applied = apply_operator(
            offsets.reshape(-1), neighbour_mask.reshape(-1), full_ops, extended, start, width
        )
        start += width
        part = scaling * lax.dot_general(
            left_projector, applied, (((0,), (0,)), ((), ())), preferred_element_type=jnp.float32
        )
        parts.append(part.reshape(tuple(size for _, size in ROW_PARTS) + (chunk_rows, width)))
        names.append(list(ROW))
    stages = len(ROW_PARTS)
    for stage in range(stages):
        axes = [order[stage] for order, _ in ORDERS]
        if sizes[axes[0]] == 2:
            continue
        pair_axis = None
        if stage + 1 < stages:
            following = [order[stage + 1] for order, _ in ORDERS]
            if sizes[following[0]] == 2 and len(set(following)) == 1 and stage + 2 == stages:
                pair_axis = following[0]
        inputs, shapes = [], []
        for index, axis in enumerate(axes):
            dim = names[index].index(axis)
            x = parts[index]
            shape = x.shape[:dim] + x.shape[dim + 1 :]
            names[index].remove(axis)
            if pair_axis is not None:
                shape = shape[1:]
                names[index].remove(pair_axis)
            shapes.append(shape)
            inputs.append(jnp.moveaxis(x, dim, 0).reshape(sizes[axis], -1, x.shape[-1]))
        outs = multi_ring_reduce(
            inputs, [(axis, sizes[axis]) for axis in axes], stage, pair_axis
        )
        parts = [out.reshape(shape) for out, shape in zip(outs, shapes)]
    for index in range(len(parts)):
        for axis in list(names[index]):
            dim = names[index].index(axis)
            parts[index] = ring_sum(parts[index], dim, axis, sizes[axis])
            names[index].remove(axis)
    pieces = parts
    return jnp.concatenate(pieces, axis=-1)


def solution(mesh):
    sizes = [mesh.shape["sec"]] + [size for _, size in ROW_PARTS] + [mesh.shape["col"]]
    fine = Mesh(np.asarray(mesh.devices).reshape(sizes), ("sec",) + ROW + ("col",))
    return jax.shard_map(
        per_device,
        mesh=fine,
        in_specs=(P(ROW, "col"), P(ROW, None, "sec", None), P(ROW, None), P(ROW, None)),
        out_specs=P(("sec",) + ROW, "col"),
        check_vma=False,
    )
```

```python
import functools
import math

import jax
import jax.numpy as jnp
import numpy as np
from jax import lax
from jax.experimental import pallas as pl
from jax.experimental.pallas import tpu as pltpu
from jax.sharding import Mesh
from jax.sharding import PartitionSpec as P

REACH = 2
ROW_PARTS = (("z", 8), ("x", 4), ("y", 2))
ROW = tuple(name for name, _ in ROW_PARTS)
UNIT = 256
ORDERS = ((("z", "x", "y"), 4), (("x", "z", "y"), 4))
TILE_COLUMNS = 1024
STATIC_OFFSETS = (0, -1, 1, -2, 2)
WINDOW_SLOTS = tuple(range(len(STATIC_OFFSETS)))


def halo(shard, width):
    count = 1
    for _, size in ROW_PARTS:
        count *= size
    length = shard.shape[0]
    axes = ("sec",) + ROW

    def index(sec, row):
        return sec * count + row

    after_pairs, before_pairs = [], []
    for sec in range(2):
        for row in range(count):
            other = sec if row % 2 == 0 else 1 - sec
            if row + 1 < count:
                after_pairs.append((index(other, row + 1), index(sec, row)))
            other = 1 - sec if row % 2 == 0 else sec
            if row >= 1:
                before_pairs.append((index(other, row - 1), index(sec, row)))
    before = lax.ppermute(shard[length - width :], axes, before_pairs)
    after = lax.ppermute(shard[:width], axes, after_pairs)
    return jnp.concatenate([before, shard, after], axis=0)


def take_chunk(x, index, dim):
    return lax.dynamic_index_in_dim(x, index, axis=dim, keepdims=False)


def multi_ring_kernel(plan, pair_axis, *refs):
    count = len(plan)
    x_refs, o_refs = refs[:count], refs[count : 2 * count]
    scratch = refs[2 * count : 2 * count + 7 * count]
    pair_scratch = refs[2 * count + 7 * count :]
    mesh = pl.DeviceIdType.MESH
    rings = []
    for index, (axis, n) in enumerate(plan):
        out_f, in_f, out_b, in_b, send_sem, recv_sem, credit_sem = scratch[7 * index : 7 * index + 7]
        p = lax.axis_index(axis)
        rings.append(
            dict(
                axis=axis, n=n, p=p, x=x_refs[index], o=o_refs[index],
                right=lax.rem(p + 1, n), left=lax.rem(p + n - 1, n),
                out_f=out_f, in_f=in_f, out_b=out_b, in_b=in_b,
                send=send_sem, recv=recv_sem, credit=credit_sem, copies=None,
            )
        )

    barrier = pltpu.get_barrier_semaphore()
    for ring in rings:
        for neighbour in (ring["left"], ring["right"]):
            pl.semaphore_signal(barrier, 1, device_id={ring["axis"]: neighbour}, device_id_type=mesh)
    signals = 2 * count
    if pair_axis is not None:
        partner = 1 - lax.axis_index(pair_axis)
        pl.semaphore_signal(barrier, 1, device_id={pair_axis: partner}, device_id_type=mesh)
        signals += 1
    pl.semaphore_wait(barrier, signals)

    ticks = max(n - 1 for _, n in plan)
    for tick in range(ticks):
        for ring in rings:
            n = ring["n"]
            due = [step for step in range(n - 1) if (step * ticks) // (n - 1) == tick]
            for step in due:
                if ring["copies"] is not None:
                    for copy in ring["copies"]:
                        copy.wait()
                    ring["copies"] = None
                slot = step % 2
                p, x, half = ring["p"], ring["x"], ring["x"].shape[-1] // 2
                chunk_f = lax.rem(p - step - 1 + 2 * n, n)
                chunk_b = lax.rem(p + step + 1, n)
                if step == 0:
                    ring["out_f"][slot] = x[chunk_f, :, :half]
                    ring["out_b"][slot] = x[chunk_b, :, half:]
                else:
                    ring["out_f"][slot] = ring["in_f"][1 - slot] + x[chunk_f, :, :half]
                    ring["out_b"][slot] = ring["in_b"][1 - slot] + x[chunk_b, :, half:]
                    if step <= n - 3:
                        pl.semaphore_signal(
                            ring["credit"].at[0], 1, device_id={ring["axis"]: ring["left"]}, device_id_type=mesh
                        )
                        pl.semaphore_signal(
                            ring["credit"].at[1], 1, device_id={ring["axis"]: ring["right"]}, device_id_type=mesh
                        )
                if step >= 2:
                    pl.semaphore_wait(ring["credit"].at[0], 1)
                    pl.semaphore_wait(ring["credit"].at[1], 1)
                copy_f = pltpu.make_async_remote_copy(
                    src_ref=ring["out_f"].at[slot], dst_ref=ring["in_f"].at[slot],
                    send_sem=ring["send"].at[0, slot], recv_sem=ring["recv"].at[0, slot],
                    device_id={ring["axis"]: ring["right"]}, device_id_type=mesh,
                )
                copy_b = pltpu.make_async_remote_copy(
                    src_ref=ring["out_b"].at[slot], dst_ref=ring["in_b"].at[slot],
                    send_sem=ring["send"].at[1, slot], recv_sem=ring["recv"].at[1, slot],
                    device_id={ring["axis"]: ring["left"]}, device_id_type=mesh,
                )
                copy_f.start()
                copy_b.start()
                ring["copies"] = (copy_f, copy_b)
    for index, ring in enumerate(rings):
        for copy in ring["copies"]:
            copy.wait()
        n, p, x = ring["n"], ring["p"], ring["x"]
        half = x.shape[-1] // 2
        last = (n - 2) % 2
        total = ring["o"] if pair_axis is None else pair_scratch[4 * index]
        total[:, :half] = ring["in_f"][last] + x[p, :, :half]
        total[:, half:] = ring["in_b"][last] + x[p, :, half:]
    if pair_axis is None:
        return
    mine = lax.axis_index(pair_axis)
    copies = []
    for index, ring in enumerate(rings):
        total, got, send_sem, recv_sem = pair_scratch[4 * index : 4 * index + 4]
        rows = got.shape[0]
        theirs = pl.multiple_of((1 - mine) * rows, rows)
        copy = pltpu.make_async_remote_copy(
            src_ref=total.at[pl.ds(theirs, rows)], dst_ref=got,
            send_sem=send_sem, recv_sem=recv_sem,
            device_id={pair_axis: 1 - mine}, device_id_type=mesh,
        )
        copy.start()
        copies.append(copy)
    for index, ring in enumerate(rings):
        total, got = pair_scratch[4 * index : 4 * index + 2]
        rows = got.shape[0]
        copies[index].wait()
        own = pl.multiple_of(mine * rows, rows)
        ring["o"][...] = got[...] + total[pl.ds(own, rows), :]


def multi_ring_reduce(inputs, plan, collective_id, pair_axis=None):
    vmem = pltpu.VMEM
    scratch = []
    for x in inputs:
        _, rows, width = x.shape
        half = width // 2
        scratch += [vmem((2, rows, half), x.dtype) for _ in range(4)]
        scratch += [
            pltpu.SemaphoreType.DMA((2, 2)),
            pltpu.SemaphoreType.DMA((2, 2)),
            pltpu.SemaphoreType.REGULAR((2,)),
        ]
    out_shapes = [x.shape[1:] for x in inputs]
    if pair_axis is not None:
        for x in inputs:
            _, rows, width = x.shape
            scratch += [
                vmem((rows, width), x.dtype),
                vmem((rows // 2, width), x.dtype),
                pltpu.SemaphoreType.DMA(()),
                pltpu.SemaphoreType.DMA(()),
            ]
        out_shapes = [(x.shape[1] // 2, x.shape[2]) for x in inputs]
    return pl.pallas_call(
        functools.partial(multi_ring_kernel, tuple(plan), pair_axis),
        out_shape=[jax.ShapeDtypeStruct(shape, x.dtype) for shape, x in zip(out_shapes, inputs)],
        in_specs=[pl.BlockSpec(memory_space=vmem) for _ in inputs],
        out_specs=[pl.BlockSpec(memory_space=vmem) for _ in inputs],
        scratch_shapes=scratch,
        compiler_params=pltpu.CompilerParams(
            collective_id=collective_id, has_side_effects=True, vmem_limit_bytes=60 * 1024 * 1024
        ),
    )(*inputs)


def ring_sum(x, dim, axis, n):
    p = lax.axis_index(axis)
    partner = [(0, 1), (1, 0)]
    got = lax.ppermute(take_chunk(x, 1 - p, dim), axis, partner)
    return got + take_chunk(x, p, dim)


def applied_kernel(offsets_ref, mask_ref, ops_ref, ext_ref, out_ref):
    block = pl.program_id(1)
    slot_count, block_rows = ops_ref.shape[1], ops_ref.shape[2]
    order = [slot for _, slot in sorted(zip(STATIC_OFFSETS, WINDOW_SLOTS))]
    lhs = jnp.concatenate(
        [
            jnp.where(mask_ref[block * slot_count + slot] != 0, ops_ref[0, slot], 0)
            for slot in order
        ],
        axis=1,
    )
    first = pl.multiple_of(block * block_rows, block_rows)
    acc = jnp.dot(
        lhs, ext_ref[pl.ds(first, len(order) * block_rows), :], preferred_element_type=jnp.float32
    )
    for slot in range(len(WINDOW_SLOTS), slot_count):
        tile_index = offsets_ref[block * slot_count + slot]
        start = pl.multiple_of(tile_index * block_rows, block_rows)
        tile = ext_ref[pl.ds(start, block_rows), :]
        product = jnp.dot(ops_ref[0, slot], tile, preferred_element_type=jnp.float32)
        live = mask_ref[block * slot_count + slot] != 0
        acc = acc + jnp.where(live, product, 0.0)
    out_ref[...] = acc.astype(out_ref.dtype)


def apply_operator(offsets, mask, full_ops, extended, column_start, column_count):
    block_count, slot_count, block_rows, _ = full_ops.shape
    ext_rows = extended.shape[0]
    tile = min(TILE_COLUMNS, column_count)
    skip = column_start // tile
    grid_spec = pltpu.PrefetchScalarGridSpec(
        num_scalar_prefetch=2,
        grid=(column_count // tile, block_count),
        in_specs=[
            pl.BlockSpec((1, slot_count, block_rows, block_rows), lambda j, b, *_: (b, 0, 0, 0)),
            pl.BlockSpec((ext_rows, tile), lambda j, b, *_: (0, j + skip)),
        ],
        out_specs=pl.BlockSpec((block_rows, tile), lambda j, b, *_: (b, j)),
    )
    flops = 2 * block_count * slot_count * block_rows * block_rows * column_count
    return pl.pallas_call(
        applied_kernel,
        grid_spec=grid_spec,
        out_shape=jax.ShapeDtypeStruct((block_count * block_rows, column_count), jnp.bfloat16),
        compiler_params=pltpu.CompilerParams(dimension_semantics=("arbitrary", "arbitrary")),
        cost_estimate=pl.CostEstimate(
            flops=flops, bytes_accessed=3 * ext_rows * column_count * 2, transcendentals=0
        ),
    )(offsets, mask, full_ops, extended)


def per_device(basis_matrix, operator_blocks, neighbours, neighbour_mask):
    local_rows, column_count = basis_matrix.shape
    block_count, slot_count, half_rows, block_rows = operator_blocks.shape
    sec = lax.axis_index("sec")
    col = lax.axis_index("col")
    row = 0
    for name, size in ROW_PARTS:
        row = row * size + lax.axis_index(name)

    share = block_count // 2
    mine = lax.dynamic_slice_in_dim(operator_blocks, col * share, share, 0)
    from_sec = lax.ppermute(mine, "sec", [(0, 1), (1, 0)])
    from_col = lax.ppermute(from_sec, "col", [(0, 1), (1, 0)])
    other_half = jnp.where(
        col == 0,
        jnp.concatenate([from_sec, from_col], axis=0),
        jnp.concatenate([from_col, from_sec], axis=0),
    )
    first = jnp.where(sec == 0, operator_blocks, other_half)
    second = jnp.where(sec == 0, other_half, operator_blocks)
    full_ops = jnp.concatenate([first, second], axis=2)

    extended = halo(basis_matrix, REACH * block_rows)

    outgoing, _, _ = lax.optimization_barrier((basis_matrix, from_col, extended))
    other_basis = lax.ppermute(outgoing, "col", [(0, 1), (1, 0)])
    left_projector = jnp.where(sec == col, basis_matrix, other_basis)
    offsets = jnp.clip(neighbours - row * block_count + REACH, 0, block_count + 2 * REACH - 1)
    row_count = 1
    for _, size in ROW_PARTS:
        row_count *= size
    scaling = 1.0 / math.sqrt(local_rows * row_count)
    chunk_rows = left_projector.shape[1] // row_count
    sizes = dict(ROW_PARTS)
    parts, names, start = [], [], 0
    for order, units in ORDERS:
        width = units * UNIT
        applied = apply_operator(
            offsets.reshape(-1), neighbour_mask.reshape(-1), full_ops, extended, start, width
        )
        start += width
        part = scaling * lax.dot_general(
            left_projector, applied, (((0,), (0,)), ((), ())), preferred_element_type=jnp.float32
        )
        parts.append(part.reshape(tuple(size for _, size in ROW_PARTS) + (chunk_rows, width)))
        names.append(list(ROW))
    stages = len(ROW_PARTS)
    for stage in range(stages):
        axes = [order[stage] for order, _ in ORDERS]
        if sizes[axes[0]] == 2:
            continue
        pair_axis = None
        if stage + 1 < stages:
            following = [order[stage + 1] for order, _ in ORDERS]
            if sizes[following[0]] == 2 and len(set(following)) == 1 and stage + 2 == stages:
                pair_axis = following[0]
        inputs, shapes = [], []
        for index, axis in enumerate(axes):
            dim = names[index].index(axis)
            x = parts[index]
            shape = x.shape[:dim] + x.shape[dim + 1 :]
            names[index].remove(axis)
            if pair_axis is not None:
                shape = shape[1:]
                names[index].remove(pair_axis)
            shapes.append(shape)
            inputs.append(jnp.moveaxis(x, dim, 0).reshape(sizes[axis], -1, x.shape[-1]))
        outs = multi_ring_reduce(
            inputs, [(axis, sizes[axis]) for axis in axes], stage, pair_axis
        )
        parts = [out.reshape(shape) for out, shape in zip(outs, shapes)]
    for index in range(len(parts)):
        for axis in list(names[index]):
            dim = names[index].index(axis)
            parts[index] = ring_sum(parts[index], dim, axis, sizes[axis])
            names[index].remove(axis)
    pieces = parts
    return jnp.concatenate(pieces, axis=-1)


def solution(mesh):
    sizes = [mesh.shape["sec"]] + [size for _, size in ROW_PARTS] + [mesh.shape["col"]]
    fine = Mesh(np.asarray(mesh.devices).reshape(sizes), ("sec",) + ROW + ("col",))
    return jax.shard_map(
        per_device,
        mesh=fine,
        in_specs=(P(ROW, "col"), P(ROW, None, "sec", None), P(ROW, None), P(ROW, None)),
        out_specs=P(("sec",) + ROW, "col"),
        check_vma=False,
    )
```

```python
import functools
import math

import jax
import jax.numpy as jnp
import numpy as np
from jax import lax
from jax.experimental import pallas as pl
from jax.experimental.pallas import tpu as pltpu
from jax.sharding import Mesh
from jax.sharding import PartitionSpec as P

REACH = 2
ROW_PARTS = (("z", 8), ("x", 4), ("y", 2))
ROW = tuple(name for name, _ in ROW_PARTS)
UNIT = 256
ORDERS = ((("z", "x", "y"), 4), (("x", "z", "y"), 4))
TILE_COLUMNS = 1024
STRIDE = 8
STATIC_OFFSETS = (0, -1, 1, -2, 2)
WINDOW_SLOTS = tuple(range(len(STATIC_OFFSETS)))


def halo(shard, width):
    count = 1
    for _, size in ROW_PARTS:
        count *= size
    length = shard.shape[0]
    axes = ("sec",) + ROW

    def index(sec, row):
        return sec * count + row

    after_pairs, before_pairs = [], []
    for sec in range(2):
        for row in range(count):
            other = sec if row % 2 == 0 else 1 - sec
            if row + 1 < count:
                after_pairs.append((index(other, row + 1), index(sec, row)))
            other = 1 - sec if row % 2 == 0 else sec
            if row >= 1:
                before_pairs.append((index(other, row - 1), index(sec, row)))
    before = lax.ppermute(shard[length - width :], axes, before_pairs)
    after = lax.ppermute(shard[:width], axes, after_pairs)
    return jnp.concatenate([before, shard, after], axis=0)


def take_chunk(x, index, dim):
    return lax.dynamic_index_in_dim(x, index, axis=dim, keepdims=False)


def multi_ring_kernel(plan, pair_axis, *refs):
    count = len(plan)
    x_refs, o_refs = refs[:count], refs[count : 2 * count]
    scratch = refs[2 * count : 2 * count + STRIDE * count]
    pair_scratch = refs[2 * count + STRIDE * count :]
    mesh = pl.DeviceIdType.MESH
    rings = []
    for index, (axis, n, halving) in enumerate(plan):
        p = lax.axis_index(axis)
        ring = dict(axis=axis, n=n, p=p, x=x_refs[index], o=o_refs[index], halving=halving, copies=None)
        if halving:
            distances = []
            d = n // 2
            while d >= 1:
                distances.append(d)
                d //= 2
            steps = len(distances)
            ring.update(
                distances=distances,
                received=scratch[STRIDE * index : STRIDE * index + steps],
                kept=scratch[STRIDE * index + steps : STRIDE * index + 2 * steps],
                send=scratch[STRIDE * index + 2 * steps],
                recv=scratch[STRIDE * index + 2 * steps + 1],
                partners=[p + (1 - 2 * lax.rem(p // d, 2)) * d for d in distances],
            )
        else:
            out_f, in_f, out_b, in_b, send_sem, recv_sem, credit_sem = scratch[STRIDE * index : STRIDE * index + 7]
            ring.update(
                right=lax.rem(p + 1, n), left=lax.rem(p + n - 1, n),
                out_f=out_f, in_f=in_f, out_b=out_b, in_b=in_b,
                send=send_sem, recv=recv_sem, credit=credit_sem,
            )
        rings.append(ring)

    barrier = pltpu.get_barrier_semaphore()
    signals = 0
    for ring in rings:
        targets = ring["partners"] if ring["halving"] else (ring["left"], ring["right"])
        for neighbour in targets:
            pl.semaphore_signal(barrier, 1, device_id={ring["axis"]: neighbour}, device_id_type=mesh)
            signals += 1
    if pair_axis is not None:
        partner = 1 - lax.axis_index(pair_axis)
        pl.semaphore_signal(barrier, 1, device_id={pair_axis: partner}, device_id_type=mesh)
        signals += 1
    pl.semaphore_wait(barrier, signals)

    def halving_source(ring, step):
        return ring["x"] if step == 0 else ring["kept"][step - 1]

    def halving_finish(ring, step):
        d = ring["distances"][step]
        keep = pl.multiple_of(lax.rem(ring["p"] // d, 2) * d, d)
        src = halving_source(ring, step)
        ring["kept"][step][...] = src[pl.ds(keep, d)] + ring["received"][step][...]

    def step_count(ring):
        return len(ring["distances"]) if ring["halving"] else ring["n"] - 1

    ticks = max(step_count(ring) for ring in rings)
    for tick in range(ticks):
        for ring in rings:
            n = ring["n"]
            total_steps = step_count(ring)
            due = [step for step in range(total_steps) if (step * ticks) // total_steps == tick]
            if ring["halving"]:
                for step in due:
                    if step > 0:
                        ring["copies"].wait()
                        halving_finish(ring, step - 1)
                    d = ring["distances"][step]
                    away = pl.multiple_of((1 - lax.rem(ring["p"] // d, 2)) * d, d)
                    copy = pltpu.make_async_remote_copy(
                        src_ref=halving_source(ring, step).at[pl.ds(away, d)],
                        dst_ref=ring["received"][step],
                        send_sem=ring["send"].at[step], recv_sem=ring["recv"].at[step],
                        device_id={ring["axis"]: ring["partners"][step]}, device_id_type=mesh,
                    )
                    copy.start()
                    ring["copies"] = copy
                continue
            for step in due:
                if ring["copies"] is not None:
                    for copy in ring["copies"]:
                        copy.wait()
                    ring["copies"] = None
                slot = step % 2
                p, x, half = ring["p"], ring["x"], ring["x"].shape[-1] // 2
                chunk_f = lax.rem(p - step - 1 + 2 * n, n)
                chunk_b = lax.rem(p + step + 1, n)
                if step == 0:
                    ring["out_f"][slot] = x[chunk_f, :, :half]
                    ring["out_b"][slot] = x[chunk_b, :, half:]
                else:
                    ring["out_f"][slot] = ring["in_f"][1 - slot] + x[chunk_f, :, :half]
                    ring["out_b"][slot] = ring["in_b"][1 - slot] + x[chunk_b, :, half:]
                    if step <= n - 3:
                        pl.semaphore_signal(
                            ring["credit"].at[0], 1, device_id={ring["axis"]: ring["left"]}, device_id_type=mesh
                        )
                        pl.semaphore_signal(
                            ring["credit"].at[1], 1, device_id={ring["axis"]: ring["right"]}, device_id_type=mesh
                        )
                if step >= 2:
                    pl.semaphore_wait(ring["credit"].at[0], 1)
                    pl.semaphore_wait(ring["credit"].at[1], 1)
                copy_f = pltpu.make_async_remote_copy(
                    src_ref=ring["out_f"].at[slot], dst_ref=ring["in_f"].at[slot],
                    send_sem=ring["send"].at[0, slot], recv_sem=ring["recv"].at[0, slot],
                    device_id={ring["axis"]: ring["right"]}, device_id_type=mesh,
                )
                copy_b = pltpu.make_async_remote_copy(
                    src_ref=ring["out_b"].at[slot], dst_ref=ring["in_b"].at[slot],
                    send_sem=ring["send"].at[1, slot], recv_sem=ring["recv"].at[1, slot],
                    device_id={ring["axis"]: ring["left"]}, device_id_type=mesh,
                )
                copy_f.start()
                copy_b.start()
                ring["copies"] = (copy_f, copy_b)
    for index, ring in enumerate(rings):
        if ring["halving"]:
            ring["copies"].wait()
            last = len(ring["distances"]) - 1
            halving_finish(ring, last)
            total = ring["o"] if pair_axis is None else pair_scratch[4 * index]
            total[...] = ring["kept"][last][0]
            continue
        for copy in ring["copies"]:
            copy.wait()
        n, p, x = ring["n"], ring["p"], ring["x"]
        half = x.shape[-1] // 2
        last = (n - 2) % 2
        total = ring["o"] if pair_axis is None else pair_scratch[4 * index]
        total[:, :half] = ring["in_f"][last] + x[p, :, :half]
        total[:, half:] = ring["in_b"][last] + x[p, :, half:]
    if pair_axis is None:
        return
    mine = lax.axis_index(pair_axis)
    copies = []
    for index, ring in enumerate(rings):
        total, got, send_sem, recv_sem = pair_scratch[4 * index : 4 * index + 4]
        rows = got.shape[0]
        theirs = pl.multiple_of((1 - mine) * rows, rows)
        copy = pltpu.make_async_remote_copy(
            src_ref=total.at[pl.ds(theirs, rows)], dst_ref=got,
            send_sem=send_sem, recv_sem=recv_sem,
            device_id={pair_axis: 1 - mine}, device_id_type=mesh,
        )
        copy.start()
        copies.append(copy)
    for index, ring in enumerate(rings):
        total, got = pair_scratch[4 * index : 4 * index + 2]
        rows = got.shape[0]
        copies[index].wait()
        own = pl.multiple_of(mine * rows, rows)
        ring["o"][...] = got[...] + total[pl.ds(own, rows), :]


def multi_ring_reduce(inputs, plan, collective_id, pair_axis=None):
    vmem = pltpu.VMEM
    scratch = []
    for x, (_, n, halving) in zip(inputs, plan):
        _, rows, width = x.shape
        half = width // 2
        if halving:
            sizes = []
            d = n // 2
            while d >= 1:
                sizes.append(d)
                d //= 2
            scratch += [vmem((d, rows, width), x.dtype) for d in sizes] * 2
            scratch += [
                pltpu.SemaphoreType.DMA((len(sizes),)),
                pltpu.SemaphoreType.DMA((len(sizes),)),
            ]
            continue
        scratch += [vmem((2, rows, half), x.dtype) for _ in range(4)]
        scratch += [
            pltpu.SemaphoreType.DMA((2, 2)),
            pltpu.SemaphoreType.DMA((2, 2)),
            pltpu.SemaphoreType.REGULAR((2,)),
            vmem((8, 128), x.dtype),
        ]
    out_shapes = [x.shape[1:] for x in inputs]
    if pair_axis is not None:
        for x in inputs:
            _, rows, width = x.shape
            scratch += [
                vmem((rows, width), x.dtype),
                vmem((rows // 2, width), x.dtype),
                pltpu.SemaphoreType.DMA(()),
                pltpu.SemaphoreType.DMA(()),
            ]
        out_shapes = [(x.shape[1] // 2, x.shape[2]) for x in inputs]
    return pl.pallas_call(
        functools.partial(multi_ring_kernel, tuple(plan), pair_axis),
        out_shape=[jax.ShapeDtypeStruct(shape, x.dtype) for shape, x in zip(out_shapes, inputs)],
        in_specs=[pl.BlockSpec(memory_space=vmem) for _ in inputs],
        out_specs=[pl.BlockSpec(memory_space=vmem) for _ in inputs],
        scratch_shapes=scratch,
        compiler_params=pltpu.CompilerParams(
            collective_id=collective_id, has_side_effects=True, vmem_limit_bytes=60 * 1024 * 1024
        ),
    )(*inputs)


def ring_sum(x, dim, axis, n):
    p = lax.axis_index(axis)
    partner = [(0, 1), (1, 0)]
    got = lax.ppermute(take_chunk(x, 1 - p, dim), axis, partner)
    return got + take_chunk(x, p, dim)


def applied_kernel(offsets_ref, mask_ref, ops_ref, ext_ref, out_ref):
    block = pl.program_id(1)
    slot_count, block_rows = ops_ref.shape[1], ops_ref.shape[2]
    order = [slot for _, slot in sorted(zip(STATIC_OFFSETS, WINDOW_SLOTS))]
    lhs = jnp.concatenate(
        [
            jnp.where(mask_ref[block * slot_count + slot] != 0, ops_ref[0, slot], 0)
            for slot in order
        ],
        axis=1,
    )
    first = pl.multiple_of(block * block_rows, block_rows)
    acc = jnp.dot(
        lhs, ext_ref[pl.ds(first, len(order) * block_rows), :], preferred_element_type=jnp.float32
    )
    for slot in range(len(WINDOW_SLOTS), slot_count):
        tile_index = offsets_ref[block * slot_count + slot]
        start = pl.multiple_of(tile_index * block_rows, block_rows)
        tile = ext_ref[pl.ds(start, block_rows), :]
        product = jnp.dot(ops_ref[0, slot], tile, preferred_element_type=jnp.float32)
        live = mask_ref[block * slot_count + slot] != 0
        acc = acc + jnp.where(live, product, 0.0)
    out_ref[...] = acc.astype(out_ref.dtype)


def apply_operator(offsets, mask, full_ops, extended, column_start, column_count):
    block_count, slot_count, block_rows, _ = full_ops.shape
    ext_rows = extended.shape[0]
    tile = min(TILE_COLUMNS, column_count)
    skip = column_start // tile
    grid_spec = pltpu.PrefetchScalarGridSpec(
        num_scalar_prefetch=2,
        grid=(column_count // tile, block_count),
        in_specs=[
            pl.BlockSpec((1, slot_count, block_rows, block_rows), lambda j, b, *_: (b, 0, 0, 0)),
            pl.BlockSpec((ext_rows, tile), lambda j, b, *_: (0, j + skip)),
        ],
        out_specs=pl.BlockSpec((block_rows, tile), lambda j, b, *_: (b, j)),
    )
    flops = 2 * block_count * slot_count * block_rows * block_rows * column_count
    return pl.pallas_call(
        applied_kernel,
        grid_spec=grid_spec,
        out_shape=jax.ShapeDtypeStruct((block_count * block_rows, column_count), jnp.bfloat16),
        compiler_params=pltpu.CompilerParams(dimension_semantics=("arbitrary", "arbitrary")),
        cost_estimate=pl.CostEstimate(
            flops=flops, bytes_accessed=3 * ext_rows * column_count * 2, transcendentals=0
        ),
    )(offsets, mask, full_ops, extended)


def per_device(basis_matrix, operator_blocks, neighbours, neighbour_mask):
    local_rows, column_count = basis_matrix.shape
    block_count, slot_count, half_rows, block_rows = operator_blocks.shape
    sec = lax.axis_index("sec")
    col = lax.axis_index("col")
    row = 0
    for name, size in ROW_PARTS:
        row = row * size + lax.axis_index(name)

    share = block_count // 2
    mine = lax.dynamic_slice_in_dim(operator_blocks, col * share, share, 0)
    from_sec = lax.ppermute(mine, "sec", [(0, 1), (1, 0)])
    from_col = lax.ppermute(from_sec, "col", [(0, 1), (1, 0)])
    other_half = jnp.where(
        col == 0,
        jnp.concatenate([from_sec, from_col], axis=0),
        jnp.concatenate([from_col, from_sec], axis=0),
    )
    first = jnp.where(sec == 0, operator_blocks, other_half)
    second = jnp.where(sec == 0, other_half, operator_blocks)
    full_ops = jnp.concatenate([first, second], axis=2)

    other_basis = lax.ppermute(basis_matrix, "col", [(0, 1), (1, 0)])
    left_projector = jnp.where(sec == col, basis_matrix, other_basis)

    extended = halo(basis_matrix, REACH * block_rows)
    offsets = jnp.clip(neighbours - row * block_count + REACH, 0, block_count + 2 * REACH - 1)
    row_count = 1
    for _, size in ROW_PARTS:
        row_count *= size
    scaling = 1.0 / math.sqrt(local_rows * row_count)
    chunk_rows = left_projector.shape[1] // row_count
    sizes = dict(ROW_PARTS)
    parts, names, start = [], [], 0
    for order, units in ORDERS:
        width = units * UNIT
        applied = apply_operator(
            offsets.reshape(-1), neighbour_mask.reshape(-1), full_ops, extended, start, width
        )
        start += width
        part = scaling * lax.dot_general(
            left_projector, applied, (((0,), (0,)), ((), ())), preferred_element_type=jnp.float32
        )
        parts.append(part.reshape(tuple(size for _, size in ROW_PARTS) + (chunk_rows, width)))
        names.append(list(ROW))
    stages = len(ROW_PARTS)
    for stage in range(stages):
        axes = [order[stage] for order, _ in ORDERS]
        if sizes[axes[0]] == 2:
            continue
        pair_axis = None
        if stage + 1 < stages:
            following = [order[stage + 1] for order, _ in ORDERS]
            if sizes[following[0]] == 2 and len(set(following)) == 1 and stage + 2 == stages:
                pair_axis = following[0]
        inputs, shapes = [], []
        for index, axis in enumerate(axes):
            dim = names[index].index(axis)
            x = parts[index]
            shape = x.shape[:dim] + x.shape[dim + 1 :]
            names[index].remove(axis)
            if pair_axis is not None:
                shape = shape[1:]
                names[index].remove(pair_axis)
            shapes.append(shape)
            inputs.append(jnp.moveaxis(x, dim, 0).reshape(sizes[axis], -1, x.shape[-1]))
        plan = [(axis, sizes[axis], stage > 0 and sizes[axis] > 4) for axis in axes]
        outs = multi_ring_reduce(inputs, plan, stage, pair_axis)
        parts = [out.reshape(shape) for out, shape in zip(outs, shapes)]
    for index in range(len(parts)):
        for axis in list(names[index]):
            dim = names[index].index(axis)
            parts[index] = ring_sum(parts[index], dim, axis, sizes[axis])
            names[index].remove(axis)
    pieces = parts
    return jnp.concatenate(pieces, axis=-1)


def solution(mesh):
    sizes = [mesh.shape["sec"]] + [size for _, size in ROW_PARTS] + [mesh.shape["col"]]
    fine = Mesh(np.asarray(mesh.devices).reshape(sizes), ("sec",) + ROW + ("col",))
    return jax.shard_map(
        per_device,
        mesh=fine,
        in_specs=(P(ROW, "col"), P(ROW, None, "sec", None), P(ROW, None), P(ROW, None)),
        out_specs=P(("sec",) + ROW, "col"),
        check_vma=False,
    )
```

```python
import functools
import math

import jax
import jax.numpy as jnp
import numpy as np
from jax import lax
from jax.experimental import pallas as pl
from jax.experimental.pallas import tpu as pltpu
from jax.sharding import Mesh
from jax.sharding import PartitionSpec as P

REACH = 2
ROW_PARTS = (("z", 8), ("x", 4), ("y", 2))
ROW = tuple(name for name, _ in ROW_PARTS)
UNIT = 256
ORDERS = ((("z", "x", "y"), 4), (("x", "z", "y"), 4))
TILE_COLUMNS = 1024
STATIC_OFFSETS = (0, -1, 1, -2, 2)
WINDOW_SLOTS = tuple(range(len(STATIC_OFFSETS)))


def halo(shard, width):
    count = 1
    for _, size in ROW_PARTS:
        count *= size
    length = shard.shape[0]
    axes = ("sec",) + ROW

    def index(sec, row):
        return sec * count + row

    after_pairs, before_pairs = [], []
    for sec in range(2):
        for row in range(count):
            other = sec if row % 2 == 0 else 1 - sec
            if row + 1 < count:
                after_pairs.append((index(other, row + 1), index(sec, row)))
            other = 1 - sec if row % 2 == 0 else sec
            if row >= 1:
                before_pairs.append((index(other, row - 1), index(sec, row)))
    before = lax.ppermute(shard[length - width :], axes, before_pairs)
    after = lax.ppermute(shard[:width], axes, after_pairs)
    return jnp.concatenate([before, shard, after], axis=0)


def take_chunk(x, index, dim):
    return lax.dynamic_index_in_dim(x, index, axis=dim, keepdims=False)


def read_chunk(x, index, columns):
    if len(x.shape) == 3:
        return x[index, :, columns]
    value = x[:, index, :, columns]
    return value.reshape(value.shape[0] * value.shape[1], value.shape[2])


def multi_ring_kernel(plan, pair_axis, *refs):
    count = len(plan)
    x_refs, o_refs = refs[:count], refs[count : 2 * count]
    scratch = refs[2 * count : 2 * count + 7 * count]
    pair_scratch = refs[2 * count + 7 * count :]
    mesh = pl.DeviceIdType.MESH
    rings = []
    for index, (axis, n) in enumerate(plan):
        out_f, in_f, out_b, in_b, send_sem, recv_sem, credit_sem = scratch[7 * index : 7 * index + 7]
        p = lax.axis_index(axis)
        rings.append(
            dict(
                axis=axis, n=n, p=p, x=x_refs[index], o=o_refs[index],
                right=lax.rem(p + 1, n), left=lax.rem(p + n - 1, n),
                out_f=out_f, in_f=in_f, out_b=out_b, in_b=in_b,
                send=send_sem, recv=recv_sem, credit=credit_sem, copies=None,
            )
        )

    barrier = pltpu.get_barrier_semaphore()
    for ring in rings:
        for neighbour in (ring["left"], ring["right"]):
            pl.semaphore_signal(barrier, 1, device_id={ring["axis"]: neighbour}, device_id_type=mesh)
    signals = 2 * count
    if pair_axis is not None:
        partner = 1 - lax.axis_index(pair_axis)
        pl.semaphore_signal(barrier, 1, device_id={pair_axis: partner}, device_id_type=mesh)
        signals += 1
    pl.semaphore_wait(barrier, signals)

    ticks = max(n - 1 for _, n in plan)
    for tick in range(ticks):
        for ring in rings:
            n = ring["n"]
            due = [step for step in range(n - 1) if (step * ticks) // (n - 1) == tick]
            for step in due:
                if ring["copies"] is not None:
                    for copy in ring["copies"]:
                        copy.wait()
                    ring["copies"] = None
                slot = step % 2
                p, x, half = ring["p"], ring["x"], ring["x"].shape[-1] // 2
                chunk_f = lax.rem(p - step - 1 + 2 * n, n)
                chunk_b = lax.rem(p + step + 1, n)
                if step == 0:
                    ring["out_f"][slot] = read_chunk(x, chunk_f, slice(None, half))
                    ring["out_b"][slot] = read_chunk(x, chunk_b, slice(half, None))
                else:
                    ring["out_f"][slot] = ring["in_f"][1 - slot] + read_chunk(x, chunk_f, slice(None, half))
                    ring["out_b"][slot] = ring["in_b"][1 - slot] + read_chunk(x, chunk_b, slice(half, None))
                    if step <= n - 3:
                        pl.semaphore_signal(
                            ring["credit"].at[0], 1, device_id={ring["axis"]: ring["left"]}, device_id_type=mesh
                        )
                        pl.semaphore_signal(
                            ring["credit"].at[1], 1, device_id={ring["axis"]: ring["right"]}, device_id_type=mesh
                        )
                if step >= 2:
                    pl.semaphore_wait(ring["credit"].at[0], 1)
                    pl.semaphore_wait(ring["credit"].at[1], 1)
                copy_f = pltpu.make_async_remote_copy(
                    src_ref=ring["out_f"].at[slot], dst_ref=ring["in_f"].at[slot],
                    send_sem=ring["send"].at[0, slot], recv_sem=ring["recv"].at[0, slot],
                    device_id={ring["axis"]: ring["right"]}, device_id_type=mesh,
                )
                copy_b = pltpu.make_async_remote_copy(
                    src_ref=ring["out_b"].at[slot], dst_ref=ring["in_b"].at[slot],
                    send_sem=ring["send"].at[1, slot], recv_sem=ring["recv"].at[1, slot],
                    device_id={ring["axis"]: ring["left"]}, device_id_type=mesh,
                )
                copy_f.start()
                copy_b.start()
                ring["copies"] = (copy_f, copy_b)
    for index, ring in enumerate(rings):
        for copy in ring["copies"]:
            copy.wait()
        n, p, x = ring["n"], ring["p"], ring["x"]
        half = x.shape[-1] // 2
        last = (n - 2) % 2
        total = ring["o"] if pair_axis is None else pair_scratch[4 * index]
        total[:, :half] = ring["in_f"][last] + read_chunk(x, p, slice(None, half))
        total[:, half:] = ring["in_b"][last] + read_chunk(x, p, slice(half, None))
    if pair_axis is None:
        return
    mine = lax.axis_index(pair_axis)
    copies = []
    for index, ring in enumerate(rings):
        total, got, send_sem, recv_sem = pair_scratch[4 * index : 4 * index + 4]
        rows = got.shape[0]
        theirs = pl.multiple_of((1 - mine) * rows, rows)
        copy = pltpu.make_async_remote_copy(
            src_ref=total.at[pl.ds(theirs, rows)], dst_ref=got,
            send_sem=send_sem, recv_sem=recv_sem,
            device_id={pair_axis: 1 - mine}, device_id_type=mesh,
        )
        copy.start()
        copies.append(copy)
    for index, ring in enumerate(rings):
        total, got = pair_scratch[4 * index : 4 * index + 2]
        rows = got.shape[0]
        copies[index].wait()
        own = pl.multiple_of(mine * rows, rows)
        ring["o"][...] = got[...] + total[pl.ds(own, rows), :]


def multi_ring_reduce(inputs, plan, collective_id, pair_axis=None):
    vmem = pltpu.VMEM
    scratch = []
    out_shapes = []
    for x in inputs:
        rows, width = x.shape[-2], x.shape[-1]
        if len(x.shape) == 4:
            rows *= x.shape[0]
        out_shapes.append((rows, width))
        half = width // 2
        scratch += [vmem((2, rows, half), x.dtype) for _ in range(4)]
        scratch += [
            pltpu.SemaphoreType.DMA((2, 2)),
            pltpu.SemaphoreType.DMA((2, 2)),
            pltpu.SemaphoreType.REGULAR((2,)),
        ]
    if pair_axis is not None:
        for rows, width in list(out_shapes):
            x = inputs[0]
            scratch += [
                vmem((rows, width), x.dtype),
                vmem((rows // 2, width), x.dtype),
                pltpu.SemaphoreType.DMA(()),
                pltpu.SemaphoreType.DMA(()),
            ]
        out_shapes = [(rows // 2, width) for rows, width in out_shapes]
    return pl.pallas_call(
        functools.partial(multi_ring_kernel, tuple(plan), pair_axis),
        out_shape=[jax.ShapeDtypeStruct(shape, x.dtype) for shape, x in zip(out_shapes, inputs)],
        in_specs=[pl.BlockSpec(memory_space=vmem) for _ in inputs],
        out_specs=[pl.BlockSpec(memory_space=vmem) for _ in inputs],
        scratch_shapes=scratch,
        compiler_params=pltpu.CompilerParams(
            collective_id=collective_id, has_side_effects=True, vmem_limit_bytes=60 * 1024 * 1024
        ),
    )(*inputs)


def ring_sum(x, dim, axis, n):
    p = lax.axis_index(axis)
    partner = [(0, 1), (1, 0)]
    got = lax.ppermute(take_chunk(x, 1 - p, dim), axis, partner)
    return got + take_chunk(x, p, dim)


def applied_kernel(offsets_ref, mask_ref, ops_ref, ext_ref, out_ref):
    block = pl.program_id(1)
    slot_count, block_rows = ops_ref.shape[1], ops_ref.shape[2]
    order = [slot for _, slot in sorted(zip(STATIC_OFFSETS, WINDOW_SLOTS))]
    lhs = jnp.concatenate(
        [
            jnp.where(mask_ref[block * slot_count + slot] != 0, ops_ref[0, slot], 0)
            for slot in order
        ],
        axis=1,
    )
    first = pl.multiple_of(block * block_rows, block_rows)
    acc = jnp.dot(
        lhs, ext_ref[pl.ds(first, len(order) * block_rows), :], preferred_element_type=jnp.float32
    )
    for slot in range(len(WINDOW_SLOTS), slot_count):
        tile_index = offsets_ref[block * slot_count + slot]
        start = pl.multiple_of(tile_index * block_rows, block_rows)
        tile = ext_ref[pl.ds(start, block_rows), :]
        product = jnp.dot(ops_ref[0, slot], tile, preferred_element_type=jnp.float32)
        live = mask_ref[block * slot_count + slot] != 0
        acc = acc + jnp.where(live, product, 0.0)
    out_ref[...] = acc.astype(out_ref.dtype)


def apply_operator(offsets, mask, full_ops, extended, column_start, column_count):
    block_count, slot_count, block_rows, _ = full_ops.shape
    ext_rows = extended.shape[0]
    tile = min(TILE_COLUMNS, column_count)
    skip = column_start // tile
    grid_spec = pltpu.PrefetchScalarGridSpec(
        num_scalar_prefetch=2,
        grid=(column_count // tile, block_count),
        in_specs=[
            pl.BlockSpec((1, slot_count, block_rows, block_rows), lambda j, b, *_: (b, 0, 0, 0)),
            pl.BlockSpec((ext_rows, tile), lambda j, b, *_: (0, j + skip)),
        ],
        out_specs=pl.BlockSpec((block_rows, tile), lambda j, b, *_: (b, j)),
    )
    flops = 2 * block_count * slot_count * block_rows * block_rows * column_count
    return pl.pallas_call(
        applied_kernel,
        grid_spec=grid_spec,
        out_shape=jax.ShapeDtypeStruct((block_count * block_rows, column_count), jnp.bfloat16),
        compiler_params=pltpu.CompilerParams(dimension_semantics=("arbitrary", "arbitrary")),
        cost_estimate=pl.CostEstimate(
            flops=flops, bytes_accessed=3 * ext_rows * column_count * 2, transcendentals=0
        ),
    )(offsets, mask, full_ops, extended)


def per_device(basis_matrix, operator_blocks, neighbours, neighbour_mask):
    local_rows, column_count = basis_matrix.shape
    block_count, slot_count, half_rows, block_rows = operator_blocks.shape
    sec = lax.axis_index("sec")
    col = lax.axis_index("col")
    row = 0
    for name, size in ROW_PARTS:
        row = row * size + lax.axis_index(name)

    share = block_count // 2
    mine = lax.dynamic_slice_in_dim(operator_blocks, col * share, share, 0)
    from_sec = lax.ppermute(mine, "sec", [(0, 1), (1, 0)])
    from_col = lax.ppermute(from_sec, "col", [(0, 1), (1, 0)])
    other_half = jnp.where(
        col == 0,
        jnp.concatenate([from_sec, from_col], axis=0),
        jnp.concatenate([from_col, from_sec], axis=0),
    )
    first = jnp.where(sec == 0, operator_blocks, other_half)
    second = jnp.where(sec == 0, other_half, operator_blocks)
    full_ops = jnp.concatenate([first, second], axis=2)

    other_basis = lax.ppermute(basis_matrix, "col", [(0, 1), (1, 0)])
    left_projector = jnp.where(sec == col, basis_matrix, other_basis)

    extended = halo(basis_matrix, REACH * block_rows)
    offsets = jnp.clip(neighbours - row * block_count + REACH, 0, block_count + 2 * REACH - 1)
    row_count = 1
    for _, size in ROW_PARTS:
        row_count *= size
    scaling = 1.0 / math.sqrt(local_rows * row_count)
    chunk_rows = left_projector.shape[1] // row_count
    sizes = dict(ROW_PARTS)
    parts, names, start = [], [], 0
    for order, units in ORDERS:
        width = units * UNIT
        applied = apply_operator(
            offsets.reshape(-1), neighbour_mask.reshape(-1), full_ops, extended, start, width
        )
        start += width
        part = scaling * lax.dot_general(
            left_projector, applied, (((0,), (0,)), ((), ())), preferred_element_type=jnp.float32
        )
        parts.append(part.reshape(tuple(size for _, size in ROW_PARTS) + (chunk_rows, width)))
        names.append(list(ROW))
    stages = len(ROW_PARTS)
    for stage in range(stages):
        axes = [order[stage] for order, _ in ORDERS]
        if sizes[axes[0]] == 2:
            continue
        pair_axis = None
        if stage + 1 < stages:
            following = [order[stage + 1] for order, _ in ORDERS]
            if sizes[following[0]] == 2 and len(set(following)) == 1 and stage + 2 == stages:
                pair_axis = following[0]
        inputs, shapes = [], []
        for index, axis in enumerate(axes):
            dim = names[index].index(axis)
            x = parts[index]
            shape = x.shape[:dim] + x.shape[dim + 1 :]
            names[index].remove(axis)
            if pair_axis is not None:
                shape = shape[1:]
                names[index].remove(pair_axis)
            shapes.append(shape)
            if dim == 0:
                inputs.append(x.reshape(sizes[axis], -1, x.shape[-1]))
            else:
                outer = math.prod(x.shape[:dim])
                inputs.append(x.reshape(outer, sizes[axis], -1, x.shape[-1]))
        outs = multi_ring_reduce(
            inputs, [(axis, sizes[axis]) for axis in axes], stage, pair_axis
        )
        parts = [out.reshape(shape) for out, shape in zip(outs, shapes)]
    for index in range(len(parts)):
        for axis in list(names[index]):
            dim = names[index].index(axis)
            parts[index] = ring_sum(parts[index], dim, axis, sizes[axis])
            names[index].remove(axis)
    pieces = parts
    return jnp.concatenate(pieces, axis=-1)


def solution(mesh):
    sizes = [mesh.shape["sec"]] + [size for _, size in ROW_PARTS] + [mesh.shape["col"]]
    fine = Mesh(np.asarray(mesh.devices).reshape(sizes), ("sec",) + ROW + ("col",))
    return jax.shard_map(
        per_device,
        mesh=fine,
        in_specs=(P(ROW, "col"), P(ROW, None, "sec", None), P(ROW, None), P(ROW, None)),
        out_specs=P(("sec",) + ROW, "col"),
        check_vma=False,
    )
```

```python
import functools
import math

import jax
import jax.numpy as jnp
import numpy as np
from jax import lax
from jax.experimental import pallas as pl
from jax.experimental.pallas import tpu as pltpu
from jax.sharding import Mesh
from jax.sharding import PartitionSpec as P

REACH = 2
ROW_PARTS = (("z", 8), ("x", 4), ("y", 2))
ROW = tuple(name for name, _ in ROW_PARTS)
UNIT = 256
ORDERS = ((("z", "x", "y"), 4), (("x", "z", "y"), 4))
TILE_COLUMNS = 1024
STATIC_OFFSETS = (0, -1, 1, -2, 2)
WINDOW_SLOTS = tuple(range(len(STATIC_OFFSETS)))


def halo(shard, width):
    count = 1
    for _, size in ROW_PARTS:
        count *= size
    length = shard.shape[0]
    axes = ("sec",) + ROW

    def index(sec, row):
        return sec * count + row

    after_pairs, before_pairs = [], []
    for sec in range(2):
        for row in range(count):
            other = sec if row % 2 == 0 else 1 - sec
            if row + 1 < count:
                after_pairs.append((index(other, row + 1), index(sec, row)))
            other = 1 - sec if row % 2 == 0 else sec
            if row >= 1:
                before_pairs.append((index(other, row - 1), index(sec, row)))
    before = lax.ppermute(shard[length - width :], axes, before_pairs)
    after = lax.ppermute(shard[:width], axes, after_pairs)
    return jnp.concatenate([before, shard, after], axis=0)


def take_chunk(x, index, dim):
    return lax.dynamic_index_in_dim(x, index, axis=dim, keepdims=False)


def read_chunk(x, index, columns):
    if len(x.shape) == 3:
        return x[index, :, columns]
    value = x[:, index, :, columns]
    return value.reshape(value.shape[0] * value.shape[1], value.shape[2])


def multi_ring_kernel(plan, pair_axis, *refs):
    count = len(plan)
    x_refs, o_refs = refs[:count], refs[count : 2 * count]
    scratch = refs[2 * count : 2 * count + 7 * count]
    pair_scratch = refs[2 * count + 7 * count :]
    mesh = pl.DeviceIdType.MESH
    rings = []
    for index, (axis, n) in enumerate(plan):
        out_f, in_f, out_b, in_b, send_sem, recv_sem, credit_sem = scratch[7 * index : 7 * index + 7]
        p = lax.axis_index(axis)
        rings.append(
            dict(
                axis=axis, n=n, p=p, x=x_refs[index], o=o_refs[index],
                right=lax.rem(p + 1, n), left=lax.rem(p + n - 1, n),
                out_f=out_f, in_f=in_f, out_b=out_b, in_b=in_b,
                send=send_sem, recv=recv_sem, credit=credit_sem, copies=None,
            )
        )

    barrier = pltpu.get_barrier_semaphore()
    for ring in rings:
        for neighbour in (ring["left"], ring["right"]):
            pl.semaphore_signal(barrier, 1, device_id={ring["axis"]: neighbour}, device_id_type=mesh)
    signals = 2 * count
    if pair_axis is not None:
        partner = 1 - lax.axis_index(pair_axis)
        pl.semaphore_signal(barrier, 1, device_id={pair_axis: partner}, device_id_type=mesh)
        signals += 1
    pl.semaphore_wait(barrier, signals)

    ticks = max(n - 1 for _, n in plan)
    for tick in range(ticks):
        for ring in rings:
            n = ring["n"]
            due = [step for step in range(n - 1) if (step * ticks) // (n - 1) == tick]
            for step in due:
                if ring["copies"] is not None:
                    for copy in ring["copies"]:
                        copy.wait()
                    ring["copies"] = None
                slot = step % 2
                p, x, half = ring["p"], ring["x"], ring["x"].shape[-1] // 2
                chunk_f = lax.rem(p - step - 1 + 2 * n, n)
                chunk_b = lax.rem(p + step + 1, n)
                if step == 0:
                    ring["out_f"][slot] = read_chunk(x, chunk_f, slice(None, half))
                    ring["out_b"][slot] = read_chunk(x, chunk_b, slice(half, None))
                else:
                    ring["out_f"][slot] = ring["in_f"][step - 1] + read_chunk(x, chunk_f, slice(None, half))
                    ring["out_b"][slot] = ring["in_b"][step - 1] + read_chunk(x, chunk_b, slice(half, None))
                copy_f = pltpu.make_async_remote_copy(
                    src_ref=ring["out_f"].at[slot], dst_ref=ring["in_f"].at[step],
                    send_sem=ring["send"].at[0, slot], recv_sem=ring["recv"].at[0, step],
                    device_id={ring["axis"]: ring["right"]}, device_id_type=mesh,
                )
                copy_b = pltpu.make_async_remote_copy(
                    src_ref=ring["out_b"].at[slot], dst_ref=ring["in_b"].at[step],
                    send_sem=ring["send"].at[1, slot], recv_sem=ring["recv"].at[1, step],
                    device_id={ring["axis"]: ring["left"]}, device_id_type=mesh,
                )
                copy_f.start()
                copy_b.start()
                ring["copies"] = (copy_f, copy_b)
    for index, ring in enumerate(rings):
        for copy in ring["copies"]:
            copy.wait()
        n, p, x = ring["n"], ring["p"], ring["x"]
        half = x.shape[-1] // 2
        last = n - 2
        total = ring["o"] if pair_axis is None else pair_scratch[4 * index]
        total[:, :half] = ring["in_f"][last] + read_chunk(x, p, slice(None, half))
        total[:, half:] = ring["in_b"][last] + read_chunk(x, p, slice(half, None))
    if pair_axis is None:
        return
    mine = lax.axis_index(pair_axis)
    copies = []
    for index, ring in enumerate(rings):
        total, got, send_sem, recv_sem = pair_scratch[4 * index : 4 * index + 4]
        rows = got.shape[0]
        theirs = pl.multiple_of((1 - mine) * rows, rows)
        copy = pltpu.make_async_remote_copy(
            src_ref=total.at[pl.ds(theirs, rows)], dst_ref=got,
            send_sem=send_sem, recv_sem=recv_sem,
            device_id={pair_axis: 1 - mine}, device_id_type=mesh,
        )
        copy.start()
        copies.append(copy)
    for index, ring in enumerate(rings):
        total, got = pair_scratch[4 * index : 4 * index + 2]
        rows = got.shape[0]
        copies[index].wait()
        own = pl.multiple_of(mine * rows, rows)
        ring["o"][...] = got[...] + total[pl.ds(own, rows), :]


def multi_ring_reduce(inputs, plan, collective_id, pair_axis=None):
    vmem = pltpu.VMEM
    scratch = []
    out_shapes = []
    for x, (_, n) in zip(inputs, plan):
        rows, width = x.shape[-2], x.shape[-1]
        if len(x.shape) == 4:
            rows *= x.shape[0]
        out_shapes.append((rows, width))
        half = width // 2
        scratch += [
            vmem((2, rows, half), x.dtype),
            vmem((n - 1, rows, half), x.dtype),
            vmem((2, rows, half), x.dtype),
            vmem((n - 1, rows, half), x.dtype),
            pltpu.SemaphoreType.DMA((2, 2)),
            pltpu.SemaphoreType.DMA((2, n - 1)),
            pltpu.SemaphoreType.REGULAR((2,)),
        ]
    if pair_axis is not None:
        for rows, width in list(out_shapes):
            x = inputs[0]
            scratch += [
                vmem((rows, width), x.dtype),
                vmem((rows // 2, width), x.dtype),
                pltpu.SemaphoreType.DMA(()),
                pltpu.SemaphoreType.DMA(()),
            ]
        out_shapes = [(rows // 2, width) for rows, width in out_shapes]
    return pl.pallas_call(
        functools.partial(multi_ring_kernel, tuple(plan), pair_axis),
        out_shape=[jax.ShapeDtypeStruct(shape, x.dtype) for shape, x in zip(out_shapes, inputs)],
        in_specs=[pl.BlockSpec(memory_space=vmem) for _ in inputs],
        out_specs=[pl.BlockSpec(memory_space=vmem) for _ in inputs],
        scratch_shapes=scratch,
        compiler_params=pltpu.CompilerParams(
            collective_id=collective_id, has_side_effects=True, vmem_limit_bytes=60 * 1024 * 1024
        ),
    )(*inputs)


def ring_sum(x, dim, axis, n):
    p = lax.axis_index(axis)
    partner = [(0, 1), (1, 0)]
    got = lax.ppermute(take_chunk(x, 1 - p, dim), axis, partner)
    return got + take_chunk(x, p, dim)


def applied_kernel(offsets_ref, mask_ref, ops_ref, ext_ref, out_ref):
    block = pl.program_id(1)
    slot_count, block_rows = ops_ref.shape[1], ops_ref.shape[2]
    order = [slot for _, slot in sorted(zip(STATIC_OFFSETS, WINDOW_SLOTS))]
    lhs = jnp.concatenate(
        [
            jnp.where(mask_ref[block * slot_count + slot] != 0, ops_ref[0, slot], 0)
            for slot in order
        ],
        axis=1,
    )
    first = pl.multiple_of(block * block_rows, block_rows)
    acc = jnp.dot(
        lhs, ext_ref[pl.ds(first, len(order) * block_rows), :], preferred_element_type=jnp.float32
    )
    for slot in range(len(WINDOW_SLOTS), slot_count):
        tile_index = offsets_ref[block * slot_count + slot]
        start = pl.multiple_of(tile_index * block_rows, block_rows)
        tile = ext_ref[pl.ds(start, block_rows), :]
        product = jnp.dot(ops_ref[0, slot], tile, preferred_element_type=jnp.float32)
        live = mask_ref[block * slot_count + slot] != 0
        acc = acc + jnp.where(live, product, 0.0)
    out_ref[...] = acc.astype(out_ref.dtype)


def apply_operator(offsets, mask, full_ops, extended, column_start, column_count):
    block_count, slot_count, block_rows, _ = full_ops.shape
    ext_rows = extended.shape[0]
    tile = min(TILE_COLUMNS, column_count)
    skip = column_start // tile
    grid_spec = pltpu.PrefetchScalarGridSpec(
        num_scalar_prefetch=2,
        grid=(column_count // tile, block_count),
        in_specs=[
            pl.BlockSpec((1, slot_count, block_rows, block_rows), lambda j, b, *_: (b, 0, 0, 0)),
            pl.BlockSpec((ext_rows, tile), lambda j, b, *_: (0, j + skip)),
        ],
        out_specs=pl.BlockSpec((block_rows, tile), lambda j, b, *_: (b, j)),
    )
    flops = 2 * block_count * slot_count * block_rows * block_rows * column_count
    return pl.pallas_call(
        applied_kernel,
        grid_spec=grid_spec,
        out_shape=jax.ShapeDtypeStruct((block_count * block_rows, column_count), jnp.bfloat16),
        compiler_params=pltpu.CompilerParams(dimension_semantics=("arbitrary", "arbitrary")),
        cost_estimate=pl.CostEstimate(
            flops=flops, bytes_accessed=3 * ext_rows * column_count * 2, transcendentals=0
        ),
    )(offsets, mask, full_ops, extended)


def per_device(basis_matrix, operator_blocks, neighbours, neighbour_mask):
    local_rows, column_count = basis_matrix.shape
    block_count, slot_count, half_rows, block_rows = operator_blocks.shape
    sec = lax.axis_index("sec")
    col = lax.axis_index("col")
    row = 0
    for name, size in ROW_PARTS:
        row = row * size + lax.axis_index(name)

    share = block_count // 2
    mine = lax.dynamic_slice_in_dim(operator_blocks, col * share, share, 0)
    from_sec = lax.ppermute(mine, "sec", [(0, 1), (1, 0)])
    from_col = lax.ppermute(from_sec, "col", [(0, 1), (1, 0)])
    other_half = jnp.where(
        col == 0,
        jnp.concatenate([from_sec, from_col], axis=0),
        jnp.concatenate([from_col, from_sec], axis=0),
    )
    first = jnp.where(sec == 0, operator_blocks, other_half)
    second = jnp.where(sec == 0, other_half, operator_blocks)
    full_ops = jnp.concatenate([first, second], axis=2)

    other_basis = lax.ppermute(basis_matrix, "col", [(0, 1), (1, 0)])
    left_projector = jnp.where(sec == col, basis_matrix, other_basis)

    extended = halo(basis_matrix, REACH * block_rows)
    offsets = jnp.clip(neighbours - row * block_count + REACH, 0, block_count + 2 * REACH - 1)
    row_count = 1
    for _, size in ROW_PARTS:
        row_count *= size
    scaling = 1.0 / math.sqrt(local_rows * row_count)
    chunk_rows = left_projector.shape[1] // row_count
    sizes = dict(ROW_PARTS)
    parts, names, start = [], [], 0
    for order, units in ORDERS:
        width = units * UNIT
        applied = apply_operator(
            offsets.reshape(-1), neighbour_mask.reshape(-1), full_ops, extended, start, width
        )
        start += width
        part = scaling * lax.dot_general(
            left_projector, applied, (((0,), (0,)), ((), ())), preferred_element_type=jnp.float32
        )
        parts.append(part.reshape(tuple(size for _, size in ROW_PARTS) + (chunk_rows, width)))
        names.append(list(ROW))
    stages = len(ROW_PARTS)
    for stage in range(stages):
        axes = [order[stage] for order, _ in ORDERS]
        if sizes[axes[0]] == 2:
            continue
        pair_axis = None
        if stage + 1 < stages:
            following = [order[stage + 1] for order, _ in ORDERS]
            if sizes[following[0]] == 2 and len(set(following)) == 1 and stage + 2 == stages:
                pair_axis = following[0]
        inputs, shapes = [], []
        for index, axis in enumerate(axes):
            dim = names[index].index(axis)
            x = parts[index]
            shape = x.shape[:dim] + x.shape[dim + 1 :]
            names[index].remove(axis)
            if pair_axis is not None:
                shape = shape[1:]
                names[index].remove(pair_axis)
            shapes.append(shape)
            if dim == 0:
                inputs.append(x.reshape(sizes[axis], -1, x.shape[-1]))
            else:
                outer = math.prod(x.shape[:dim])
                inputs.append(x.reshape(outer, sizes[axis], -1, x.shape[-1]))
        outs = multi_ring_reduce(
            inputs, [(axis, sizes[axis]) for axis in axes], stage, pair_axis
        )
        parts = [out.reshape(shape) for out, shape in zip(outs, shapes)]
    for index in range(len(parts)):
        for axis in list(names[index]):
            dim = names[index].index(axis)
            parts[index] = ring_sum(parts[index], dim, axis, sizes[axis])
            names[index].remove(axis)
    pieces = parts
    return jnp.concatenate(pieces, axis=-1)


def solution(mesh):
    sizes = [mesh.shape["sec"]] + [size for _, size in ROW_PARTS] + [mesh.shape["col"]]
    fine = Mesh(np.asarray(mesh.devices).reshape(sizes), ("sec",) + ROW + ("col",))
    return jax.shard_map(
        per_device,
        mesh=fine,
        in_specs=(P(ROW, "col"), P(ROW, None, "sec", None), P(ROW, None), P(ROW, None)),
        out_specs=P(("sec",) + ROW, "col"),
        check_vma=False,
    )
```

```python
import functools
import math

import jax
import jax.numpy as jnp
import numpy as np
from jax import lax
from jax.experimental import pallas as pl
from jax.experimental.pallas import tpu as pltpu
from jax.sharding import Mesh
from jax.sharding import PartitionSpec as P

REACH = 2
ROW_PARTS = (("z", 8), ("x", 4), ("y", 2))
ROW = tuple(name for name, _ in ROW_PARTS)
UNIT = 256
ORDERS = ((("z", "x", "y"), 4), (("x", "z", "y"), 4))
TILE_COLUMNS = 1024
STATIC_OFFSETS = (0, -1, 1, -2, 2)
WINDOW_SLOTS = tuple(range(len(STATIC_OFFSETS)))


def halo(shard, width):
    count = 1
    for _, size in ROW_PARTS:
        count *= size
    length = shard.shape[0]
    axes = ("sec",) + ROW

    def index(sec, row):
        return sec * count + row

    after_pairs, before_pairs = [], []
    for sec in range(2):
        for row in range(count):
            other = sec if row % 2 == 0 else 1 - sec
            if row + 1 < count:
                after_pairs.append((index(other, row + 1), index(sec, row)))
            other = 1 - sec if row % 2 == 0 else sec
            if row >= 1:
                before_pairs.append((index(other, row - 1), index(sec, row)))
    before = lax.ppermute(shard[length - width :], axes, before_pairs)
    after = lax.ppermute(shard[:width], axes, after_pairs)
    return jnp.concatenate([before, shard, after], axis=0)


def take_chunk(x, index, dim):
    return lax.dynamic_index_in_dim(x, index, axis=dim, keepdims=False)


def read_chunk(x, index, columns):
    if len(x.shape) == 3:
        return x[index, :, columns]
    value = x[:, index, :, columns]
    return value.reshape(value.shape[0] * value.shape[1], value.shape[2])


def multi_ring_kernel(plan, pairs, *refs):
    count = len(plan)
    x_refs, o_refs = refs[:count], refs[count : 2 * count]
    scratch = refs[2 * count : 2 * count + 7 * count]
    pair_scratch = refs[2 * count + 7 * count :]
    mesh = pl.DeviceIdType.MESH
    rings = []
    for index, (axis, n) in enumerate(plan):
        out_f, in_f, out_b, in_b, send_sem, recv_sem, credit_sem = scratch[7 * index : 7 * index + 7]
        p = lax.axis_index(axis)
        rings.append(
            dict(
                axis=axis, n=n, p=p, x=x_refs[index], o=o_refs[index],
                right=lax.rem(p + 1, n), left=lax.rem(p + n - 1, n),
                out_f=out_f, in_f=in_f, out_b=out_b, in_b=in_b,
                send=send_sem, recv=recv_sem, credit=credit_sem, copies=None,
            )
        )

    barrier = pltpu.get_barrier_semaphore()
    for ring in rings:
        for neighbour in (ring["left"], ring["right"]):
            pl.semaphore_signal(barrier, 1, device_id={ring["axis"]: neighbour}, device_id_type=mesh)
    signals = 2 * count
    pair_axes = sorted({pair[0] for pair in pairs if pair is not None})
    for pair_axis in pair_axes:
        partner = 1 - lax.axis_index(pair_axis)
        pl.semaphore_signal(barrier, 1, device_id={pair_axis: partner}, device_id_type=mesh)
        signals += 1
    pl.semaphore_wait(barrier, signals)

    ticks = max(n - 1 for _, n in plan)
    for tick in range(ticks):
        for ring in rings:
            n = ring["n"]
            due = [step for step in range(n - 1) if (step * ticks) // (n - 1) == tick]
            for step in due:
                if ring["copies"] is not None:
                    for copy in ring["copies"]:
                        copy.wait()
                    ring["copies"] = None
                slot = step % 2
                p, x, half = ring["p"], ring["x"], ring["x"].shape[-1] // 2
                chunk_f = lax.rem(p - step - 1 + 2 * n, n)
                chunk_b = lax.rem(p + step + 1, n)
                if step == 0:
                    ring["out_f"][slot] = read_chunk(x, chunk_f, slice(None, half))
                    ring["out_b"][slot] = read_chunk(x, chunk_b, slice(half, None))
                else:
                    ring["out_f"][slot] = ring["in_f"][1 - slot] + read_chunk(x, chunk_f, slice(None, half))
                    ring["out_b"][slot] = ring["in_b"][1 - slot] + read_chunk(x, chunk_b, slice(half, None))
                    if step <= n - 3:
                        pl.semaphore_signal(
                            ring["credit"].at[0], 1, device_id={ring["axis"]: ring["left"]}, device_id_type=mesh
                        )
                        pl.semaphore_signal(
                            ring["credit"].at[1], 1, device_id={ring["axis"]: ring["right"]}, device_id_type=mesh
                        )
                if step >= 2:
                    pl.semaphore_wait(ring["credit"].at[0], 1)
                    pl.semaphore_wait(ring["credit"].at[1], 1)
                copy_f = pltpu.make_async_remote_copy(
                    src_ref=ring["out_f"].at[slot], dst_ref=ring["in_f"].at[slot],
                    send_sem=ring["send"].at[0, slot], recv_sem=ring["recv"].at[0, slot],
                    device_id={ring["axis"]: ring["right"]}, device_id_type=mesh,
                )
                copy_b = pltpu.make_async_remote_copy(
                    src_ref=ring["out_b"].at[slot], dst_ref=ring["in_b"].at[slot],
                    send_sem=ring["send"].at[1, slot], recv_sem=ring["recv"].at[1, slot],
                    device_id={ring["axis"]: ring["left"]}, device_id_type=mesh,
                )
                copy_f.start()
                copy_b.start()
                ring["copies"] = (copy_f, copy_b)
    pending = []
    for index in sorted(range(count), key=lambda i: rings[i]["n"]):
        ring = rings[index]
        for copy in ring["copies"]:
            copy.wait()
        n, p, x = ring["n"], ring["p"], ring["x"]
        half = x.shape[-1] // 2
        last = (n - 2) % 2
        forward = ring["in_f"][last] + read_chunk(x, p, slice(None, half))
        backward = ring["in_b"][last] + read_chunk(x, p, slice(half, None))
        if pairs[index] is None:
            ring["o"][:, :half] = forward
            ring["o"][:, half:] = backward
            continue
        pair_axis, _ = pairs[index]
        total, got, send_sem, recv_sem = pair_scratch[4 * index : 4 * index + 4]
        outer, _, rows, _ = total.shape
        total[:, :, :, :half] = forward.reshape(outer, 2, rows, half)
        total[:, :, :, half:] = backward.reshape(outer, 2, rows, half)
        mine = lax.axis_index(pair_axis)
        copy = pltpu.make_async_remote_copy(
            src_ref=total.at[:, pl.ds(1 - mine, 1)], dst_ref=got,
            send_sem=send_sem, recv_sem=recv_sem,
            device_id={pair_axis: 1 - mine}, device_id_type=mesh,
        )
        copy.start()
        pending.append((index, copy, mine))
    for index, copy, mine in pending:
        total, got = pair_scratch[4 * index : 4 * index + 2]
        outer, _, rows, width = total.shape
        copy.wait()
        summed = got[...] + total[:, pl.ds(mine, 1)]
        rings[index]["o"][...] = summed.reshape(outer * rows, width)


def multi_ring_reduce(inputs, plan, collective_id, pairs):
    vmem = pltpu.VMEM
    scratch, pair_scratch, out_shapes = [], [], []
    for x, pair in zip(inputs, pairs):
        rows, width = x.shape[-2], x.shape[-1]
        if len(x.shape) == 4:
            rows *= x.shape[0]
        half = width // 2
        scratch += [vmem((2, rows, half), x.dtype) for _ in range(4)]
        scratch += [
            pltpu.SemaphoreType.DMA((2, 2)),
            pltpu.SemaphoreType.DMA((2, 2)),
            pltpu.SemaphoreType.REGULAR((2,)),
        ]
        if pair is None:
            out_shapes.append((rows, width))
            pair_scratch += [vmem((8, 128), x.dtype), vmem((8, 128), x.dtype)]
        else:
            outer = pair[1]
            inner = rows // (2 * outer)
            out_shapes.append((rows // 2, width))
            pair_scratch += [
                vmem((outer, 2, inner, width), x.dtype),
                vmem((outer, 1, inner, width), x.dtype),
            ]
        pair_scratch += [pltpu.SemaphoreType.DMA(()), pltpu.SemaphoreType.DMA(())]
    scratch += pair_scratch
    return pl.pallas_call(
        functools.partial(multi_ring_kernel, tuple(plan), tuple(pairs)),
        out_shape=[jax.ShapeDtypeStruct(shape, x.dtype) for shape, x in zip(out_shapes, inputs)],
        in_specs=[pl.BlockSpec(memory_space=vmem) for _ in inputs],
        out_specs=[pl.BlockSpec(memory_space=vmem) for _ in inputs],
        scratch_shapes=scratch,
        compiler_params=pltpu.CompilerParams(
            collective_id=collective_id, has_side_effects=True, vmem_limit_bytes=60 * 1024 * 1024
        ),
    )(*inputs)


def ring_sum(x, dim, axis, n):
    p = lax.axis_index(axis)
    partner = [(0, 1), (1, 0)]
    got = lax.ppermute(take_chunk(x, 1 - p, dim), axis, partner)
    return got + take_chunk(x, p, dim)


def applied_kernel(offsets_ref, mask_ref, ops_ref, ext_ref, out_ref):
    block = pl.program_id(1)
    slot_count, block_rows = ops_ref.shape[1], ops_ref.shape[2]
    order = [slot for _, slot in sorted(zip(STATIC_OFFSETS, WINDOW_SLOTS))]
    lhs = jnp.concatenate(
        [
            jnp.where(mask_ref[block * slot_count + slot] != 0, ops_ref[0, slot], 0)
            for slot in order
        ],
        axis=1,
    )
    first = pl.multiple_of(block * block_rows, block_rows)
    acc = jnp.dot(
        lhs, ext_ref[pl.ds(first, len(order) * block_rows), :], preferred_element_type=jnp.float32
    )
    for slot in range(len(WINDOW_SLOTS), slot_count):
        tile_index = offsets_ref[block * slot_count + slot]
        start = pl.multiple_of(tile_index * block_rows, block_rows)
        tile = ext_ref[pl.ds(start, block_rows), :]
        product = jnp.dot(ops_ref[0, slot], tile, preferred_element_type=jnp.float32)
        live = mask_ref[block * slot_count + slot] != 0
        acc = acc + jnp.where(live, product, 0.0)
    out_ref[...] = acc.astype(out_ref.dtype)


def apply_operator(offsets, mask, full_ops, extended, column_start, column_count):
    block_count, slot_count, block_rows, _ = full_ops.shape
    ext_rows = extended.shape[0]
    tile = min(TILE_COLUMNS, column_count)
    skip = column_start // tile
    grid_spec = pltpu.PrefetchScalarGridSpec(
        num_scalar_prefetch=2,
        grid=(column_count // tile, block_count),
        in_specs=[
            pl.BlockSpec((1, slot_count, block_rows, block_rows), lambda j, b, *_: (b, 0, 0, 0)),
            pl.BlockSpec((ext_rows, tile), lambda j, b, *_: (0, j + skip)),
        ],
        out_specs=pl.BlockSpec((block_rows, tile), lambda j, b, *_: (b, j)),
    )
    flops = 2 * block_count * slot_count * block_rows * block_rows * column_count
    return pl.pallas_call(
        applied_kernel,
        grid_spec=grid_spec,
        out_shape=jax.ShapeDtypeStruct((block_count * block_rows, column_count), jnp.bfloat16),
        compiler_params=pltpu.CompilerParams(dimension_semantics=("arbitrary", "arbitrary")),
        cost_estimate=pl.CostEstimate(
            flops=flops, bytes_accessed=3 * ext_rows * column_count * 2, transcendentals=0
        ),
    )(offsets, mask, full_ops, extended)


def per_device(basis_matrix, operator_blocks, neighbours, neighbour_mask):
    local_rows, column_count = basis_matrix.shape
    block_count, slot_count, half_rows, block_rows = operator_blocks.shape
    sec = lax.axis_index("sec")
    col = lax.axis_index("col")
    row = 0
    for name, size in ROW_PARTS:
        row = row * size + lax.axis_index(name)

    share = block_count // 2
    mine = lax.dynamic_slice_in_dim(operator_blocks, col * share, share, 0)
    from_sec = lax.ppermute(mine, "sec", [(0, 1), (1, 0)])
    from_col = lax.ppermute(from_sec, "col", [(0, 1), (1, 0)])
    other_half = jnp.where(
        col == 0,
        jnp.concatenate([from_sec, from_col], axis=0),
        jnp.concatenate([from_col, from_sec], axis=0),
    )
    first = jnp.where(sec == 0, operator_blocks, other_half)
    second = jnp.where(sec == 0, other_half, operator_blocks)
    full_ops = jnp.concatenate([first, second], axis=2)

    other_basis = lax.ppermute(basis_matrix, "col", [(0, 1), (1, 0)])
    left_projector = jnp.where(sec == col, basis_matrix, other_basis)

    extended = halo(basis_matrix, REACH * block_rows)
    offsets = jnp.clip(neighbours - row * block_count + REACH, 0, block_count + 2 * REACH - 1)
    row_count = 1
    for _, size in ROW_PARTS:
        row_count *= size
    scaling = 1.0 / math.sqrt(local_rows * row_count)
    chunk_rows = left_projector.shape[1] // row_count
    sizes = dict(ROW_PARTS)
    parts, names, start = [], [], 0
    for order, units in ORDERS:
        width = units * UNIT
        applied = apply_operator(
            offsets.reshape(-1), neighbour_mask.reshape(-1), full_ops, extended, start, width
        )
        start += width
        part = scaling * lax.dot_general(
            left_projector, applied, (((0,), (0,)), ((), ())), preferred_element_type=jnp.float32
        )
        parts.append(part.reshape(tuple(size for _, size in ROW_PARTS) + (chunk_rows, width)))
        names.append(list(ROW))
    (first_order, _), (second_order, _) = ORDERS
    assert first_order == ("z", "x", "y") and second_order == ("x", "z", "y")
    nz, nx, ny = sizes["z"], sizes["x"], sizes["y"]
    a, b = parts
    width_a, width_b = a.shape[-1], b.shape[-1]
    a, b = multi_ring_reduce(
        [a.reshape(nz, -1, width_a), b.reshape(nz, nx, -1, width_b)],
        [("z", nz), ("x", nx)],
        0,
        [None, ("y", nz)],
    )
    a, b = multi_ring_reduce(
        [a.reshape(nx, -1, width_a), b.reshape(nz, -1, width_b)],
        [("x", nx), ("z", nz)],
        1,
        [("y", 1), None],
    )
    parts = [a, b]
    pieces = parts
    return jnp.concatenate(pieces, axis=-1)


def solution(mesh):
    sizes = [mesh.shape["sec"]] + [size for _, size in ROW_PARTS] + [mesh.shape["col"]]
    fine = Mesh(np.asarray(mesh.devices).reshape(sizes), ("sec",) + ROW + ("col",))
    return jax.shard_map(
        per_device,
        mesh=fine,
        in_specs=(P(ROW, "col"), P(ROW, None, "sec", None), P(ROW, None), P(ROW, None)),
        out_specs=P(("sec",) + ROW, "col"),
        check_vma=False,
    )
```

```python
import functools
import math

import jax
import jax.numpy as jnp
import numpy as np
from jax import lax
from jax.experimental import pallas as pl
from jax.experimental.pallas import tpu as pltpu
from jax.sharding import Mesh
from jax.sharding import PartitionSpec as P

REACH = 2
ROW_PARTS = (("z", 8), ("x", 4), ("y", 2))
ROW = tuple(name for name, _ in ROW_PARTS)
UNIT = 256
ORDERS = ((("z", "x", "y"), 4), (("x", "z", "y"), 4))
TILE_COLUMNS = 1024
STATIC_OFFSETS = (0, -1, 1, -2, 2)
WINDOW_SLOTS = tuple(range(len(STATIC_OFFSETS)))


def halo(shard, width):
    count = 1
    for _, size in ROW_PARTS:
        count *= size
    length = shard.shape[0]
    axes = ("sec",) + ROW

    def index(sec, row):
        return sec * count + row

    after_pairs, before_pairs = [], []
    for sec in range(2):
        for row in range(count):
            other = sec if row % 2 == 0 else 1 - sec
            if row + 1 < count:
                after_pairs.append((index(other, row + 1), index(sec, row)))
            other = 1 - sec if row % 2 == 0 else sec
            if row >= 1:
                before_pairs.append((index(other, row - 1), index(sec, row)))
    before = lax.ppermute(shard[length - width :], axes, before_pairs)
    after = lax.ppermute(shard[:width], axes, after_pairs)
    return jnp.concatenate([before, shard, after], axis=0)


def take_chunk(x, index, dim):
    return lax.dynamic_index_in_dim(x, index, axis=dim, keepdims=False)


def read_chunk(x, index, columns):
    if len(x.shape) == 3:
        return x[index, :, columns]
    value = x[:, index, :, columns]
    return value.reshape(value.shape[0] * value.shape[1], value.shape[2])


def multi_ring_kernel(plan, pairs, *refs):
    count = len(plan)
    x_refs, o_refs = refs[:count], refs[count : 2 * count]
    scratch = refs[2 * count : 2 * count + 7 * count]
    pair_scratch = refs[2 * count + 7 * count :]
    mesh = pl.DeviceIdType.MESH
    rings = []
    for index, (axis, n) in enumerate(plan):
        out_f, in_f, out_b, in_b, send_sem, recv_sem, credit_sem = scratch[7 * index : 7 * index + 7]
        p = lax.axis_index(axis)
        rings.append(
            dict(
                axis=axis, n=n, p=p, x=x_refs[index], o=o_refs[index],
                right=lax.rem(p + 1, n), left=lax.rem(p + n - 1, n),
                out_f=out_f, in_f=in_f, out_b=out_b, in_b=in_b,
                send=send_sem, recv=recv_sem, credit=credit_sem, copies=None,
            )
        )

    barrier = pltpu.get_barrier_semaphore()
    for ring in rings:
        for neighbour in (ring["left"], ring["right"]):
            pl.semaphore_signal(barrier, 1, device_id={ring["axis"]: neighbour}, device_id_type=mesh)
    signals = 2 * count
    pair_axes = sorted({pair[0] for pair in pairs if pair is not None})
    for pair_axis in pair_axes:
        partner = 1 - lax.axis_index(pair_axis)
        pl.semaphore_signal(barrier, 1, device_id={pair_axis: partner}, device_id_type=mesh)
        signals += 1
    pl.semaphore_wait(barrier, signals)

    pending = []

    def finish(index):
        ring = rings[index]
        for copy in ring["copies"]:
            copy.wait()
        n, p, x = ring["n"], ring["p"], ring["x"]
        half = x.shape[-1] // 2
        last = (n - 2) % 2
        forward = ring["in_f"][last] + read_chunk(x, p, slice(None, half))
        backward = ring["in_b"][last] + read_chunk(x, p, slice(half, None))
        if pairs[index] is None:
            ring["o"][:, :half] = forward
            ring["o"][:, half:] = backward
            return
        pair_axis, _ = pairs[index]
        total, got, send_sem, recv_sem = pair_scratch[4 * index : 4 * index + 4]
        outer, _, rows, _ = total.shape
        total[:, :, :, :half] = forward.reshape(outer, 2, rows, half)
        total[:, :, :, half:] = backward.reshape(outer, 2, rows, half)
        mine = lax.axis_index(pair_axis)
        copy = pltpu.make_async_remote_copy(
            src_ref=total.at[:, pl.ds(1 - mine, 1)], dst_ref=got,
            send_sem=send_sem, recv_sem=recv_sem,
            device_id={pair_axis: 1 - mine}, device_id_type=mesh,
        )
        copy.start()
        pending.append((index, copy, mine))

    done = set()
    ticks = max(n - 1 for _, n in plan)
    for tick in range(ticks):
        for ring in rings:
            n = ring["n"]
            due = [step for step in range(n - 1) if (step * ticks) // (n - 1) == tick]
            for step in due:
                if ring["copies"] is not None:
                    for copy in ring["copies"]:
                        copy.wait()
                    ring["copies"] = None
                slot = step % 2
                p, x, half = ring["p"], ring["x"], ring["x"].shape[-1] // 2
                chunk_f = lax.rem(p - step - 1 + 2 * n, n)
                chunk_b = lax.rem(p + step + 1, n)
                if step == 0:
                    ring["out_f"][slot] = read_chunk(x, chunk_f, slice(None, half))
                    ring["out_b"][slot] = read_chunk(x, chunk_b, slice(half, None))
                else:
                    ring["out_f"][slot] = ring["in_f"][1 - slot] + read_chunk(x, chunk_f, slice(None, half))
                    ring["out_b"][slot] = ring["in_b"][1 - slot] + read_chunk(x, chunk_b, slice(half, None))
                    if step <= n - 3:
                        pl.semaphore_signal(
                            ring["credit"].at[0], 1, device_id={ring["axis"]: ring["left"]}, device_id_type=mesh
                        )
                        pl.semaphore_signal(
                            ring["credit"].at[1], 1, device_id={ring["axis"]: ring["right"]}, device_id_type=mesh
                        )
                if step >= 2:
                    pl.semaphore_wait(ring["credit"].at[0], 1)
                    pl.semaphore_wait(ring["credit"].at[1], 1)
                copy_f = pltpu.make_async_remote_copy(
                    src_ref=ring["out_f"].at[slot], dst_ref=ring["in_f"].at[slot],
                    send_sem=ring["send"].at[0, slot], recv_sem=ring["recv"].at[0, slot],
                    device_id={ring["axis"]: ring["right"]}, device_id_type=mesh,
                )
                copy_b = pltpu.make_async_remote_copy(
                    src_ref=ring["out_b"].at[slot], dst_ref=ring["in_b"].at[slot],
                    send_sem=ring["send"].at[1, slot], recv_sem=ring["recv"].at[1, slot],
                    device_id={ring["axis"]: ring["left"]}, device_id_type=mesh,
                )
                copy_f.start()
                copy_b.start()
                ring["copies"] = (copy_f, copy_b)
        for index, ring in enumerate(rings):
            last_tick = ((ring["n"] - 2) * ticks) // (ring["n"] - 1)
            if pairs[index] is not None and last_tick + 1 == tick:
                finish(index)
                done.add(index)
    for index in sorted(range(count), key=lambda i: rings[i]["n"]):
        if index not in done:
            finish(index)
    for index, copy, mine in pending:
        total, got = pair_scratch[4 * index : 4 * index + 2]
        outer, _, rows, width = total.shape
        copy.wait()
        summed = got[...] + total[:, pl.ds(mine, 1)]
        rings[index]["o"][...] = summed.reshape(outer * rows, width)


def multi_ring_reduce(inputs, plan, collective_id, pairs):
    vmem = pltpu.VMEM
    scratch, pair_scratch, out_shapes = [], [], []
    for x, pair in zip(inputs, pairs):
        rows, width = x.shape[-2], x.shape[-1]
        if len(x.shape) == 4:
            rows *= x.shape[0]
        half = width // 2
        scratch += [vmem((2, rows, half), x.dtype) for _ in range(4)]
        scratch += [
            pltpu.SemaphoreType.DMA((2, 2)),
            pltpu.SemaphoreType.DMA((2, 2)),
            pltpu.SemaphoreType.REGULAR((2,)),
        ]
        if pair is None:
            out_shapes.append((rows, width))
            pair_scratch += [vmem((8, 128), x.dtype), vmem((8, 128), x.dtype)]
        else:
            outer = pair[1]
            inner = rows // (2 * outer)
            out_shapes.append((rows // 2, width))
            pair_scratch += [
                vmem((outer, 2, inner, width), x.dtype),
                vmem((outer, 1, inner, width), x.dtype),
            ]
        pair_scratch += [pltpu.SemaphoreType.DMA(()), pltpu.SemaphoreType.DMA(())]
    scratch += pair_scratch
    return pl.pallas_call(
        functools.partial(multi_ring_kernel, tuple(plan), tuple(pairs)),
        out_shape=[jax.ShapeDtypeStruct(shape, x.dtype) for shape, x in zip(out_shapes, inputs)],
        in_specs=[pl.BlockSpec(memory_space=vmem) for _ in inputs],
        out_specs=[pl.BlockSpec(memory_space=vmem) for _ in inputs],
        scratch_shapes=scratch,
        compiler_params=pltpu.CompilerParams(
            collective_id=collective_id, has_side_effects=True, vmem_limit_bytes=60 * 1024 * 1024
        ),
    )(*inputs)


def ring_sum(x, dim, axis, n):
    p = lax.axis_index(axis)
    partner = [(0, 1), (1, 0)]
    got = lax.ppermute(take_chunk(x, 1 - p, dim), axis, partner)
    return got + take_chunk(x, p, dim)


def applied_kernel(offsets_ref, mask_ref, ops_ref, ext_ref, out_ref):
    block = pl.program_id(1)
    slot_count, block_rows = ops_ref.shape[1], ops_ref.shape[2]
    order = [slot for _, slot in sorted(zip(STATIC_OFFSETS, WINDOW_SLOTS))]
    lhs = jnp.concatenate(
        [
            jnp.where(mask_ref[block * slot_count + slot] != 0, ops_ref[0, slot], 0)
            for slot in order
        ],
        axis=1,
    )
    first = pl.multiple_of(block * block_rows, block_rows)
    acc = jnp.dot(
        lhs, ext_ref[pl.ds(first, len(order) * block_rows), :], preferred_element_type=jnp.float32
    )
    for slot in range(len(WINDOW_SLOTS), slot_count):
        tile_index = offsets_ref[block * slot_count + slot]
        start = pl.multiple_of(tile_index * block_rows, block_rows)
        tile = ext_ref[pl.ds(start, block_rows), :]
        product = jnp.dot(ops_ref[0, slot], tile, preferred_element_type=jnp.float32)
        live = mask_ref[block * slot_count + slot] != 0
        acc = acc + jnp.where(live, product, 0.0)
    out_ref[...] = acc.astype(out_ref.dtype)


def apply_operator(offsets, mask, full_ops, extended, column_start, column_count):
    block_count, slot_count, block_rows, _ = full_ops.shape
    ext_rows = extended.shape[0]
    tile = min(TILE_COLUMNS, column_count)
    skip = column_start // tile
    grid_spec = pltpu.PrefetchScalarGridSpec(
        num_scalar_prefetch=2,
        grid=(column_count // tile, block_count),
        in_specs=[
            pl.BlockSpec((1, slot_count, block_rows, block_rows), lambda j, b, *_: (b, 0, 0, 0)),
            pl.BlockSpec((ext_rows, tile), lambda j, b, *_: (0, j + skip)),
        ],
        out_specs=pl.BlockSpec((block_rows, tile), lambda j, b, *_: (b, j)),
    )
    flops = 2 * block_count * slot_count * block_rows * block_rows * column_count
    return pl.pallas_call(
        applied_kernel,
        grid_spec=grid_spec,
        out_shape=jax.ShapeDtypeStruct((block_count * block_rows, column_count), jnp.bfloat16),
        compiler_params=pltpu.CompilerParams(dimension_semantics=("arbitrary", "arbitrary")),
        cost_estimate=pl.CostEstimate(
            flops=flops, bytes_accessed=3 * ext_rows * column_count * 2, transcendentals=0
        ),
    )(offsets, mask, full_ops, extended)


def per_device(basis_matrix, operator_blocks, neighbours, neighbour_mask):
    local_rows, column_count = basis_matrix.shape
    block_count, slot_count, half_rows, block_rows = operator_blocks.shape
    sec = lax.axis_index("sec")
    col = lax.axis_index("col")
    row = 0
    for name, size in ROW_PARTS:
        row = row * size + lax.axis_index(name)

    share = block_count // 2
    mine = lax.dynamic_slice_in_dim(operator_blocks, col * share, share, 0)
    from_sec = lax.ppermute(mine, "sec", [(0, 1), (1, 0)])
    from_col = lax.ppermute(from_sec, "col", [(0, 1), (1, 0)])
    other_half = jnp.where(
        col == 0,
        jnp.concatenate([from_sec, from_col], axis=0),
        jnp.concatenate([from_col, from_sec], axis=0),
    )
    first = jnp.where(sec == 0, operator_blocks, other_half)
    second = jnp.where(sec == 0, other_half, operator_blocks)
    full_ops = jnp.concatenate([first, second], axis=2)

    other_basis = lax.ppermute(basis_matrix, "col", [(0, 1), (1, 0)])
    left_projector = jnp.where(sec == col, basis_matrix, other_basis)

    extended = halo(basis_matrix, REACH * block_rows)
    offsets = jnp.clip(neighbours - row * block_count + REACH, 0, block_count + 2 * REACH - 1)
    row_count = 1
    for _, size in ROW_PARTS:
        row_count *= size
    scaling = 1.0 / math.sqrt(local_rows * row_count)
    chunk_rows = left_projector.shape[1] // row_count
    sizes = dict(ROW_PARTS)
    parts, names, start = [], [], 0
    for order, units in ORDERS:
        width = units * UNIT
        applied = apply_operator(
            offsets.reshape(-1), neighbour_mask.reshape(-1), full_ops, extended, start, width
        )
        start += width
        part = scaling * lax.dot_general(
            left_projector, applied, (((0,), (0,)), ((), ())), preferred_element_type=jnp.float32
        )
        parts.append(part.reshape(tuple(size for _, size in ROW_PARTS) + (chunk_rows, width)))
        names.append(list(ROW))
    (first_order, _), (second_order, _) = ORDERS
    assert first_order == ("z", "x", "y") and second_order == ("x", "z", "y")
    nz, nx, ny = sizes["z"], sizes["x"], sizes["y"]
    a, b = parts
    width_a, width_b = a.shape[-1], b.shape[-1]
    a, b = multi_ring_reduce(
        [a.reshape(nz, -1, width_a), b.reshape(nz, nx, -1, width_b)],
        [("z", nz), ("x", nx)],
        0,
        [None, ("y", nz)],
    )
    a, b = multi_ring_reduce(
        [a.reshape(nx, -1, width_a), b.reshape(nz, -1, width_b)],
        [("x", nx), ("z", nz)],
        1,
        [("y", 1), None],
    )
    parts = [a, b]
    pieces = parts
    return jnp.concatenate(pieces, axis=-1)


def solution(mesh):
    sizes = [mesh.shape["sec"]] + [size for _, size in ROW_PARTS] + [mesh.shape["col"]]
    fine = Mesh(np.asarray(mesh.devices).reshape(sizes), ("sec",) + ROW + ("col",))
    return jax.shard_map(
        per_device,
        mesh=fine,
        in_specs=(P(ROW, "col"), P(ROW, None, "sec", None), P(ROW, None), P(ROW, None)),
        out_specs=P(("sec",) + ROW, "col"),
        check_vma=False,
    )
```

```python
import functools
import math

import jax
import jax.numpy as jnp
import numpy as np
from jax import lax
from jax.experimental import pallas as pl
from jax.experimental.pallas import tpu as pltpu
from jax.sharding import Mesh
from jax.sharding import PartitionSpec as P

REACH = 2
ROW_PARTS = (("z", 8), ("x", 4), ("y", 2))
ROW = tuple(name for name, _ in ROW_PARTS)
UNIT = 256
ORDERS = ((("z", "x", "y"), 4), (("x", "z", "y"), 4))
TILE_COLUMNS = 1024
STATIC_OFFSETS = (0, -1, 1, -2, 2)
WINDOW_SLOTS = tuple(range(len(STATIC_OFFSETS)))


def halo(shard, width):
    count = 1
    for _, size in ROW_PARTS:
        count *= size
    length = shard.shape[0]
    axes = ("sec",) + ROW

    def index(sec, row):
        return sec * count + row

    after_pairs, before_pairs = [], []
    for sec in range(2):
        for row in range(count):
            other = sec if row % 2 == 0 else 1 - sec
            if row + 1 < count:
                after_pairs.append((index(other, row + 1), index(sec, row)))
            other = 1 - sec if row % 2 == 0 else sec
            if row >= 1:
                before_pairs.append((index(other, row - 1), index(sec, row)))
    before = lax.ppermute(shard[length - width :], axes, before_pairs)
    after = lax.ppermute(shard[:width], axes, after_pairs)
    return jnp.concatenate([before, shard, after], axis=0)


def take_chunk(x, index, dim):
    return lax.dynamic_index_in_dim(x, index, axis=dim, keepdims=False)


def read_chunk(x, index, columns):
    if len(x.shape) == 3:
        return x[index, :, columns]
    value = x[:, index, :, columns]
    return value.reshape(value.shape[0] * value.shape[1], value.shape[2])


def multi_ring_kernel(plan, pairs, *refs):
    count = len(plan)
    x_refs, o_refs = refs[:count], refs[count : 2 * count]
    scratch = refs[2 * count : 2 * count + 7 * count]
    pair_scratch = refs[2 * count + 7 * count :]
    mesh = pl.DeviceIdType.MESH
    rings = []
    for index, (axis, n) in enumerate(plan):
        out_f, in_f, out_b, in_b, send_sem, recv_sem, credit_sem = scratch[7 * index : 7 * index + 7]
        p = lax.axis_index(axis)
        rings.append(
            dict(
                axis=axis, n=n, p=p, x=x_refs[index], o=o_refs[index],
                right=lax.rem(p + 1, n), left=lax.rem(p + n - 1, n),
                out_f=out_f, in_f=in_f, out_b=out_b, in_b=in_b,
                send=send_sem, recv=recv_sem, credit=credit_sem, copies=None,
            )
        )

    barrier = pltpu.get_barrier_semaphore()
    for ring in rings:
        for neighbour in (ring["left"], ring["right"]):
            pl.semaphore_signal(barrier, 1, device_id={ring["axis"]: neighbour}, device_id_type=mesh)
    signals = 2 * count
    pair_axes = sorted({pair[0] for pair in pairs if pair is not None})
    for pair_axis in pair_axes:
        partner = 1 - lax.axis_index(pair_axis)
        pl.semaphore_signal(barrier, 1, device_id={pair_axis: partner}, device_id_type=mesh)
        signals += 1
    pl.semaphore_wait(barrier, signals)

    pending = []

    def finish(index):
        ring = rings[index]
        for copy in ring["copies"]:
            copy.wait()
        n, p, x = ring["n"], ring["p"], ring["x"]
        half = x.shape[-1] // 2
        last = (n - 2) % 2
        forward = ring["in_f"][last] + read_chunk(x, p, slice(None, half))
        backward = ring["in_b"][last] + read_chunk(x, p, slice(half, None))
        if pairs[index] is None:
            ring["o"][:, :half] = forward
            ring["o"][:, half:] = backward
            return
        pair_axis, _ = pairs[index]
        total, got, send_sem, recv_sem = pair_scratch[4 * index : 4 * index + 4]
        outer, _, rows, _ = total.shape
        total[:, :, :, :half] = forward.reshape(outer, 2, rows, half)
        total[:, :, :, half:] = backward.reshape(outer, 2, rows, half)
        mine = lax.axis_index(pair_axis)
        copy = pltpu.make_async_remote_copy(
            src_ref=total.at[:, pl.ds(1 - mine, 1)], dst_ref=got,
            send_sem=send_sem, recv_sem=recv_sem,
            device_id={pair_axis: 1 - mine}, device_id_type=mesh,
        )
        copy.start()
        pending.append((index, copy, mine))

    done = set()
    ticks = max(n - 1 for _, n in plan)

    def step_tick(index, step):
        n = rings[index]["n"]
        if pairs[index] is not None and 2 < n - 1 + 2 < ticks:
            return (step * (ticks - 4)) // (n - 2)
        return (step * ticks) // (n - 1)

    for tick in range(ticks):
        for ring_index, ring in enumerate(rings):
            n = ring["n"]
            due = [step for step in range(n - 1) if step_tick(ring_index, step) == tick]
            for step in due:
                if ring["copies"] is not None:
                    for copy in ring["copies"]:
                        copy.wait()
                    ring["copies"] = None
                slot = step % 2
                p, x, half = ring["p"], ring["x"], ring["x"].shape[-1] // 2
                chunk_f = lax.rem(p - step - 1 + 2 * n, n)
                chunk_b = lax.rem(p + step + 1, n)
                if step == 0:
                    ring["out_f"][slot] = read_chunk(x, chunk_f, slice(None, half))
                    ring["out_b"][slot] = read_chunk(x, chunk_b, slice(half, None))
                else:
                    ring["out_f"][slot] = ring["in_f"][1 - slot] + read_chunk(x, chunk_f, slice(None, half))
                    ring["out_b"][slot] = ring["in_b"][1 - slot] + read_chunk(x, chunk_b, slice(half, None))
                    if step <= n - 3:
                        pl.semaphore_signal(
                            ring["credit"].at[0], 1, device_id={ring["axis"]: ring["left"]}, device_id_type=mesh
                        )
                        pl.semaphore_signal(
                            ring["credit"].at[1], 1, device_id={ring["axis"]: ring["right"]}, device_id_type=mesh
                        )
                if step >= 2:
                    pl.semaphore_wait(ring["credit"].at[0], 1)
                    pl.semaphore_wait(ring["credit"].at[1], 1)
                copy_f = pltpu.make_async_remote_copy(
                    src_ref=ring["out_f"].at[slot], dst_ref=ring["in_f"].at[slot],
                    send_sem=ring["send"].at[0, slot], recv_sem=ring["recv"].at[0, slot],
                    device_id={ring["axis"]: ring["right"]}, device_id_type=mesh,
                )
                copy_b = pltpu.make_async_remote_copy(
                    src_ref=ring["out_b"].at[slot], dst_ref=ring["in_b"].at[slot],
                    send_sem=ring["send"].at[1, slot], recv_sem=ring["recv"].at[1, slot],
                    device_id={ring["axis"]: ring["left"]}, device_id_type=mesh,
                )
                copy_f.start()
                copy_b.start()
                ring["copies"] = (copy_f, copy_b)
        for index, ring in enumerate(rings):
            last_tick = step_tick(index, ring["n"] - 2)
            if pairs[index] is not None and last_tick + 1 == tick:
                finish(index)
                done.add(index)
    for index in sorted(range(count), key=lambda i: rings[i]["n"]):
        if index not in done:
            finish(index)
    for index, copy, mine in pending:
        total, got = pair_scratch[4 * index : 4 * index + 2]
        outer, _, rows, width = total.shape
        copy.wait()
        summed = got[...] + total[:, pl.ds(mine, 1)]
        rings[index]["o"][...] = summed.reshape(outer * rows, width)


def multi_ring_reduce(inputs, plan, collective_id, pairs):
    vmem = pltpu.VMEM
    scratch, pair_scratch, out_shapes = [], [], []
    for x, pair in zip(inputs, pairs):
        rows, width = x.shape[-2], x.shape[-1]
        if len(x.shape) == 4:
            rows *= x.shape[0]
        half = width // 2
        scratch += [vmem((2, rows, half), x.dtype) for _ in range(4)]
        scratch += [
            pltpu.SemaphoreType.DMA((2, 2)),
            pltpu.SemaphoreType.DMA((2, 2)),
            pltpu.SemaphoreType.REGULAR((2,)),
        ]
        if pair is None:
            out_shapes.append((rows, width))
            pair_scratch += [vmem((8, 128), x.dtype), vmem((8, 128), x.dtype)]
        else:
            outer = pair[1]
            inner = rows // (2 * outer)
            out_shapes.append((rows // 2, width))
            pair_scratch += [
                vmem((outer, 2, inner, width), x.dtype),
                vmem((outer, 1, inner, width), x.dtype),
            ]
        pair_scratch += [pltpu.SemaphoreType.DMA(()), pltpu.SemaphoreType.DMA(())]
    scratch += pair_scratch
    return pl.pallas_call(
        functools.partial(multi_ring_kernel, tuple(plan), tuple(pairs)),
        out_shape=[jax.ShapeDtypeStruct(shape, x.dtype) for shape, x in zip(out_shapes, inputs)],
        in_specs=[pl.BlockSpec(memory_space=vmem) for _ in inputs],
        out_specs=[pl.BlockSpec(memory_space=vmem) for _ in inputs],
        scratch_shapes=scratch,
        compiler_params=pltpu.CompilerParams(
            collective_id=collective_id, has_side_effects=True, vmem_limit_bytes=60 * 1024 * 1024
        ),
    )(*inputs)


def ring_sum(x, dim, axis, n):
    p = lax.axis_index(axis)
    partner = [(0, 1), (1, 0)]
    got = lax.ppermute(take_chunk(x, 1 - p, dim), axis, partner)
    return got + take_chunk(x, p, dim)


def applied_kernel(offsets_ref, mask_ref, ops_ref, ext_ref, out_ref):
    block = pl.program_id(1)
    slot_count, block_rows = ops_ref.shape[1], ops_ref.shape[2]
    order = [slot for _, slot in sorted(zip(STATIC_OFFSETS, WINDOW_SLOTS))]
    lhs = jnp.concatenate(
        [
            jnp.where(mask_ref[block * slot_count + slot] != 0, ops_ref[0, slot], 0)
            for slot in order
        ],
        axis=1,
    )
    first = pl.multiple_of(block * block_rows, block_rows)
    acc = jnp.dot(
        lhs, ext_ref[pl.ds(first, len(order) * block_rows), :], preferred_element_type=jnp.float32
    )
    for slot in range(len(WINDOW_SLOTS), slot_count):
        tile_index = offsets_ref[block * slot_count + slot]
        start = pl.multiple_of(tile_index * block_rows, block_rows)
        tile = ext_ref[pl.ds(start, block_rows), :]
        product = jnp.dot(ops_ref[0, slot], tile, preferred_element_type=jnp.float32)
        live = mask_ref[block * slot_count + slot] != 0
        acc = acc + jnp.where(live, product, 0.0)
    out_ref[...] = acc.astype(out_ref.dtype)


def apply_operator(offsets, mask, full_ops, extended, column_start, column_count):
    block_count, slot_count, block_rows, _ = full_ops.shape
    ext_rows = extended.shape[0]
    tile = min(TILE_COLUMNS, column_count)
    skip = column_start // tile
    grid_spec = pltpu.PrefetchScalarGridSpec(
        num_scalar_prefetch=2,
        grid=(column_count // tile, block_count),
        in_specs=[
            pl.BlockSpec((1, slot_count, block_rows, block_rows), lambda j, b, *_: (b, 0, 0, 0)),
            pl.BlockSpec((ext_rows, tile), lambda j, b, *_: (0, j + skip)),
        ],
        out_specs=pl.BlockSpec((block_rows, tile), lambda j, b, *_: (b, j)),
    )
    flops = 2 * block_count * slot_count * block_rows * block_rows * column_count
    return pl.pallas_call(
        applied_kernel,
        grid_spec=grid_spec,
        out_shape=jax.ShapeDtypeStruct((block_count * block_rows, column_count), jnp.bfloat16),
        compiler_params=pltpu.CompilerParams(dimension_semantics=("arbitrary", "arbitrary")),
        cost_estimate=pl.CostEstimate(
            flops=flops, bytes_accessed=3 * ext_rows * column_count * 2, transcendentals=0
        ),
    )(offsets, mask, full_ops, extended)


def per_device(basis_matrix, operator_blocks, neighbours, neighbour_mask):
    local_rows, column_count = basis_matrix.shape
    block_count, slot_count, half_rows, block_rows = operator_blocks.shape
    sec = lax.axis_index("sec")
    col = lax.axis_index("col")
    row = 0
    for name, size in ROW_PARTS:
        row = row * size + lax.axis_index(name)

    share = block_count // 2
    mine = lax.dynamic_slice_in_dim(operator_blocks, col * share, share, 0)
    from_sec = lax.ppermute(mine, "sec", [(0, 1), (1, 0)])
    from_col = lax.ppermute(from_sec, "col", [(0, 1), (1, 0)])
    other_half = jnp.where(
        col == 0,
        jnp.concatenate([from_sec, from_col], axis=0),
        jnp.concatenate([from_col, from_sec], axis=0),
    )
    first = jnp.where(sec == 0, operator_blocks, other_half)
    second = jnp.where(sec == 0, other_half, operator_blocks)
    full_ops = jnp.concatenate([first, second], axis=2)

    other_basis = lax.ppermute(basis_matrix, "col", [(0, 1), (1, 0)])
    left_projector = jnp.where(sec == col, basis_matrix, other_basis)

    extended = halo(basis_matrix, REACH * block_rows)
    offsets = jnp.clip(neighbours - row * block_count + REACH, 0, block_count + 2 * REACH - 1)
    row_count = 1
    for _, size in ROW_PARTS:
        row_count *= size
    scaling = 1.0 / math.sqrt(local_rows * row_count)
    chunk_rows = left_projector.shape[1] // row_count
    sizes = dict(ROW_PARTS)
    parts, names, start = [], [], 0
    for order, units in ORDERS:
        width = units * UNIT
        applied = apply_operator(
            offsets.reshape(-1), neighbour_mask.reshape(-1), full_ops, extended, start, width
        )
        start += width
        part = scaling * lax.dot_general(
            left_projector, applied, (((0,), (0,)), ((), ())), preferred_element_type=jnp.float32
        )
        parts.append(part.reshape(tuple(size for _, size in ROW_PARTS) + (chunk_rows, width)))
        names.append(list(ROW))
    (first_order, _), (second_order, _) = ORDERS
    assert first_order == ("z", "x", "y") and second_order == ("x", "z", "y")
    nz, nx, ny = sizes["z"], sizes["x"], sizes["y"]
    a, b = parts
    width_a, width_b = a.shape[-1], b.shape[-1]
    a, b = multi_ring_reduce(
        [a.reshape(nz, -1, width_a), b.reshape(nz, nx, -1, width_b)],
        [("z", nz), ("x", nx)],
        0,
        [None, ("y", nz)],
    )
    a, b = multi_ring_reduce(
        [a.reshape(nx, -1, width_a), b.reshape(nz, -1, width_b)],
        [("x", nx), ("z", nz)],
        1,
        [("y", 1), None],
    )
    parts = [a, b]
    pieces = parts
    return jnp.concatenate(pieces, axis=-1)


def solution(mesh):
    sizes = [mesh.shape["sec"]] + [size for _, size in ROW_PARTS] + [mesh.shape["col"]]
    fine = Mesh(np.asarray(mesh.devices).reshape(sizes), ("sec",) + ROW + ("col",))
    return jax.shard_map(
        per_device,
        mesh=fine,
        in_specs=(P(ROW, "col"), P(ROW, None, "sec", None), P(ROW, None), P(ROW, None)),
        out_specs=P(("sec",) + ROW, "col"),
        check_vma=False,
    )
```

```python
import functools
import math

import jax
import jax.numpy as jnp
import numpy as np
from jax import lax
from jax.experimental import pallas as pl
from jax.experimental.pallas import tpu as pltpu
from jax.sharding import Mesh
from jax.sharding import PartitionSpec as P

REACH = 2
ROW_PARTS = (("z", 8), ("x", 4), ("y", 2))
ROW = tuple(name for name, _ in ROW_PARTS)
UNIT = 256
ORDERS = ((("z", "x", "y"), 4), (("x", "z", "y"), 4))
TILE_COLUMNS = 1024
STATIC_OFFSETS = (0, -1, 1, -2, 2)
WINDOW_SLOTS = tuple(range(len(STATIC_OFFSETS)))


def halo(shard, width):
    count = 1
    for _, size in ROW_PARTS:
        count *= size
    length = shard.shape[0]
    axes = ("sec",) + ROW

    def index(sec, row):
        return sec * count + row

    after_pairs, before_pairs = [], []
    for sec in range(2):
        for row in range(count):
            other = sec if row % 2 == 0 else 1 - sec
            if row + 1 < count:
                after_pairs.append((index(other, row + 1), index(sec, row)))
            other = 1 - sec if row % 2 == 0 else sec
            if row >= 1:
                before_pairs.append((index(other, row - 1), index(sec, row)))
    before = lax.ppermute(shard[length - width :], axes, before_pairs)
    after = lax.ppermute(shard[:width], axes, after_pairs)
    return before, shard, after


def take_chunk(x, index, dim):
    return lax.dynamic_index_in_dim(x, index, axis=dim, keepdims=False)


def read_chunk(x, index, columns):
    if len(x.shape) == 3:
        return x[index, :, columns]
    value = x[:, index, :, columns]
    return value.reshape(value.shape[0] * value.shape[1], value.shape[2])


def multi_ring_kernel(plan, pairs, *refs):
    count = len(plan)
    x_refs, o_refs = refs[:count], refs[count : 2 * count]
    scratch = refs[2 * count : 2 * count + 7 * count]
    pair_scratch = refs[2 * count + 7 * count :]
    mesh = pl.DeviceIdType.MESH
    rings = []
    for index, (axis, n) in enumerate(plan):
        out_f, in_f, out_b, in_b, send_sem, recv_sem, credit_sem = scratch[7 * index : 7 * index + 7]
        p = lax.axis_index(axis)
        rings.append(
            dict(
                axis=axis, n=n, p=p, x=x_refs[index], o=o_refs[index],
                right=lax.rem(p + 1, n), left=lax.rem(p + n - 1, n),
                out_f=out_f, in_f=in_f, out_b=out_b, in_b=in_b,
                send=send_sem, recv=recv_sem, credit=credit_sem, copies=None,
            )
        )

    barrier = pltpu.get_barrier_semaphore()
    for ring in rings:
        for neighbour in (ring["left"], ring["right"]):
            pl.semaphore_signal(barrier, 1, device_id={ring["axis"]: neighbour}, device_id_type=mesh)
    signals = 2 * count
    pair_axes = sorted({pair[0] for pair in pairs if pair is not None})
    for pair_axis in pair_axes:
        partner = 1 - lax.axis_index(pair_axis)
        pl.semaphore_signal(barrier, 1, device_id={pair_axis: partner}, device_id_type=mesh)
        signals += 1
    pl.semaphore_wait(barrier, signals)

    pending = []

    def finish(index):
        ring = rings[index]
        for copy in ring["copies"]:
            copy.wait()
        n, p, x = ring["n"], ring["p"], ring["x"]
        half = x.shape[-1] // 2
        last = (n - 2) % 2
        forward = ring["in_f"][last] + read_chunk(x, p, slice(None, half))
        backward = ring["in_b"][last] + read_chunk(x, p, slice(half, None))
        if pairs[index] is None:
            ring["o"][:, :half] = forward
            ring["o"][:, half:] = backward
            return
        pair_axis, _ = pairs[index]
        total, got, send_sem, recv_sem = pair_scratch[4 * index : 4 * index + 4]
        outer, _, rows, _ = total.shape
        total[:, :, :, :half] = forward.reshape(outer, 2, rows, half)
        total[:, :, :, half:] = backward.reshape(outer, 2, rows, half)
        mine = lax.axis_index(pair_axis)
        copy = pltpu.make_async_remote_copy(
            src_ref=total.at[:, pl.ds(1 - mine, 1)], dst_ref=got,
            send_sem=send_sem, recv_sem=recv_sem,
            device_id={pair_axis: 1 - mine}, device_id_type=mesh,
        )
        copy.start()
        pending.append((index, copy, mine))

    done = set()
    ticks = max(n - 1 for _, n in plan)
    for tick in range(ticks):
        for ring in rings:
            n = ring["n"]
            due = [step for step in range(n - 1) if (step * ticks) // (n - 1) == tick]
            for step in due:
                if ring["copies"] is not None:
                    for copy in ring["copies"]:
                        copy.wait()
                    ring["copies"] = None
                slot = step % 2
                p, x, half = ring["p"], ring["x"], ring["x"].shape[-1] // 2
                chunk_f = lax.rem(p - step - 1 + 2 * n, n)
                chunk_b = lax.rem(p + step + 1, n)
                if step == 0:
                    ring["out_f"][slot] = read_chunk(x, chunk_f, slice(None, half))
                    ring["out_b"][slot] = read_chunk(x, chunk_b, slice(half, None))
                else:
                    ring["out_f"][slot] = ring["in_f"][1 - slot] + read_chunk(x, chunk_f, slice(None, half))
                    ring["out_b"][slot] = ring["in_b"][1 - slot] + read_chunk(x, chunk_b, slice(half, None))
                    if step <= n - 3:
                        pl.semaphore_signal(
                            ring["credit"].at[0], 1, device_id={ring["axis"]: ring["left"]}, device_id_type=mesh
                        )
                        pl.semaphore_signal(
                            ring["credit"].at[1], 1, device_id={ring["axis"]: ring["right"]}, device_id_type=mesh
                        )
                if step >= 2:
                    pl.semaphore_wait(ring["credit"].at[0], 1)
                    pl.semaphore_wait(ring["credit"].at[1], 1)
                copy_f = pltpu.make_async_remote_copy(
                    src_ref=ring["out_f"].at[slot], dst_ref=ring["in_f"].at[slot],
                    send_sem=ring["send"].at[0, slot], recv_sem=ring["recv"].at[0, slot],
                    device_id={ring["axis"]: ring["right"]}, device_id_type=mesh,
                )
                copy_b = pltpu.make_async_remote_copy(
                    src_ref=ring["out_b"].at[slot], dst_ref=ring["in_b"].at[slot],
                    send_sem=ring["send"].at[1, slot], recv_sem=ring["recv"].at[1, slot],
                    device_id={ring["axis"]: ring["left"]}, device_id_type=mesh,
                )
                copy_f.start()
                copy_b.start()
                ring["copies"] = (copy_f, copy_b)
        for index, ring in enumerate(rings):
            last_tick = ((ring["n"] - 2) * ticks) // (ring["n"] - 1)
            if pairs[index] is not None and last_tick + 1 == tick:
                finish(index)
                done.add(index)
    for index in sorted(range(count), key=lambda i: rings[i]["n"]):
        if index not in done:
            finish(index)
    for index, copy, mine in pending:
        total, got = pair_scratch[4 * index : 4 * index + 2]
        outer, _, rows, width = total.shape
        copy.wait()
        summed = got[...] + total[:, pl.ds(mine, 1)]
        rings[index]["o"][...] = summed.reshape(outer * rows, width)


def multi_ring_reduce(inputs, plan, collective_id, pairs):
    vmem = pltpu.VMEM
    scratch, pair_scratch, out_shapes = [], [], []
    for x, pair in zip(inputs, pairs):
        rows, width = x.shape[-2], x.shape[-1]
        if len(x.shape) == 4:
            rows *= x.shape[0]
        half = width // 2
        scratch += [vmem((2, rows, half), x.dtype) for _ in range(4)]
        scratch += [
            pltpu.SemaphoreType.DMA((2, 2)),
            pltpu.SemaphoreType.DMA((2, 2)),
            pltpu.SemaphoreType.REGULAR((2,)),
        ]
        if pair is None:
            out_shapes.append((rows, width))
            pair_scratch += [vmem((8, 128), x.dtype), vmem((8, 128), x.dtype)]
        else:
            outer = pair[1]
            inner = rows // (2 * outer)
            out_shapes.append((rows // 2, width))
            pair_scratch += [
                vmem((outer, 2, inner, width), x.dtype),
                vmem((outer, 1, inner, width), x.dtype),
            ]
        pair_scratch += [pltpu.SemaphoreType.DMA(()), pltpu.SemaphoreType.DMA(())]
    scratch += pair_scratch
    return pl.pallas_call(
        functools.partial(multi_ring_kernel, tuple(plan), tuple(pairs)),
        out_shape=[jax.ShapeDtypeStruct(shape, x.dtype) for shape, x in zip(out_shapes, inputs)],
        in_specs=[pl.BlockSpec(memory_space=vmem) for _ in inputs],
        out_specs=[pl.BlockSpec(memory_space=vmem) for _ in inputs],
        scratch_shapes=scratch,
        compiler_params=pltpu.CompilerParams(
            collective_id=collective_id, has_side_effects=True, vmem_limit_bytes=60 * 1024 * 1024
        ),
    )(*inputs)


def ring_sum(x, dim, axis, n):
    p = lax.axis_index(axis)
    partner = [(0, 1), (1, 0)]
    got = lax.ppermute(take_chunk(x, 1 - p, dim), axis, partner)
    return got + take_chunk(x, p, dim)


def applied_kernel(offsets_ref, mask_ref, ops_ref, before_ref, basis_ref, after_ref, out_ref, ext_ref):
    block = pl.program_id(1)
    slot_count, block_rows = ops_ref.shape[1], ops_ref.shape[2]

    @pl.when(block == 0)
    def _():
        width, local = before_ref.shape[0], basis_ref.shape[0]
        ext_ref[pl.ds(0, width), :] = before_ref[...]
        ext_ref[pl.ds(width, local), :] = basis_ref[...]
        ext_ref[pl.ds(width + local, width), :] = after_ref[...]

    order = [slot for _, slot in sorted(zip(STATIC_OFFSETS, WINDOW_SLOTS))]
    lhs = jnp.concatenate(
        [
            jnp.where(mask_ref[block * slot_count + slot] != 0, ops_ref[0, slot], 0)
            for slot in order
        ],
        axis=1,
    )
    first = pl.multiple_of(block * block_rows, block_rows)
    acc = jnp.dot(
        lhs, ext_ref[pl.ds(first, len(order) * block_rows), :], preferred_element_type=jnp.float32
    )
    for slot in range(len(WINDOW_SLOTS), slot_count):
        tile_index = offsets_ref[block * slot_count + slot]
        start = pl.multiple_of(tile_index * block_rows, block_rows)
        tile = ext_ref[pl.ds(start, block_rows), :]
        product = jnp.dot(ops_ref[0, slot], tile, preferred_element_type=jnp.float32)
        live = mask_ref[block * slot_count + slot] != 0
        acc = acc + jnp.where(live, product, 0.0)
    out_ref[...] = acc.astype(out_ref.dtype)


def apply_operator(offsets, mask, full_ops, sides, column_start, column_count):
    before, basis, after = sides
    block_count, slot_count, block_rows, _ = full_ops.shape
    ext_rows = before.shape[0] + basis.shape[0] + after.shape[0]
    tile = min(TILE_COLUMNS, column_count)
    skip = column_start // tile
    grid_spec = pltpu.PrefetchScalarGridSpec(
        num_scalar_prefetch=2,
        grid=(column_count // tile, block_count),
        in_specs=[
            pl.BlockSpec((1, slot_count, block_rows, block_rows), lambda j, b, *_: (b, 0, 0, 0)),
            pl.BlockSpec((before.shape[0], tile), lambda j, b, *_: (0, j + skip)),
            pl.BlockSpec((basis.shape[0], tile), lambda j, b, *_: (0, j + skip)),
            pl.BlockSpec((after.shape[0], tile), lambda j, b, *_: (0, j + skip)),
        ],
        out_specs=pl.BlockSpec((block_rows, tile), lambda j, b, *_: (b, j)),
        scratch_shapes=[pltpu.VMEM((ext_rows, tile), basis.dtype)],
    )
    flops = 2 * block_count * slot_count * block_rows * block_rows * column_count
    return pl.pallas_call(
        applied_kernel,
        grid_spec=grid_spec,
        out_shape=jax.ShapeDtypeStruct((block_count * block_rows, column_count), jnp.bfloat16),
        compiler_params=pltpu.CompilerParams(dimension_semantics=("arbitrary", "arbitrary")),
        cost_estimate=pl.CostEstimate(
            flops=flops, bytes_accessed=3 * ext_rows * column_count * 2, transcendentals=0
        ),
    )(offsets, mask, full_ops, before, basis, after)


def per_device(basis_matrix, operator_blocks, neighbours, neighbour_mask):
    local_rows, column_count = basis_matrix.shape
    block_count, slot_count, half_rows, block_rows = operator_blocks.shape
    sec = lax.axis_index("sec")
    col = lax.axis_index("col")
    row = 0
    for name, size in ROW_PARTS:
        row = row * size + lax.axis_index(name)

    share = block_count // 2
    mine = lax.dynamic_slice_in_dim(operator_blocks, col * share, share, 0)
    from_sec = lax.ppermute(mine, "sec", [(0, 1), (1, 0)])
    from_col = lax.ppermute(from_sec, "col", [(0, 1), (1, 0)])
    other_half = jnp.where(
        col == 0,
        jnp.concatenate([from_sec, from_col], axis=0),
        jnp.concatenate([from_col, from_sec], axis=0),
    )
    first = jnp.where(sec == 0, operator_blocks, other_half)
    second = jnp.where(sec == 0, other_half, operator_blocks)
    full_ops = jnp.concatenate([first, second], axis=2)

    other_basis = lax.ppermute(basis_matrix, "col", [(0, 1), (1, 0)])
    left_projector = jnp.where(sec == col, basis_matrix, other_basis)

    sides = halo(basis_matrix, REACH * block_rows)
    offsets = jnp.clip(neighbours - row * block_count + REACH, 0, block_count + 2 * REACH - 1)
    row_count = 1
    for _, size in ROW_PARTS:
        row_count *= size
    scaling = 1.0 / math.sqrt(local_rows * row_count)
    chunk_rows = left_projector.shape[1] // row_count
    sizes = dict(ROW_PARTS)
    parts, names, start = [], [], 0
    for order, units in ORDERS:
        width = units * UNIT
        applied = apply_operator(
            offsets.reshape(-1), neighbour_mask.reshape(-1), full_ops, sides, start, width
        )
        start += width
        part = scaling * lax.dot_general(
            left_projector, applied, (((0,), (0,)), ((), ())), preferred_element_type=jnp.float32
        )
        parts.append(part.reshape(tuple(size for _, size in ROW_PARTS) + (chunk_rows, width)))
        names.append(list(ROW))
    (first_order, _), (second_order, _) = ORDERS
    assert first_order == ("z", "x", "y") and second_order == ("x", "z", "y")
    nz, nx, ny = sizes["z"], sizes["x"], sizes["y"]
    a, b = parts
    width_a, width_b = a.shape[-1], b.shape[-1]
    a, b = multi_ring_reduce(
        [a.reshape(nz, -1, width_a), b.reshape(nz, nx, -1, width_b)],
        [("z", nz), ("x", nx)],
        0,
        [None, ("y", nz)],
    )
    a, b = multi_ring_reduce(
        [a.reshape(nx, -1, width_a), b.reshape(nz, -1, width_b)],
        [("x", nx), ("z", nz)],
        1,
        [("y", 1), None],
    )
    parts = [a, b]
    pieces = parts
    return jnp.concatenate(pieces, axis=-1)


def solution(mesh):
    sizes = [mesh.shape["sec"]] + [size for _, size in ROW_PARTS] + [mesh.shape["col"]]
    fine = Mesh(np.asarray(mesh.devices).reshape(sizes), ("sec",) + ROW + ("col",))
    return jax.shard_map(
        per_device,
        mesh=fine,
        in_specs=(P(ROW, "col"), P(ROW, None, "sec", None), P(ROW, None), P(ROW, None)),
        out_specs=P(("sec",) + ROW, "col"),
        check_vma=False,
    )
```

```python
import functools
import math

import jax
import jax.numpy as jnp
import numpy as np
from jax import lax
from jax.experimental import pallas as pl
from jax.experimental.pallas import tpu as pltpu
from jax.sharding import Mesh
from jax.sharding import PartitionSpec as P

REACH = 2
ROW_PARTS = (("z", 8), ("x", 4), ("y", 2))
ROW = tuple(name for name, _ in ROW_PARTS)
UNIT = 256
ORDERS = ((("z", "x", "y"), 4), (("x", "z", "y"), 4))
TILE_COLUMNS = 1024
STATIC_OFFSETS = (0, -1, 1, -2, 2)
WINDOW_SLOTS = tuple(range(len(STATIC_OFFSETS)))


def halo(shard, width):
    count = 1
    for _, size in ROW_PARTS:
        count *= size
    length = shard.shape[0]
    axes = ("sec",) + ROW

    def index(sec, row):
        return sec * count + row

    after_pairs, before_pairs = [], []
    for sec in range(2):
        for row in range(count):
            other = sec if row % 2 == 0 else 1 - sec
            if row + 1 < count:
                after_pairs.append((index(other, row + 1), index(sec, row)))
            other = 1 - sec if row % 2 == 0 else sec
            if row >= 1:
                before_pairs.append((index(other, row - 1), index(sec, row)))
    before = lax.ppermute(shard[length - width :], axes, before_pairs)
    after = lax.ppermute(shard[:width], axes, after_pairs)
    return jnp.concatenate([before, shard, after], axis=0)


def take_chunk(x, index, dim):
    return lax.dynamic_index_in_dim(x, index, axis=dim, keepdims=False)


def read_chunk(x, index, columns):
    if len(x.shape) == 3:
        return x[index, :, columns]
    value = x[:, index, :, columns]
    return value.reshape(value.shape[0] * value.shape[1], value.shape[2])


def multi_ring_kernel(plan, pairs, *refs):
    count = len(plan)
    x_refs, o_refs = refs[:count], refs[count : 2 * count]
    scratch = refs[2 * count : 2 * count + 7 * count]
    pair_scratch = refs[2 * count + 7 * count :]
    mesh = pl.DeviceIdType.MESH
    rings = []
    for index, (axis, n) in enumerate(plan):
        out_f, in_f, out_b, in_b, send_sem, recv_sem, credit_sem = scratch[7 * index : 7 * index + 7]
        p = lax.axis_index(axis)
        rings.append(
            dict(
                axis=axis, n=n, p=p, x=x_refs[index], o=o_refs[index],
                right=lax.rem(p + 1, n), left=lax.rem(p + n - 1, n),
                out_f=out_f, in_f=in_f, out_b=out_b, in_b=in_b,
                send=send_sem, recv=recv_sem, credit=credit_sem, copies=None,
            )
        )

    barrier = pltpu.get_barrier_semaphore()
    for ring in rings:
        for neighbour in (ring["left"], ring["right"]):
            pl.semaphore_signal(barrier, 1, device_id={ring["axis"]: neighbour}, device_id_type=mesh)
    signals = 2 * count
    pair_axes = sorted({pair[0] for pair in pairs if pair is not None})
    for pair_axis in pair_axes:
        partner = 1 - lax.axis_index(pair_axis)
        pl.semaphore_signal(barrier, 1, device_id={pair_axis: partner}, device_id_type=mesh)
        signals += 1
    pl.semaphore_wait(barrier, signals)

    pending = []

    def finish(index):
        ring = rings[index]
        for copy in ring["copies"]:
            copy.wait()
        n, p, x = ring["n"], ring["p"], ring["x"]
        half = x.shape[-1] // 2
        last = (n - 2) % 2
        forward = ring["in_f"][last] + read_chunk(x, p, slice(None, half))
        backward = ring["in_b"][last] + read_chunk(x, p, slice(half, None))
        if pairs[index] is None:
            ring["o"][:, :half] = forward
            ring["o"][:, half:] = backward
            return
        pair_axis, _ = pairs[index]
        total, got, send_sem, recv_sem = pair_scratch[4 * index : 4 * index + 4]
        outer, _, rows, _ = total.shape
        total[:, :, :, :half] = forward.reshape(outer, 2, rows, half)
        total[:, :, :, half:] = backward.reshape(outer, 2, rows, half)
        mine = lax.axis_index(pair_axis)
        copy = pltpu.make_async_remote_copy(
            src_ref=total.at[:, pl.ds(1 - mine, 1)], dst_ref=got,
            send_sem=send_sem, recv_sem=recv_sem,
            device_id={pair_axis: 1 - mine}, device_id_type=mesh,
        )
        copy.start()
        pending.append((index, copy, mine))

    done = set()
    ticks = max(n - 1 for _, n in plan)
    for tick in range(ticks):
        for ring in rings:
            n = ring["n"]
            due = [step for step in range(n - 1) if (step * ticks) // (n - 1) == tick]
            for step in due:
                if ring["copies"] is not None:
                    for copy in ring["copies"]:
                        copy.wait()
                    ring["copies"] = None
                slot = step % 2
                p, x, half = ring["p"], ring["x"], ring["x"].shape[-1] // 2
                chunk_f = lax.rem(p - step - 1 + 2 * n, n)
                chunk_b = lax.rem(p + step + 1, n)
                if step == 0:
                    ring["out_f"][slot] = read_chunk(x, chunk_f, slice(None, half))
                    ring["out_b"][slot] = read_chunk(x, chunk_b, slice(half, None))
                else:
                    ring["out_f"][slot] = ring["in_f"][1 - slot] + read_chunk(x, chunk_f, slice(None, half))
                    ring["out_b"][slot] = ring["in_b"][1 - slot] + read_chunk(x, chunk_b, slice(half, None))
                    if step <= n - 3:
                        pl.semaphore_signal(
                            ring["credit"].at[0], 1, device_id={ring["axis"]: ring["left"]}, device_id_type=mesh
                        )
                        pl.semaphore_signal(
                            ring["credit"].at[1], 1, device_id={ring["axis"]: ring["right"]}, device_id_type=mesh
                        )
                if step >= 2:
                    pl.semaphore_wait(ring["credit"].at[0], 1)
                    pl.semaphore_wait(ring["credit"].at[1], 1)
                copy_f = pltpu.make_async_remote_copy(
                    src_ref=ring["out_f"].at[slot], dst_ref=ring["in_f"].at[slot],
                    send_sem=ring["send"].at[0, slot], recv_sem=ring["recv"].at[0, slot],
                    device_id={ring["axis"]: ring["right"]}, device_id_type=mesh,
                )
                copy_b = pltpu.make_async_remote_copy(
                    src_ref=ring["out_b"].at[slot], dst_ref=ring["in_b"].at[slot],
                    send_sem=ring["send"].at[1, slot], recv_sem=ring["recv"].at[1, slot],
                    device_id={ring["axis"]: ring["left"]}, device_id_type=mesh,
                )
                copy_f.start()
                copy_b.start()
                ring["copies"] = (copy_f, copy_b)
        for index, ring in enumerate(rings):
            last_tick = ((ring["n"] - 2) * ticks) // (ring["n"] - 1)
            if pairs[index] is not None and last_tick + 1 == tick:
                finish(index)
                done.add(index)
    for index in sorted(range(count), key=lambda i: rings[i]["n"]):
        if index not in done:
            finish(index)
    for index, copy, mine in pending:
        total, got = pair_scratch[4 * index : 4 * index + 2]
        outer, _, rows, width = total.shape
        copy.wait()
        summed = got[...] + total[:, pl.ds(mine, 1)]
        rings[index]["o"][...] = summed.reshape(outer * rows, width)


def multi_ring_reduce(inputs, plan, collective_id, pairs):
    vmem = pltpu.VMEM
    scratch, pair_scratch, out_shapes = [], [], []
    for x, pair in zip(inputs, pairs):
        rows, width = x.shape[-2], x.shape[-1]
        if len(x.shape) == 4:
            rows *= x.shape[0]
        half = width // 2
        scratch += [vmem((2, rows, half), x.dtype) for _ in range(4)]
        scratch += [
            pltpu.SemaphoreType.DMA((2, 2)),
            pltpu.SemaphoreType.DMA((2, 2)),
            pltpu.SemaphoreType.REGULAR((2,)),
        ]
        if pair is None:
            out_shapes.append((rows, width))
            pair_scratch += [vmem((8, 128), x.dtype), vmem((8, 128), x.dtype)]
        else:
            outer = pair[1]
            inner = rows // (2 * outer)
            out_shapes.append((rows // 2, width))
            pair_scratch += [
                vmem((outer, 2, inner, width), x.dtype),
                vmem((outer, 1, inner, width), x.dtype),
            ]
        pair_scratch += [pltpu.SemaphoreType.DMA(()), pltpu.SemaphoreType.DMA(())]
    scratch += pair_scratch
    return pl.pallas_call(
        functools.partial(multi_ring_kernel, tuple(plan), tuple(pairs)),
        out_shape=[jax.ShapeDtypeStruct(shape, x.dtype) for shape, x in zip(out_shapes, inputs)],
        in_specs=[pl.BlockSpec(memory_space=vmem) for _ in inputs],
        out_specs=[pl.BlockSpec(memory_space=vmem) for _ in inputs],
        scratch_shapes=scratch,
        compiler_params=pltpu.CompilerParams(
            collective_id=collective_id, has_side_effects=True, vmem_limit_bytes=60 * 1024 * 1024
        ),
    )(*inputs)


def ring_sum(x, dim, axis, n):
    p = lax.axis_index(axis)
    partner = [(0, 1), (1, 0)]
    got = lax.ppermute(take_chunk(x, 1 - p, dim), axis, partner)
    return got + take_chunk(x, p, dim)


def applied_kernel(offsets_ref, mask_ref, ops_ref, ext_ref, out_ref):
    block_count, slot_count, block_rows = ops_ref.shape[0], ops_ref.shape[1], ops_ref.shape[2]
    order = [slot for _, slot in sorted(zip(STATIC_OFFSETS, WINDOW_SLOTS))]

    def one_block(block, carry):
        lhs = jnp.concatenate(
            [
                jnp.where(mask_ref[block * slot_count + slot] != 0, ops_ref[block, slot], 0)
                for slot in order
            ],
            axis=1,
        )
        first = pl.multiple_of(block * block_rows, block_rows)
        acc = jnp.dot(
            lhs, ext_ref[pl.ds(first, len(order) * block_rows), :], preferred_element_type=jnp.float32
        )
        for slot in range(len(WINDOW_SLOTS), slot_count):
            tile_index = offsets_ref[block * slot_count + slot]
            start = pl.multiple_of(tile_index * block_rows, block_rows)
            tile = ext_ref[pl.ds(start, block_rows), :]
            product = jnp.dot(ops_ref[block, slot], tile, preferred_element_type=jnp.float32)
            live = mask_ref[block * slot_count + slot] != 0
            acc = acc + jnp.where(live, product, 0.0)
        out_ref[pl.ds(first, block_rows), :] = acc.astype(out_ref.dtype)
        return carry

    lax.fori_loop(0, block_count, one_block, 0)


def apply_operator(offsets, mask, full_ops, extended, column_start, column_count):
    block_count, slot_count, block_rows, _ = full_ops.shape
    ext_rows = extended.shape[0]
    tile = min(TILE_COLUMNS, column_count)
    skip = column_start // tile
    grid_spec = pltpu.PrefetchScalarGridSpec(
        num_scalar_prefetch=2,
        grid=(column_count // tile,),
        in_specs=[
            pl.BlockSpec((block_count, slot_count, block_rows, block_rows), lambda j, *_: (0, 0, 0, 0)),
            pl.BlockSpec((ext_rows, tile), lambda j, *_: (0, j + skip)),
        ],
        out_specs=pl.BlockSpec((block_count * block_rows, tile), lambda j, *_: (0, j)),
    )
    flops = 2 * block_count * slot_count * block_rows * block_rows * column_count
    return pl.pallas_call(
        applied_kernel,
        grid_spec=grid_spec,
        out_shape=jax.ShapeDtypeStruct((block_count * block_rows, column_count), jnp.bfloat16),
        compiler_params=pltpu.CompilerParams(dimension_semantics=("arbitrary",)),
        cost_estimate=pl.CostEstimate(
            flops=flops, bytes_accessed=3 * ext_rows * column_count * 2, transcendentals=0
        ),
    )(offsets, mask, full_ops, extended)


def per_device(basis_matrix, operator_blocks, neighbours, neighbour_mask):
    local_rows, column_count = basis_matrix.shape
    block_count, slot_count, half_rows, block_rows = operator_blocks.shape
    sec = lax.axis_index("sec")
    col = lax.axis_index("col")
    row = 0
    for name, size in ROW_PARTS:
        row = row * size + lax.axis_index(name)

    share = block_count // 2
    mine = lax.dynamic_slice_in_dim(operator_blocks, col * share, share, 0)
    from_sec = lax.ppermute(mine, "sec", [(0, 1), (1, 0)])
    from_col = lax.ppermute(from_sec, "col", [(0, 1), (1, 0)])
    other_half = jnp.where(
        col == 0,
        jnp.concatenate([from_sec, from_col], axis=0),
        jnp.concatenate([from_col, from_sec], axis=0),
    )
    first = jnp.where(sec == 0, operator_blocks, other_half)
    second = jnp.where(sec == 0, other_half, operator_blocks)
    full_ops = jnp.concatenate([first, second], axis=2)

    other_basis = lax.ppermute(basis_matrix, "col", [(0, 1), (1, 0)])
    left_projector = jnp.where(sec == col, basis_matrix, other_basis)

    extended = halo(basis_matrix, REACH * block_rows)
    offsets = jnp.clip(neighbours - row * block_count + REACH, 0, block_count + 2 * REACH - 1)
    row_count = 1
    for _, size in ROW_PARTS:
        row_count *= size
    scaling = 1.0 / math.sqrt(local_rows * row_count)
    chunk_rows = left_projector.shape[1] // row_count
    sizes = dict(ROW_PARTS)
    parts, names, start = [], [], 0
    for order, units in ORDERS:
        width = units * UNIT
        applied = apply_operator(
            offsets.reshape(-1), neighbour_mask.reshape(-1), full_ops, extended, start, width
        )
        start += width
        part = scaling * lax.dot_general(
            left_projector, applied, (((0,), (0,)), ((), ())), preferred_element_type=jnp.float32
        )
        parts.append(part.reshape(tuple(size for _, size in ROW_PARTS) + (chunk_rows, width)))
        names.append(list(ROW))
    (first_order, _), (second_order, _) = ORDERS
    assert first_order == ("z", "x", "y") and second_order == ("x", "z", "y")
    nz, nx, ny = sizes["z"], sizes["x"], sizes["y"]
    a, b = parts
    width_a, width_b = a.shape[-1], b.shape[-1]
    a, b = multi_ring_reduce(
        [a.reshape(nz, -1, width_a), b.reshape(nz, nx, -1, width_b)],
        [("z", nz), ("x", nx)],
        0,
        [None, ("y", nz)],
    )
    a, b = multi_ring_reduce(
        [a.reshape(nx, -1, width_a), b.reshape(nz, -1, width_b)],
        [("x", nx), ("z", nz)],
        1,
        [("y", 1), None],
    )
    parts = [a, b]
    pieces = parts
    return jnp.concatenate(pieces, axis=-1)


def solution(mesh):
    sizes = [mesh.shape["sec"]] + [size for _, size in ROW_PARTS] + [mesh.shape["col"]]
    fine = Mesh(np.asarray(mesh.devices).reshape(sizes), ("sec",) + ROW + ("col",))
    return jax.shard_map(
        per_device,
        mesh=fine,
        in_specs=(P(ROW, "col"), P(ROW, None, "sec", None), P(ROW, None), P(ROW, None)),
        out_specs=P(("sec",) + ROW, "col"),
        check_vma=False,
    )
```

```python
import functools
import math

import jax
import jax.numpy as jnp
import numpy as np
from jax import lax
from jax.experimental import pallas as pl
from jax.experimental.pallas import tpu as pltpu
from jax.sharding import Mesh
from jax.sharding import PartitionSpec as P

REACH = 2
ROW_PARTS = (("z", 8), ("x", 4), ("y", 2))
ROW = tuple(name for name, _ in ROW_PARTS)
UNIT = 256
ORDERS = ((("z", "x", "y"), 4), (("x", "z", "y"), 4))
TILE_COLUMNS = 1024
STATIC_OFFSETS = (0, -1, 1, -2, 2)
WINDOW_SLOTS = tuple(range(len(STATIC_OFFSETS)))


def halo(shard, width):
    count = 1
    for _, size in ROW_PARTS:
        count *= size
    length = shard.shape[0]
    axes = ("sec",) + ROW

    def index(sec, row):
        return sec * count + row

    after_pairs, before_pairs = [], []
    for sec in range(2):
        for row in range(count):
            other = sec if row % 2 == 0 else 1 - sec
            if row + 1 < count:
                after_pairs.append((index(other, row + 1), index(sec, row)))
            other = 1 - sec if row % 2 == 0 else sec
            if row >= 1:
                before_pairs.append((index(other, row - 1), index(sec, row)))
    before = lax.ppermute(shard[length - width :], axes, before_pairs)
    after = lax.ppermute(shard[:width], axes, after_pairs)
    return jnp.concatenate([before, shard, after], axis=0)


def take_chunk(x, index, dim):
    return lax.dynamic_index_in_dim(x, index, axis=dim, keepdims=False)


def read_chunk(x, index, columns):
    if len(x.shape) == 3:
        return x[index, :, columns]
    value = x[:, index, :, columns]
    return value.reshape(value.shape[0] * value.shape[1], value.shape[2])


def multi_ring_kernel(plan, pairs, *refs):
    count = len(plan)
    x_refs, o_refs = refs[:count], refs[count : 2 * count]
    scratch = refs[2 * count : 2 * count + 7 * count]
    pair_scratch = refs[2 * count + 7 * count :]
    mesh = pl.DeviceIdType.MESH
    rings = []
    for index, (axis, n) in enumerate(plan):
        out_f, in_f, out_b, in_b, send_sem, recv_sem, credit_sem = scratch[7 * index : 7 * index + 7]
        p = lax.axis_index(axis)
        rings.append(
            dict(
                axis=axis, n=n, p=p, x=x_refs[index], o=o_refs[index],
                right=lax.rem(p + 1, n), left=lax.rem(p + n - 1, n),
                out_f=out_f, in_f=in_f, out_b=out_b, in_b=in_b,
                send=send_sem, recv=recv_sem, credit=credit_sem, copies=None,
            )
        )

    barrier = pltpu.get_barrier_semaphore()
    for ring in rings:
        for neighbour in (ring["left"], ring["right"]):
            pl.semaphore_signal(barrier, 1, device_id={ring["axis"]: neighbour}, device_id_type=mesh)
    signals = 2 * count
    pair_axes = sorted({pair[0] for pair in pairs if pair is not None})
    for pair_axis in pair_axes:
        partner = 1 - lax.axis_index(pair_axis)
        pl.semaphore_signal(barrier, 1, device_id={pair_axis: partner}, device_id_type=mesh)
        signals += 1
    pl.semaphore_wait(barrier, signals)

    pending = []

    def finish(index):
        ring = rings[index]
        for copy in ring["copies"]:
            copy.wait()
        n, p, x = ring["n"], ring["p"], ring["x"]
        half = x.shape[-1] // 2
        last = (n - 2) % 2
        forward = ring["in_f"][last] + read_chunk(x, p, slice(None, half))
        backward = ring["in_b"][last] + read_chunk(x, p, slice(half, None))
        if pairs[index] is None:
            ring["o"][:, :half] = forward
            ring["o"][:, half:] = backward
            return
        pair_axis, _ = pairs[index]
        total, got, send_sem, recv_sem = pair_scratch[4 * index : 4 * index + 4]
        outer, _, rows, _ = total.shape
        total[:, :, :, :half] = forward.reshape(outer, 2, rows, half)
        total[:, :, :, half:] = backward.reshape(outer, 2, rows, half)
        mine = lax.axis_index(pair_axis)
        copy = pltpu.make_async_remote_copy(
            src_ref=total.at[:, pl.ds(1 - mine, 1)], dst_ref=got,
            send_sem=send_sem, recv_sem=recv_sem,
            device_id={pair_axis: 1 - mine}, device_id_type=mesh,
        )
        copy.start()
        pending.append((index, copy, mine))

    done = set()
    ticks = max(n - 1 for _, n in plan)
    for tick in range(ticks):
        for ring in rings:
            n = ring["n"]
            due = [step for step in range(n - 1) if (step * ticks) // (n - 1) == tick]
            for step in due:
                if ring["copies"] is not None:
                    for copy in ring["copies"]:
                        copy.wait()
                    ring["copies"] = None
                slot = step % 2
                p, x, half = ring["p"], ring["x"], ring["x"].shape[-1] // 2
                chunk_f = lax.rem(p - step - 1 + 2 * n, n)
                chunk_b = lax.rem(p + step + 1, n)
                if step == 0:
                    ring["out_f"][slot] = read_chunk(x, chunk_f, slice(None, half))
                    ring["out_b"][slot] = read_chunk(x, chunk_b, slice(half, None))
                else:
                    ring["out_f"][slot] = ring["in_f"][1 - slot] + read_chunk(x, chunk_f, slice(None, half))
                    ring["out_b"][slot] = ring["in_b"][1 - slot] + read_chunk(x, chunk_b, slice(half, None))
                    if step <= n - 3:
                        pl.semaphore_signal(
                            ring["credit"].at[0], 1, device_id={ring["axis"]: ring["left"]}, device_id_type=mesh
                        )
                        pl.semaphore_signal(
                            ring["credit"].at[1], 1, device_id={ring["axis"]: ring["right"]}, device_id_type=mesh
                        )
                if step >= 2:
                    pl.semaphore_wait(ring["credit"].at[0], 1)
                    pl.semaphore_wait(ring["credit"].at[1], 1)
                copy_f = pltpu.make_async_remote_copy(
                    src_ref=ring["out_f"].at[slot], dst_ref=ring["in_f"].at[slot],
                    send_sem=ring["send"].at[0, slot], recv_sem=ring["recv"].at[0, slot],
                    device_id={ring["axis"]: ring["right"]}, device_id_type=mesh,
                )
                copy_b = pltpu.make_async_remote_copy(
                    src_ref=ring["out_b"].at[slot], dst_ref=ring["in_b"].at[slot],
                    send_sem=ring["send"].at[1, slot], recv_sem=ring["recv"].at[1, slot],
                    device_id={ring["axis"]: ring["left"]}, device_id_type=mesh,
                )
                copy_f.start()
                copy_b.start()
                ring["copies"] = (copy_f, copy_b)
        for index, ring in enumerate(rings):
            last_tick = ((ring["n"] - 2) * ticks) // (ring["n"] - 1)
            if pairs[index] is not None and last_tick + 1 == tick:
                finish(index)
                done.add(index)
    for index in sorted(range(count), key=lambda i: rings[i]["n"]):
        if index not in done:
            finish(index)
    for index, copy, mine in pending:
        total, got = pair_scratch[4 * index : 4 * index + 2]
        outer, _, rows, width = total.shape
        copy.wait()
        summed = got[...] + total[:, pl.ds(mine, 1)]
        rings[index]["o"][...] = summed.reshape(outer * rows, width)


def multi_ring_reduce(inputs, plan, collective_id, pairs):
    vmem = pltpu.VMEM
    scratch, pair_scratch, out_shapes = [], [], []
    for x, pair in zip(inputs, pairs):
        rows, width = x.shape[-2], x.shape[-1]
        if len(x.shape) == 4:
            rows *= x.shape[0]
        half = width // 2
        scratch += [vmem((2, rows, half), x.dtype) for _ in range(4)]
        scratch += [
            pltpu.SemaphoreType.DMA((2, 2)),
            pltpu.SemaphoreType.DMA((2, 2)),
            pltpu.SemaphoreType.REGULAR((2,)),
        ]
        if pair is None:
            out_shapes.append((rows, width))
            pair_scratch += [vmem((8, 128), x.dtype), vmem((8, 128), x.dtype)]
        else:
            outer = pair[1]
            inner = rows // (2 * outer)
            out_shapes.append((rows // 2, width))
            pair_scratch += [
                vmem((outer, 2, inner, width), x.dtype),
                vmem((outer, 1, inner, width), x.dtype),
            ]
        pair_scratch += [pltpu.SemaphoreType.DMA(()), pltpu.SemaphoreType.DMA(())]
    scratch += pair_scratch
    return pl.pallas_call(
        functools.partial(multi_ring_kernel, tuple(plan), tuple(pairs)),
        out_shape=[jax.ShapeDtypeStruct(shape, x.dtype) for shape, x in zip(out_shapes, inputs)],
        in_specs=[pl.BlockSpec(memory_space=vmem) for _ in inputs],
        out_specs=[pl.BlockSpec(memory_space=vmem) for _ in inputs],
        scratch_shapes=scratch,
        compiler_params=pltpu.CompilerParams(
            collective_id=collective_id, has_side_effects=True, vmem_limit_bytes=60 * 1024 * 1024
        ),
    )(*inputs)


def ring_sum(x, dim, axis, n):
    p = lax.axis_index(axis)
    partner = [(0, 1), (1, 0)]
    got = lax.ppermute(take_chunk(x, 1 - p, dim), axis, partner)
    return got + take_chunk(x, p, dim)


def applied_kernel(offsets_ref, mask_ref, ops_ref, ext_ref, out_ref):
    block_count, slot_count, block_rows = ops_ref.shape[0], ops_ref.shape[1], ops_ref.shape[2]
    order = [slot for _, slot in sorted(zip(STATIC_OFFSETS, WINDOW_SLOTS))]

    def one_block(block, carry):
        lhs = jnp.concatenate(
            [
                jnp.where(mask_ref[block * slot_count + slot] != 0, ops_ref[block, slot], 0)
                for slot in order
            ],
            axis=1,
        )
        first = pl.multiple_of(block * block_rows, block_rows)
        acc = jnp.dot(
            lhs, ext_ref[pl.ds(first, len(order) * block_rows), :], preferred_element_type=jnp.float32
        )
        for slot in range(len(WINDOW_SLOTS), slot_count):
            tile_index = offsets_ref[block * slot_count + slot]
            start = pl.multiple_of(tile_index * block_rows, block_rows)
            tile = ext_ref[pl.ds(start, block_rows), :]
            product = jnp.dot(ops_ref[block, slot], tile, preferred_element_type=jnp.float32)
            live = mask_ref[block * slot_count + slot] != 0
            acc = acc + jnp.where(live, product, 0.0)
        out_ref[pl.ds(first, block_rows), :] = acc.astype(out_ref.dtype)
        return carry

    lax.fori_loop(0, block_count, one_block, 0, unroll=True)


def apply_operator(offsets, mask, full_ops, extended, column_start, column_count):
    block_count, slot_count, block_rows, _ = full_ops.shape
    ext_rows = extended.shape[0]
    tile = min(TILE_COLUMNS, column_count)
    skip = column_start // tile
    grid_spec = pltpu.PrefetchScalarGridSpec(
        num_scalar_prefetch=2,
        grid=(column_count // tile,),
        in_specs=[
            pl.BlockSpec((block_count, slot_count, block_rows, block_rows), lambda j, *_: (0, 0, 0, 0)),
            pl.BlockSpec((ext_rows, tile), lambda j, *_: (0, j + skip)),
        ],
        out_specs=pl.BlockSpec((block_count * block_rows, tile), lambda j, *_: (0, j)),
    )
    flops = 2 * block_count * slot_count * block_rows * block_rows * column_count
    return pl.pallas_call(
        applied_kernel,
        grid_spec=grid_spec,
        out_shape=jax.ShapeDtypeStruct((block_count * block_rows, column_count), jnp.bfloat16),
        compiler_params=pltpu.CompilerParams(dimension_semantics=("arbitrary",)),
        cost_estimate=pl.CostEstimate(
            flops=flops, bytes_accessed=3 * ext_rows * column_count * 2, transcendentals=0
        ),
    )(offsets, mask, full_ops, extended)


def per_device(basis_matrix, operator_blocks, neighbours, neighbour_mask):
    local_rows, column_count = basis_matrix.shape
    block_count, slot_count, half_rows, block_rows = operator_blocks.shape
    sec = lax.axis_index("sec")
    col = lax.axis_index("col")
    row = 0
    for name, size in ROW_PARTS:
        row = row * size + lax.axis_index(name)

    share = block_count // 2
    mine = lax.dynamic_slice_in_dim(operator_blocks, col * share, share, 0)
    from_sec = lax.ppermute(mine, "sec", [(0, 1), (1, 0)])
    from_col = lax.ppermute(from_sec, "col", [(0, 1), (1, 0)])
    other_half = jnp.where(
        col == 0,
        jnp.concatenate([from_sec, from_col], axis=0),
        jnp.concatenate([from_col, from_sec], axis=0),
    )
    first = jnp.where(sec == 0, operator_blocks, other_half)
    second = jnp.where(sec == 0, other_half, operator_blocks)
    full_ops = jnp.concatenate([first, second], axis=2)

    other_basis = lax.ppermute(basis_matrix, "col", [(0, 1), (1, 0)])
    left_projector = jnp.where(sec == col, basis_matrix, other_basis)

    extended = halo(basis_matrix, REACH * block_rows)
    offsets = jnp.clip(neighbours - row * block_count + REACH, 0, block_count + 2 * REACH - 1)
    row_count = 1
    for _, size in ROW_PARTS:
        row_count *= size
    scaling = 1.0 / math.sqrt(local_rows * row_count)
    chunk_rows = left_projector.shape[1] // row_count
    sizes = dict(ROW_PARTS)
    parts, names, start = [], [], 0
    for order, units in ORDERS:
        width = units * UNIT
        applied = apply_operator(
            offsets.reshape(-1), neighbour_mask.reshape(-1), full_ops, extended, start, width
        )
        start += width
        part = scaling * lax.dot_general(
            left_projector, applied, (((0,), (0,)), ((), ())), preferred_element_type=jnp.float32
        )
        parts.append(part.reshape(tuple(size for _, size in ROW_PARTS) + (chunk_rows, width)))
        names.append(list(ROW))
    (first_order, _), (second_order, _) = ORDERS
    assert first_order == ("z", "x", "y") and second_order == ("x", "z", "y")
    nz, nx, ny = sizes["z"], sizes["x"], sizes["y"]
    a, b = parts
    width_a, width_b = a.shape[-1], b.shape[-1]
    a, b = multi_ring_reduce(
        [a.reshape(nz, -1, width_a), b.reshape(nz, nx, -1, width_b)],
        [("z", nz), ("x", nx)],
        0,
        [None, ("y", nz)],
    )
    a, b = multi_ring_reduce(
        [a.reshape(nx, -1, width_a), b.reshape(nz, -1, width_b)],
        [("x", nx), ("z", nz)],
        1,
        [("y", 1), None],
    )
    parts = [a, b]
    pieces = parts
    return jnp.concatenate(pieces, axis=-1)


def solution(mesh):
    sizes = [mesh.shape["sec"]] + [size for _, size in ROW_PARTS] + [mesh.shape["col"]]
    fine = Mesh(np.asarray(mesh.devices).reshape(sizes), ("sec",) + ROW + ("col",))
    return jax.shard_map(
        per_device,
        mesh=fine,
        in_specs=(P(ROW, "col"), P(ROW, None, "sec", None), P(ROW, None), P(ROW, None)),
        out_specs=P(("sec",) + ROW, "col"),
        check_vma=False,
    )
```
